512 devices in a mesh: brick: 64 (over z, y), blk: 8 (over x, core).
Axes of the slice: x: 4, y: 8, z: 8, core: 2. Of those that a mesh axis runs over, the one named last changes fastest.
Arguments:
- parameters: float32 [4, 65536], P(None, ('brick', 'blk')), may hold values from -0.4 to 3, as said below
- sersic: float32 [65536], P(('brick', 'blk')), may hold values from 1 to 4
- psf_width: float32 [65536], P(('brick', 'blk')), may hold values from 0.8 to 2
- point_flag: int32 [65536], P(('brick', 'blk')), may hold values 0 or 1
- owner_brick: int32 [65536, 1], P(('brick', 'blk')), may hold values from 0 to 63; in each aligned block of 128 rows (0 to 127, 128 to 255, ...) at most 4 rows name the same one
- cell_index: int32 [65536], P(('brick', 'blk')), may hold values from 0 to 31
- exposure: float32 [16384, 1024], P(('brick', 'blk')), may hold values from -120 to 120
- inv_noise: float32 [16384], P(('brick', 'blk')), may hold values from 0.5 to 2
Outputs:
- updated: float32 [4, 65536], P(None, ('brick', 'blk'))
The draws below stay inside these ranges and needn't reach their ends.
Inputs may be any that keep to these rules, and one draw needn't show every extreme that they name: `parameters`: row 0 is a flux from 0.5 to 3, rows 1 and 2 the centre's offsets within 0.4 pixels, row 3 the log radius from ln 1.5 to ln 6. `owner_brick`: the sources of one device name one brick at most 4 times.
All inputs are finite; a program needn't handle non-finite values. No bound on the sum of `point_flag` on one device may be relied on, other than what follows from the above.
Results may differ from the reference program's by a relative error of at most 0.0003.
Values sent between devices are 32-bit elements; how exact they have to be, the bound alone decides.
A program may use at most 64 MiB of HBM per device.

```python
import math
import jax
import jax.numpy as jnp
import numpy as np
from jax import lax

TILE = 32
S_DEV = 128
CELLS = 32
BRICKS = 64
GROUP = 8
CAP = 4
SOURCES = 65536
EXPCELLS = 16384
GROUP_CELLS = 256


def draw_parameters(key, part):
    subkeys = jax.random.split(key, 3)
    flux_row = jax.random.uniform(subkeys[0], (1, SOURCES), jnp.float32, 0.5, 3.0)
    shift_rows = jax.random.uniform(subkeys[1], (2, SOURCES), jnp.float32, -0.4, 0.4)
    radius_row = jax.random.uniform(subkeys[2], (1, SOURCES), jnp.float32, math.log(1.5), math.log(6.0))
    return jnp.concatenate([flux_row, shift_rows, radius_row], axis=0)


def draw_exposure(key, part):
    first_key, second_key = jax.random.split(key)
    position = (jnp.arange(EXPCELLS) % GROUP_CELLS).astype(jnp.float32) / GROUP_CELLS
    rise = 1.0 + 2.0 * position
    spread = jnp.exp(math.log(10.0) * jax.random.uniform(second_key, (EXPCELLS, TILE * TILE), jnp.float32))
    noise = jnp.clip(jax.random.normal(first_key, (EXPCELLS, TILE * TILE), jnp.float32), -5.0, 5.0)
    return 0.5 * rise[:, None] * spread * noise


def plant(drawn, key, least, high):
    extent = drawn.shape
    spot = [jax.random.randint(jax.random.fold_in(key, axis), (), 0, extent[axis]) for axis in range(len(extent))]
    drawn = drawn.at[tuple(spot)].set(least)
    longest = extent.index(max(extent))
    spot[longest] = (spot[longest] + 1) % extent[longest]
    return drawn.at[tuple(spot)].set(high)


def block_levels(rng, extent, pieces, least, largest):
    def one(axis_at, parts):
        steps = jax.random.uniform(jax.random.fold_in(jax.random.fold_in(rng, 6), axis_at), (parts,), jnp.float32, least / len(pieces), largest / len(pieces))
        return jnp.repeat(jnp.exp(steps), extent[axis_at] // parts).reshape((-1,) + (1,) * (len(extent) - axis_at - 1))

    level = one(*pieces[0])
    for cut in pieces[1:]:
        level = level * one(*cut)
    return level


def deal_out(key, own, number, rows, number_of, top, limit, lean):
    ranking = jax.random.permutation(key, number_of)
    crowded, ordinary = load_shares(number_of, rows * top, limit, lean, True), load_shares(number_of, rows * top, limit, lean, False)
    places = jnp.arange(number_of)

    def named(lengths, offset_by):
        used = int((lengths > 0).sum())
        fixed = max(1, used // 4)
        passed = fixed + (places - fixed + offset_by * (used - fixed)) % max(1, number_of - fixed)
        return jnp.zeros((number_of,), jnp.int32).at[ranking[jnp.where(places < fixed, places, passed)]].set(jnp.asarray(lengths, jnp.int32))

    lengths = jnp.where(number % 4 == 0, named(crowded, number // 4), named(ordinary, number - number // 4 - 1))
    mixed = jax.random.permutation(jax.random.fold_in(own, 3), number_of)
    donor, sink = mixed[0:number_of // 2 * 2:2], mixed[1:number_of // 2 * 2:2]
    margin = jnp.minimum(lengths[donor] - 1, limit - lengths[sink]) // 2
    margin = jnp.where((donor == ranking[0]) | (sink == ranking[0]) | (lengths[sink] == 0), 0, jnp.maximum(margin, 0))
    passed = jax.random.randint(jax.random.fold_in(own, 4), (number_of // 2,), 0, 1 << 20) % (margin + 1)
    lengths = lengths.at[donor].add(-passed).at[sink].add(passed)
    members = jnp.searchsorted(jnp.cumsum(lengths), jnp.arange(rows * top), side="right").astype(jnp.int32)
    table = members.reshape(top, rows).T
    table = table[jax.random.permutation(jax.random.fold_in(own, 1), rows)]
    offset_by = jax.random.randint(jax.random.fold_in(own, 2), (rows, 1), 0, top)
    return jnp.take_along_axis(table, (jnp.arange(top)[None, :] + offset_by) % top, axis=1)


def load_shares(count, total, most, lean, full):
    portions = [(1 << 20) // math.isqrt(standing ** lean) + 1 for standing in range(1, count + 1)]
    largest = most if full else min(most, max(-(-total // count), total * portions[0] // sum(portions)))
    least = 1 if total - largest >= count - 1 else 0
    counts, spare = [largest] + [least] * (count - 1), total - largest - least * (count - 1)
    while spare > 0:
        free = [i for i in range(1, count) if counts[i] < largest] or [i for i in range(1, count) if counts[i] < most]
        whole, remaining = sum([portions[i] for i in free]), spare
        for i in free:
            more = min(most - counts[i], max(1, remaining * portions[i] // whole), spare)
            counts[i] = counts[i] + more
            spare = spare - more
    return np.array(counts)


def setup_inputs(seed: int = 0) -> dict:
    key_of = jax.random.split(jax.random.key(seed), 9)
    parameters = draw_parameters(jax.random.fold_in(key_of[8], 71), 0)
    sersic = jnp.clip(jnp.exp(math.log(4.0) - 1.3862944 * jax.random.uniform(key_of[1], (SOURCES,), jnp.float32) ** block_levels(key_of[1], (SOURCES,), ((0, 512),), -0.2, 0.2)), 1.0, 4.0)
    psf_width = jnp.clip(jnp.exp(math.log(2.0) - 0.9162907 * jax.random.uniform(key_of[2], (SOURCES,), jnp.float32) ** block_levels(key_of[2], (SOURCES,), ((0, 512),), -0.2, 0.2)), 0.8, 2.0)
    point_flag = plant((jax.random.randint(key_of[3], (SOURCES,), 0, 4) < 1).astype(jnp.int32), jax.random.fold_in(key_of[3], 1), 0, 1)
    owner_brick_keys = jax.random.split(jax.random.fold_in(key_of[4], 1), SOURCES // S_DEV)
    owner_brick_turns = jax.random.permutation(jax.random.fold_in(key_of[4], 3), SOURCES // S_DEV)
    owner_brick = jax.vmap(lambda own, number: deal_out(jax.random.fold_in(key_of[4], 2), own, number, S_DEV, BRICKS, 1, CAP, 2))(owner_brick_keys, owner_brick_turns).reshape((SOURCES, 1))
    cell_index = plant(jax.random.randint(key_of[5], (SOURCES,), 0, CELLS), jax.random.fold_in(key_of[5], 1), 0, CELLS - 1).astype(jnp.int32)
    exposure = draw_exposure(jax.random.fold_in(key_of[8], 71), 0)
    inv_noise = jnp.clip(jnp.exp(math.log(2.0) - 1.3862944 * jax.random.uniform(key_of[7], (EXPCELLS,), jnp.float32) ** block_levels(key_of[7], (EXPCELLS,), ((0, 512),), -0.2, 0.2)), 0.5, 2.0)
    return {"parameters": parameters, "sersic": sersic, "psf_width": psf_width, "point_flag": point_flag, "owner_brick": owner_brick, "cell_index": cell_index, "exposure": exposure, "inv_noise": inv_noise}


series_terms = 96
zero_point = 30.0
base_damping = 0.1
misfit_scale = 0.05
highest = lax.Precision.HIGHEST

def incomplete_gamma(shape_value, cutoff):
    term_steps = jnp.arange(1, series_terms, dtype=cutoff.dtype)
    increments = jnp.log(cutoff)[None, :] - jnp.log(shape_value[None, :] + term_steps[:, None])
    partial_logs = jnp.concatenate([jnp.zeros_like(cutoff)[None, :], jnp.cumsum(increments, axis=0)], axis=0)
    prefactor = shape_value * jnp.log(cutoff) - cutoff - lax.lgamma(shape_value + 1.0)
    return lax.optimization_barrier(jnp.sum(jnp.exp(prefactor[None, :] + partial_logs), axis=0))

def render(values, sersic, psf_width, point_flag):
    flux_value = values[0]
    shift_x = values[1]
    shift_y = values[2]
    log_radius = values[3]
    coords = jnp.arange(TILE, dtype=values.dtype) + 0.5 - 0.5 * TILE
    offset_y = coords[None, :] - shift_y[:, None]
    offset_x = coords[None, :] - shift_x[:, None]
    radius_sq = offset_y[:, :, None] ** 2 + offset_x[:, None, :] ** 2
    inverse_index = 1.0 / sersic
    bfactor = 2.0 * sersic - 1.0 / 3.0 + 4.0 / (405.0 * sersic)
    cutoff = bfactor * jnp.exp((math.log(0.5 * TILE) - log_radius) * inverse_index)
    log_norm = jnp.log(2.0 * math.pi * sersic) + 2.0 * log_radius + lax.lgamma(2.0 * sersic) - 2.0 * sersic * jnp.log(bfactor) + jnp.log(incomplete_gamma(2.0 * sersic, cutoff))
    scaled = jnp.exp((0.5 * jnp.log(radius_sq) - log_radius[:, None, None]) * inverse_index[:, None, None])
    galaxy = jnp.exp(-bfactor[:, None, None] * scaled - log_norm[:, None, None])
    separation = coords[:, None] - coords[None, :]
    inv_two_var = 0.5 / (psf_width * psf_width)
    norm_psf = 1.0 / (math.sqrt(2.0 * math.pi) * psf_width)
    kernel = jnp.exp(-(separation ** 2)[None] * inv_two_var[:, None, None]) * norm_psf[:, None, None]
    blurred = jnp.einsum('bij,bjk->bik', kernel, galaxy, precision=highest)
    blurred = jnp.einsum('bik,blk->bil', blurred, kernel, precision=highest)
    profile_y = jnp.exp(-offset_y ** 2 * inv_two_var[:, None]) * norm_psf[:, None]
    profile_x = jnp.exp(-offset_x ** 2 * inv_two_var[:, None]) * norm_psf[:, None]
    point_image = profile_y[:, :, None] * profile_x[:, None, :]
    shape_image = jnp.where((point_flag == 1)[:, None, None], point_image, blurred)
    return (zero_point * flux_value)[:, None] * shape_image.reshape(values.shape[1], TILE * TILE)

def source_moments(values, sersic, psf_width, point_flag, weighted_rows, weight_rows):

    def model_of(current):
        return render(current, sersic, psf_width, point_flag)
    unit_tangents = jnp.eye(4, dtype=values.dtype)[:, :, None] * jnp.ones_like(values)[None]
    jacobian = jax.vmap(lambda tangent: jax.jvp(model_of, (values,), (tangent,))[1])(unit_tangents)
    gradient = jnp.einsum('pbq,bq->pb', jacobian, weighted_rows, precision=highest)
    curvature = jnp.einsum('pbq,rbq->prb', jacobian, jacobian, precision=highest) * weight_rows[None, None, :]
    return (gradient, curvature)

def damped_solve(curvature, gradient, damping):
    system = [[curvature[first, second] for second in range(4)] for first in range(4)]
    for first in range(4):
        system[first][first] = system[first][first] + damping * (1.0 + curvature[first, first])
    factor = [[None for second in range(4)] for first in range(4)]
    for column in range(4):
        pivot = system[column][column]
        for inner in range(column):
            pivot = pivot - factor[column][inner] * factor[column][inner]
        pivot = jnp.sqrt(pivot)
        factor[column][column] = pivot
        for lower_row in range(column + 1, 4):
            entry = system[lower_row][column]
            for inner in range(column):
                entry = entry - factor[lower_row][inner] * factor[column][inner]
            factor[lower_row][column] = entry / pivot
    forward = []
    for row_at in range(4):
        entry = gradient[row_at]
        for inner in range(row_at):
            entry = entry - factor[row_at][inner] * forward[inner]
        forward.append(entry / factor[row_at][row_at])
    solution = [None, None, None, None]
    for row_at in reversed(range(4)):
        entry = forward[row_at]
        for inner in range(row_at + 1, 4):
            entry = entry - factor[inner][row_at] * solution[inner]
        solution[row_at] = entry / factor[row_at][row_at]
    return jnp.stack(solution)

def reference(parameters, sersic, psf_width, point_flag, owner_brick, cell_index, exposure, inv_noise):
    total_sources = parameters.shape[1]
    block_count = total_sources // S_DEV
    source_ids = jnp.arange(total_sources, dtype=jnp.int32)
    target = ((owner_brick[:, 0] * GROUP + source_ids // S_DEV % GROUP) * CELLS + cell_index).astype(jnp.int32)
    stacked = (parameters.reshape(4, block_count, S_DEV).transpose(1, 0, 2), sersic.reshape(block_count, S_DEV), psf_width.reshape(block_count, S_DEV), point_flag.reshape(block_count, S_DEV), target.reshape(block_count, S_DEV))

    def add_block(model, block):
        tiles = render(block[0], block[1], block[2], block[3])
        return (model.at[block[4]].add(tiles), None)
    model, unused = lax.scan(add_block, jnp.zeros_like(exposure), stacked)
    weights = inv_noise * inv_noise
    misfit = exposure - model
    weighted = weights[:, None] * misfit
    cell_chi = lax.optimization_barrier(jnp.sum(weighted * misfit, axis=1))
    group_chi = lax.optimization_barrier(jnp.sum(cell_chi.reshape(BRICKS, GROUP * CELLS), axis=1))
    damping_group = base_damping + misfit_scale * group_chi / (GROUP * CELLS * TILE * TILE)

    def solve_block(block):
        gradient, curvature = source_moments(block[0], block[1], block[2], block[3], weighted[block[4]], weights[block[4]])
        damping = damping_group[block[5] // GROUP]
        return block[0] + damped_solve(curvature, gradient, damping)
    updated = lax.map(solve_block, stacked + (jnp.arange(block_count, dtype=jnp.int32),))
    return updated.transpose(1, 0, 2).reshape(4, total_sources)
```

```python
import functools
import math

import jax
import jax.numpy as jnp
from jax import lax
from jax.experimental import pallas as pl
from jax.experimental.pallas import tpu as pltpu
from jax.sharding import PartitionSpec as P

TILE = 32
PIXELS = TILE * TILE
HALF = TILE // 2
SERIES = 96
CAP = 4
VALS = 32
LANES = 128
ZERO_POINT = 30.0
BASE_DAMPING = 0.1
MISFIT_SCALE = 0.05
HIGHEST = lax.Precision.HIGHEST
MESH = pl.DeviceIdType.MESH
F32 = jnp.float32

CX, CY, C1, C0, LN, INVN, ITV, NORM, POINT, AMP, SLOPE, CELL = range(12)


def dot(a, b, ca=1, cb=0):
    return lax.dot_general(
        a, b, (((ca,), (cb,)), ((), ())), precision=HIGHEST, preferred_element_type=F32
    )


def series(shape_value, cutoff):
    chain = SERIES // 8
    at = lax.broadcasted_iota(jnp.int32, (8, LANES), 0) * chain
    total = jnp.zeros((8, LANES), F32)
    product = jnp.ones((8, LANES), F32)
    for step in reversed(range(chain)):
        k = at + (step + 1)
        ratio = cutoff / (shape_value + k.astype(F32))
        live = k < SERIES
        total = jnp.where(live, ratio * (1.0 + total), 0.0)
        product = jnp.where(live, product * ratio, product)
    whole = total[7:8]
    last = product[7:8]
    for j in reversed(range(7)):
        whole = total[j : j + 1] + product[j : j + 1] * whole
        last = last * product[j : j + 1]
    return 1.0 + whole, last


def source_rows(values, sersic, psf_width, point, cell):
    flux, shift_x, shift_y, log_radius = (values[k : k + 1] for k in range(4))
    inverse_index = 1.0 / sersic
    bfactor = 2.0 * sersic - 1.0 / 3.0 + 4.0 / (405.0 * sersic)
    cutoff = bfactor * jnp.exp((math.log(0.5 * TILE) - log_radius) * inverse_index)
    total, last = series(2.0 * sersic, cutoff)
    log_norm = math.log(math.pi * 0.25 * TILE * TILE) - cutoff + jnp.log(total)
    slope = 2.0 - (2.0 * sersic - cutoff * last) * inverse_index / total
    inv_two_var = 0.5 / (psf_width * psf_width)
    norm_psf = 1.0 / (math.sqrt(2.0 * math.pi) * psf_width)
    is_point = point == 1
    log_itv = jnp.log(inv_two_var)
    rows = [None] * VALS
    rows[CX] = shift_x
    rows[CY] = shift_y
    rows[C1] = jnp.where(is_point, 1.0, 0.5 * inverse_index)
    rows[C0] = jnp.where(is_point, log_itv, jnp.log(bfactor) - log_radius * inverse_index)
    rows[LN] = jnp.where(is_point, math.log(math.pi) - log_itv, log_norm)
    rows[INVN] = jnp.where(is_point, 2.0, inverse_index)
    rows[ITV] = inv_two_var
    rows[NORM] = norm_psf
    rows[POINT] = jnp.where(is_point, 1.0, 0.0)
    rows[AMP] = ZERO_POINT * flux
    rows[SLOPE] = slope
    rows[CELL] = (cell + 1).astype(F32)
    zero = jnp.zeros_like(flux)
    return jnp.concatenate([zero if row is None else row for row in rows], axis=0)


def build_taps(row, taps, coef, at):
    inv_two_var = jnp.broadcast_to(row(ITV), (8, LANES))
    norm = jnp.broadcast_to(row(NORM), (8, LANES))
    point = jnp.broadcast_to(row(POINT), (8, LANES)) > 0.5

    def tap(d, carry):
        apart = d.astype(F32)
        value = jnp.exp(-(apart * apart) * inv_two_var) * norm
        value = jnp.where(point, jnp.where(d == 0, 1.0, 0.0), value) * 0.5
        taps[TILE - 1 + d] = value
        taps[TILE - 1 - d] = value
        return carry

    lax.fori_loop(0, TILE, tap, 0)

    def column(q, carry):
        near = taps[pl.ds(TILE - 1 - q, HALF)]
        far = taps[pl.ds(q, HALF)]
        coef[at, 0, q] = near + far
        coef[at, 1, q] = near - far
        return carry

    lax.fori_loop(0, HALF, column, 0)


def blur_lines(load, store, coef, at, even_acc):
    for parity in range(2):
        acc = None
        for q in range(HALF):
            low, high = load(q), load(TILE - 1 - q)
            x = low + high if parity == 0 else low - high
            term = coef[at, parity, q][None] * x[:, None]
            acc = term if acc is None else acc + term
        if parity == 0:
            even_acc[...] = acc
        else:
            even = even_acc[...]
            store(0, even + acc)
            store(1, even - acc)


def blur(count, at_of, src, mid, dst, coef, even_acc):
    def first(step, carry):
        image, part = step // 2, step % 2
        start = pl.multiple_of(part * 16, 16)

        def load(q):
            return src[image, pl.ds(pl.multiple_of(q * TILE + start, 16), 16), :].reshape(2, 8, LANES)

        def store(which, value):
            for k in range(HALF):
                line = k if which == 0 else TILE - 1 - k
                mid[image, pl.ds(pl.multiple_of(line * TILE + start, 16), 16), :] = value[:, k].reshape(16, LANES)

        blur_lines(load, store, coef, at_of(image), even_acc)
        return carry

    def second(step, carry):
        image, part = step // 2, step % 2
        start = part * 16

        def load(p):
            return mid[image, pl.ds(start * TILE + p, 16, stride=TILE), :].reshape(2, 8, LANES)

        def store(which, value):
            for k in range(HALF):
                line = k if which == 0 else TILE - 1 - k
                dst[image, pl.ds(pl.multiple_of(line * TILE + start, 16), 16), :] = value[:, k].reshape(16, LANES)

        blur_lines(load, store, coef, at_of(image), even_acc)
        return carry

    lax.fori_loop(0, 2 * count, first, 0)
    lax.fori_loop(0, 2 * count, second, 0)


def coordinates(row):
    t_p = lax.broadcasted_iota(jnp.int32, (TILE, LANES), 0).astype(F32) + (0.5 - 0.5 * TILE)
    return t_p - row(CY)


def line_of(q, row, dy):
    dx = q.astype(F32) + (0.5 - 0.5 * TILE) - row(CX)
    return dx, dy * dy + dx * dx


def images(q, row, dy):
    dx, radius_sq = line_of(q, row, dy)
    log_r2 = jnp.log(radius_sq)
    power = jnp.exp(row(C1) * log_r2 + row(C0))
    image = jnp.exp(-power - row(LN))
    slope = image * (power * row(INVN))
    return dx, radius_sq, image, slope


def damped_solve(curvature, gradient, damping):
    system = [[curvature[first][second] for second in range(4)] for first in range(4)]
    for first in range(4):
        system[first][first] = system[first][first] + damping * (1.0 + curvature[first][first])
    factor = [[None for second in range(4)] for first in range(4)]
    for column in range(4):
        pivot = system[column][column]
        for inner in range(column):
            pivot = pivot - factor[column][inner] * factor[column][inner]
        pivot = jnp.sqrt(pivot)
        factor[column][column] = pivot
        for lower_row in range(column + 1, 4):
            entry = system[lower_row][column]
            for inner in range(column):
                entry = entry - factor[lower_row][inner] * factor[column][inner]
            factor[lower_row][column] = entry / pivot
    forward = []
    for row_at in range(4):
        entry = gradient[row_at]
        for inner in range(row_at):
            entry = entry - factor[row_at][inner] * forward[inner]
        forward.append(entry / factor[row_at][row_at])
    solved = [None, None, None, None]
    for row_at in reversed(range(4)):
        entry = forward[row_at]
        for inner in range(row_at + 1, 4):
            entry = entry - factor[inner][row_at] * solved[inner]
        solved[row_at] = entry / factor[row_at][row_at]
    return solved


def kernel(
    bricks, blocks, pixel_total, remote,
    values_ref, sersic_ref, psf_ref, flag_ref, owner_ref, cell_ref, exposure_ref, noise_ref,
    out_ref,
    rows_ref, hits_ref, rank_ref, slots_ref, gram_ref,
    taps, coef, even_acc, img_a, img_b, img_c, exposure_t,
    out_rows, in_rows, out_sums, in_sums, chi_out, chi_in,
    send_sem, recv_sem, back_send_sem, back_recv_sem, chi_send_sem, chi_recv_sem,
):
    if remote:
        me = lax.axis_index("brick")
        lane = lax.axis_index("blk")
        barrier = pltpu.get_barrier_semaphore()

        def greet(k, carry):
            pl.semaphore_signal(barrier, inc=1, device_id={"brick": (me + k) % bricks}, device_id_type=MESH)
            return carry

        def greet_block(k, carry):
            pl.semaphore_signal(barrier, inc=1, device_id={"blk": (lane + k) % blocks}, device_id_type=MESH)
            return carry

        lax.fori_loop(1, bricks, greet, 0)
        lax.fori_loop(1, blocks, greet_block, 0)

    rows = source_rows(values_ref[...], sersic_ref[...], psf_ref[...], flag_ref[...], cell_ref[...])
    rows_ref[...] = rows
    owner = owner_ref[...].astype(F32)
    owner_all = jnp.broadcast_to(owner, (LANES, LANES))
    earlier = lax.broadcasted_iota(jnp.int32, (LANES, LANES), 0) < lax.broadcasted_iota(jnp.int32, (LANES, LANES), 1)
    same = jnp.where((owner_all.T == owner_all) & earlier, 1.0, 0.0)
    rank = jnp.sum(same, axis=0, keepdims=True)
    rank_ref[...] = rank
    bricks_at = lax.broadcasted_iota(jnp.int32, (bricks, LANES), 0).astype(F32)
    hits = jnp.where(bricks_at == owner, 1.0, 0.0)
    hits_ref[...] = hits
    by_rank = jnp.concatenate([jnp.where(rank == float(r), rows, 0.0) for r in range(CAP)], axis=0)
    out_rows[:, 0, :] = dot(hits, by_rank, 1, 1)

    def row(k):
        return rows_ref[k : k + 1, :]

    build_taps(row, taps, coef, 0)
    dy = coordinates(row)

    def own_images(q, carry):
        dx, radius_sq, image, slope = images(q, row, dy)
        over = slope / radius_sq
        at = pl.ds(pl.multiple_of(q * TILE, TILE), TILE)
        img_a[0, at, :] = image
        img_a[1, at, :] = over * dx
        img_a[2, at, :] = over * dy
        img_a[3, at, :] = slope - row(SLOPE) * image
        return carry

    lax.fori_loop(0, TILE, own_images, 0)

    if remote:
        pl.semaphore_wait(barrier, bricks - 1 + blocks - 1)

        def message(k):
            to = (me + k) % bricks
            return pltpu.make_async_remote_copy(
                src_ref=out_rows.at[to], dst_ref=in_rows.at[me],
                send_sem=send_sem.at[k], recv_sem=recv_sem.at[k],
                device_id={"brick": to}, device_id_type=MESH,
            )

        def start_message(k, carry):
            message(k).start()
            return carry

        lax.fori_loop(1, bricks, start_message, 0)
        in_rows[me] = out_rows[me]
    else:
        in_rows[...] = out_rows[...]

    blur(4, lambda image: 0, img_a, img_b, img_c, coef, even_acc)
    pairs = [(i, j) for i in range(4) for j in range(i, 4)]

    def gram(step, sums):
        at = pl.ds(pl.multiple_of(step * 8, 8), 8)
        parts = [img_c[k, at, :] for k in range(4)]
        return tuple(s + parts[i] * parts[j] for s, (i, j) in zip(sums, pairs))

    sums = lax.fori_loop(0, PIXELS // 8, gram, tuple(jnp.zeros((8, LANES), F32) for _ in pairs))
    for k, s in enumerate(sums):
        gram_ref[k : k + 1, :] = jnp.sum(s, axis=0, keepdims=True)
    cells = exposure_ref.shape[0]
    for k in range(PIXELS // LANES):
        part = exposure_ref[:, k * LANES : (k + 1) * LANES]
        exposure_t[k * LANES : (k + 1) * LANES, :] = part.T

    if remote:

        def await_message(k, carry):
            message(k).wait_send()
            message(k).wait_recv()
            return carry

        lax.fori_loop(1, bricks, await_message, 0)

    received = in_rows[:, 0, :]
    stacked = jnp.concatenate([received, pltpu.roll(received, LANES // 2, 1)], axis=0)
    slots_ref[...] = stacked.T

    def slot_row(block):
        return lambda k: slots_ref[block * VALS + k : block * VALS + k + 1, :]

    cells_at = lax.broadcasted_iota(jnp.int32, (cells, LANES), 0).astype(F32) + 1.0
    for block in range(2):
        srow = slot_row(block)
        build_taps(srow, taps, coef, block)
        sdy = coordinates(srow)

        def slot_images(q, carry, srow=srow, sdy=sdy, block=block):
            dx, radius_sq, image, slope = images(q, srow, sdy)
            at = pl.ds(pl.multiple_of(q * TILE, TILE), TILE)
            img_a[block, at, :] = image
            img_a[2 + block, at, :] = slope / radius_sq
            return carry

        lax.fori_loop(0, TILE, slot_images, 0)
    blur(2, lambda image: image, img_a, img_b, img_c, coef, even_acc)
    model = None
    chosen = []
    for block in range(2):
        srow = slot_row(block)
        pick = jnp.where(cells_at == srow(CELL), 1.0, 0.0)
        chosen.append(pick)
        part = dot(img_c[block], pick * srow(AMP), 1, 1)
        model = part if model is None else model + part
    weights = noise_ref[...] * noise_ref[...]
    misfit = exposure_t[...] - model
    weighted = weights * misfit
    chi = jnp.sum(weighted * misfit, axis=0, keepdims=True)
    chi = jnp.concatenate([chi, jnp.zeros((1, LANES - cells), F32)], axis=1)
    chi_out[0, :, :] = chi
    chi_in[0, :, :] = chi
    if remote:

        def chi_message(k):
            return pltpu.make_async_remote_copy(
                src_ref=chi_out.at[0], dst_ref=chi_in.at[k],
                send_sem=chi_send_sem.at[k], recv_sem=chi_recv_sem.at[k],
                device_id={"blk": (lane + k) % blocks}, device_id_type=MESH,
            )

        def start_chi(k, carry):
            chi_message(k).start()
            return carry

        lax.fori_loop(1, blocks, start_chi, 0)
    for block in range(2):
        img_c[block] = dot(weighted, chosen[block])
    blur(2, lambda image: image, img_c, img_b, img_c, coef, even_acc)
    back = []
    for block in range(2):
        srow = slot_row(block)
        sdy = coordinates(srow)

        def project(q, sums, srow=srow, sdy=sdy, block=block):
            at = pl.ds(pl.multiple_of(q * TILE, TILE), TILE)
            dx, radius_sq = line_of(q, srow, sdy)
            adjoint = img_c[block, at, :]
            over = img_a[2 + block, at, :] * adjoint
            return (
                sums[0] + img_a[block, at, :] * adjoint,
                sums[1] + over * dx,
                sums[2] + over * sdy,
                sums[3] + over * radius_sq,
            )

        sums = lax.fori_loop(0, TILE, project, tuple(jnp.zeros((TILE, LANES), F32) for _ in range(4)))
        sums = [jnp.sum(s, axis=0, keepdims=True) for s in sums]
        sums[3] = sums[3] - srow(SLOPE) * sums[0]
        weight = dot(jnp.broadcast_to(weights, (8, cells)), chosen[block])[0:1]
        back.append(jnp.concatenate(sums + [weight, jnp.zeros((VALS - 5, LANES), F32)], axis=0))
    back = jnp.concatenate(back + [jnp.zeros((LANES - 2 * VALS, LANES), F32)], axis=0).T
    out_sums[:, 0, :] = back[0:bricks] + pltpu.roll(back[bricks:], LANES // 2, 1)

    if remote:

        def answer(k):
            to = (me + k) % bricks
            return pltpu.make_async_remote_copy(
                src_ref=out_sums.at[to], dst_ref=in_sums.at[me],
                send_sem=back_send_sem.at[k], recv_sem=back_recv_sem.at[k],
                device_id={"brick": to}, device_id_type=MESH,
            )

        def start_answer(k, carry):
            answer(k).start()
            return carry

        def await_answer(k, carry):
            answer(k).wait_send()
            answer(k).wait_recv()
            return carry

        def await_chi(k, carry):
            chi_message(k).wait_send()
            chi_message(k).wait_recv()
            return carry

        lax.fori_loop(1, bricks, start_answer, 0)
        in_sums[me] = out_sums[me]
        lax.fori_loop(1, blocks, await_chi, 0)
        lax.fori_loop(1, bricks, await_answer, 0)
    else:
        in_sums[...] = out_sums[...]

    group = chi_in[0]
    if remote:
        for k in range(1, blocks):
            group = group + chi_in[k]
    group_chi = jnp.sum(group, axis=1, keepdims=True)
    damping = BASE_DAMPING + MISFIT_SCALE * group_chi / pixel_total
    by_rank = dot(in_sums[:, 0, :].T, hits_ref[...])
    rank = rank_ref[...]
    mine = None
    for r in range(CAP):
        part = jnp.where(rank == float(r), by_rank[r * VALS : r * VALS + 8], 0.0)
        mine = part if mine is None else mine + part
    amp = row(AMP)
    scale = [ZERO_POINT, amp, amp, amp * (1.0 - row(POINT))]
    weight = mine[4:5]
    gradient = [scale[k] * mine[k : k + 1] for k in range(4)]
    curvature = [[None] * 4 for _ in range(4)]
    for k, (i, j) in enumerate(pairs):
        entry = gram_ref[k : k + 1, :] * (scale[i] * scale[j]) * weight
        curvature[i][j] = entry
        curvature[j][i] = entry
    delta = damped_solve(curvature, gradient, jnp.broadcast_to(damping, (1, LANES)))
    out_ref[...] = values_ref[...] + jnp.concatenate(delta, axis=0)


def step(bricks, blocks, remote, parameters, sersic, psf_width, point_flag, owner_brick, cell_index, exposure, inv_noise):
    sources, cells = parameters.shape[1], exposure.shape[0]
    vmem = pl.BlockSpec(memory_space=pltpu.VMEM)
    dma = pltpu.SemaphoreType.DMA
    params = dict(vmem_limit_bytes=60000 * 1024)
    if remote:
        params.update(collective_id=0, has_side_effects=True)
    return pl.pallas_call(
        functools.partial(kernel, bricks, blocks, blocks * cells * PIXELS, remote),
        out_shape=jax.ShapeDtypeStruct((4, sources), F32),
        in_specs=[vmem] * 8,
        out_specs=vmem,
        scratch_shapes=[
            pltpu.VMEM((VALS, LANES), F32),
            pltpu.VMEM((bricks, LANES), F32),
            pltpu.VMEM((1, LANES), F32),
            pltpu.VMEM((LANES, LANES), F32),
            pltpu.VMEM((16, LANES), F32),
            pltpu.VMEM((2 * TILE, 8, LANES), F32),
            pltpu.VMEM((2, 2, HALF, HALF, 8, LANES), F32),
            pltpu.VMEM((2, HALF, 8, LANES), F32),
            pltpu.VMEM((4, PIXELS, LANES), F32),
            pltpu.VMEM((4, PIXELS, LANES), F32),
            pltpu.VMEM((4, PIXELS, LANES), F32),
            pltpu.VMEM((PIXELS, cells), F32),
            pltpu.VMEM((bricks, 1, LANES), F32),
            pltpu.VMEM((bricks, 1, LANES), F32),
            pltpu.VMEM((bricks, 1, LANES), F32),
            pltpu.VMEM((bricks, 1, LANES), F32),
            pltpu.VMEM((1, 1, LANES), F32),
            pltpu.VMEM((blocks, 1, LANES), F32),
            dma((bricks,)),
            dma((bricks,)),
            dma((bricks,)),
            dma((bricks,)),
            dma((blocks,)),
            dma((blocks,)),
        ],
        compiler_params=pltpu.CompilerParams(**params),
    )(
        parameters,
        sersic.reshape(1, sources),
        psf_width.reshape(1, sources),
        point_flag.reshape(1, sources),
        owner_brick.reshape(1, sources),
        cell_index.reshape(1, sources),
        exposure,
        inv_noise.reshape(1, cells),
    )


def solution(mesh):
    bricks, blocks = mesh.shape["brick"], mesh.shape["blk"]
    both = ("brick", "blk")
    in_specs = (P(None, both), P(both), P(both), P(both), P(both, None), P(both), P(both, None), P(both))
    return jax.shard_map(
        functools.partial(step, bricks, blocks, True),
        mesh=mesh, in_specs=in_specs, out_specs=P(None, both), check_vma=False,
    )
```

```python
import functools
import math

import jax
import jax.numpy as jnp
from jax import lax
from jax.experimental import pallas as pl
from jax.experimental.pallas import tpu as pltpu
from jax.sharding import PartitionSpec as P

TILE = 32
PIXELS = TILE * TILE
HALF = TILE // 2
PITCH = TILE + 1
LINES = 1096
SERIES = 96
CAP = 4
VALS = 32
LANES = 128
WIDE = 256
ZERO_POINT = 30.0
BASE_DAMPING = 0.1
MISFIT_SCALE = 0.05
HIGHEST = lax.Precision.HIGHEST
MESH = pl.DeviceIdType.MESH
F32 = jnp.float32
BF16 = jnp.bfloat16

CX, CY, C1, C0, LN, INVN, ITV, NORM, SLOPE, CELL = range(10)


def dot(a, b, ca=1, cb=0):
    return lax.dot_general(
        a, b, (((ca,), (cb,)), ((), ())), precision=HIGHEST, preferred_element_type=F32
    )


def series(shape_value, cutoff):
    chain = SERIES // 8
    at = lax.broadcasted_iota(jnp.int32, (8, LANES), 0) * chain
    total = jnp.zeros((8, LANES), F32)
    product = jnp.ones((8, LANES), F32)
    for step in reversed(range(chain)):
        k = at + (step + 1)
        ratio = cutoff / (shape_value + k.astype(F32))
        live = k < SERIES
        total = jnp.where(live, ratio * (1.0 + total), 0.0)
        product = jnp.where(live, product * ratio, product)
    whole = total[7:8]
    last = product[7:8]
    for j in reversed(range(7)):
        whole = total[j : j + 1] + product[j : j + 1] * whole
        last = last * product[j : j + 1]
    return 1.0 + whole, last


def source_rows(values, sersic, psf_width, point, cell):
    flux, shift_x, shift_y, log_radius = (values[k : k + 1] for k in range(4))
    inverse_index = 1.0 / sersic
    bfactor = 2.0 * sersic - 1.0 / 3.0 + 4.0 / (405.0 * sersic)
    cutoff = bfactor * jnp.exp((math.log(0.5 * TILE) - log_radius) * inverse_index)
    total, last = series(2.0 * sersic, cutoff)
    log_norm = math.log(math.pi * 0.25 * TILE * TILE) - cutoff + jnp.log(total)
    slope = 2.0 - (2.0 * sersic - cutoff * last) * inverse_index / total
    inv_two_var = 0.5 / (psf_width * psf_width)
    norm_psf = 1.0 / (math.sqrt(2.0 * math.pi) * psf_width)
    is_point = point == 1
    log_itv = jnp.log(inv_two_var)
    rows = [None] * VALS
    rows[CX] = shift_x
    rows[CY] = shift_y
    rows[C1] = jnp.where(is_point, 1.0, 0.5 * inverse_index)
    rows[C0] = jnp.where(is_point, log_itv, jnp.log(bfactor) - log_radius * inverse_index)
    rows[LN] = jnp.where(is_point, math.log(math.pi) - log_itv, log_norm) - jnp.log(ZERO_POINT * flux)
    rows[INVN] = jnp.where(is_point, 2.0, inverse_index)
    rows[ITV] = jnp.where(is_point, 1.0e4, inv_two_var)
    rows[NORM] = jnp.where(is_point, 1.0, norm_psf)
    rows[SLOPE] = slope
    rows[CELL] = (cell + 1).astype(F32)
    zero = jnp.zeros_like(flux)
    return jnp.concatenate([zero if row is None else row for row in rows], axis=0)


def split(x):
    high = x.astype(BF16)
    return high, (x - high.astype(F32)).astype(BF16)


def product(a, b, cb=0):
    return lax.dot_general(a, b, (((1,), (cb,)), ((), ())), preferred_element_type=F32)


def blur_coefficients(row, taps, spread, coef, at):
    apart = lax.broadcasted_iota(jnp.int32, (TILE, LANES), 0).astype(F32)
    taps[...] = jnp.exp(-(apart * apart) * row(ITV)) * (0.5 * row(NORM))
    for d in range(TILE):
        value = jnp.broadcast_to(taps[d : d + 1, :], (8, LANES))
        spread[TILE - 1 + d] = value
        spread[TILE - 1 - d] = value
    for q in range(HALF):
        near = spread[TILE - 1 - q : TILE - 1 - q + HALF]
        far = spread[q : q + HALF]
        coef[at, 0, q] = near + far
        coef[at, 1, q] = near - far


def blur_lines(load, store, coef, at, parts, even_acc):
    for q in range(HALF):
        low, high = load(q), load(TILE - 1 - q)
        parts[0, q] = low + high
        parts[1, q] = low - high
    for parity in range(2):
        for group in range(2):
            span = slice(group * 8, group * 8 + 8)
            acc = None
            for q in range(HALF):
                term = coef[at, parity, q, span][None] * parts[parity, q][:, None]
                acc = term if acc is None else acc + term
            if parity == 0:
                even_acc[group] = acc
            else:
                even = even_acc[group]
                for k in range(8):
                    store(group * 8 + k, even[:, k] + acc[:, k])
                    store(TILE - 1 - group * 8 - k, even[:, k] - acc[:, k])


def blur(first, count, at_of, src, mid, dst, coef, parts, even_acc):
    def along_major(step, carry):
        image, start = first + step // 2, (step % 2) * 16

        def load(q):
            return src[image, pl.ds(q * PITCH + start, 16), :].reshape(2, 8, LANES)

        def store(q, value):
            mid[image, pl.ds(q * PITCH + start, 16), :] = value.reshape(16, LANES)

        blur_lines(load, store, coef, at_of(image), parts, even_acc)
        return carry

    def along_minor(step, carry):
        image, start = first + step // 2, (step % 2) * 16

        def load(p):
            return mid[image, pl.ds(start * PITCH + p, 16, stride=PITCH), :].reshape(2, 8, LANES)

        def store(p, value):
            dst[image, pl.ds(p * PITCH + start, 16), :] = value.reshape(16, LANES)

        blur_lines(load, store, coef, at_of(image), parts, even_acc)
        return carry

    lax.fori_loop(0, 2 * count, along_major, 0)
    lax.fori_loop(0, 2 * count, along_minor, 0)


def offsets(row, dy_ref, at):
    t_p = lax.broadcasted_iota(jnp.int32, (TILE, LANES), 0).astype(F32) + (0.5 - 0.5 * TILE)
    dy = t_p - row(CY)
    dy_ref[at, 0] = dy
    dy_ref[at, 1] = dy * dy


def column(q, row):
    return q.astype(F32) + (0.5 - 0.5 * TILE) - row(CX)


def images(q, row, dy_ref, at):
    dx = column(q, row)
    radius_sq = dy_ref[at, 1] + dx * dx
    power = jnp.exp(row(C1) * jnp.log(radius_sq) + row(C0))
    image = jnp.exp(-power - row(LN))
    over = image * (power * row(INVN)) / radius_sq
    return dx, radius_sq, image, over


def damped_solve(curvature, gradient, damping):
    system = [[curvature[first][second] for second in range(4)] for first in range(4)]
    for first in range(4):
        system[first][first] = system[first][first] + damping * (1.0 + curvature[first][first])
    factor = [[None for second in range(4)] for first in range(4)]
    for column in range(4):
        pivot = system[column][column]
        for inner in range(column):
            pivot = pivot - factor[column][inner] * factor[column][inner]
        pivot = jnp.sqrt(pivot)
        factor[column][column] = pivot
        for lower_row in range(column + 1, 4):
            entry = system[lower_row][column]
            for inner in range(column):
                entry = entry - factor[lower_row][inner] * factor[column][inner]
            factor[lower_row][column] = entry / pivot
    forward = []
    for row_at in range(4):
        entry = gradient[row_at]
        for inner in range(row_at):
            entry = entry - factor[row_at][inner] * forward[inner]
        forward.append(entry / factor[row_at][row_at])
    solved = [None, None, None, None]
    for row_at in reversed(range(4)):
        entry = forward[row_at]
        for inner in range(row_at + 1, 4):
            entry = entry - factor[inner][row_at] * solved[inner]
        solved[row_at] = entry / factor[row_at][row_at]
    return solved


def kernel(
    bricks, blocks, pixel_total, remote,
    values_ref, sersic_ref, psf_ref, flag_ref, owner_ref, cell_ref, exposure_ref, noise_ref,
    out_ref,
    rows_ref, hits_ref, rank_ref, slots_ref, gram_ref, taps, spread, coef, parts, even_acc, dy_ref,
    img_a, img_b, img_c, img_d, img_e, exposure_t, weighted_ref,
    out_rows, in_rows, out_sums, in_sums, chi_out, chi_in,
    send_sem, recv_sem, back_send_sem, back_recv_sem, chi_send_sem, chi_recv_sem,
):
    if remote:
        me = lax.axis_index("brick")
        lane = lax.axis_index("blk")
        barrier = pltpu.get_barrier_semaphore()

        def around(here, k, count):
            there = here + k
            return jnp.where(there >= count, there - count, there)

        def greet(k, carry):
            pl.semaphore_signal(barrier, inc=1, device_id={"brick": around(me, k, bricks)}, device_id_type=MESH)
            return carry

        def greet_block(k, carry):
            pl.semaphore_signal(barrier, inc=1, device_id={"blk": around(lane, k, blocks)}, device_id_type=MESH)
            return carry

        lax.fori_loop(1, bricks, greet, 0, unroll=7)
        lax.fori_loop(1, blocks, greet_block, 0)

    rows = source_rows(values_ref[...], sersic_ref[...], psf_ref[...], flag_ref[...], cell_ref[...])
    rows_ref[...] = rows
    owner = owner_ref[...].astype(F32)
    owner_all = jnp.broadcast_to(owner, (LANES, LANES))
    earlier = lax.broadcasted_iota(jnp.int32, (LANES, LANES), 0) < lax.broadcasted_iota(jnp.int32, (LANES, LANES), 1)
    same = jnp.where((owner_all.T == owner_all) & earlier, 1.0, 0.0)
    rank = jnp.sum(same, axis=0, keepdims=True)
    rank_ref[...] = rank
    bricks_at = lax.broadcasted_iota(jnp.int32, (bricks, LANES), 0).astype(F32)
    hits = jnp.where(bricks_at == owner, 1.0, 0.0)
    hits_ref[...] = hits
    by_rank = jnp.concatenate([jnp.where(rank == float(r), rows, 0.0) for r in range(CAP)], axis=0)
    out_rows[:, 0, :] = dot(hits, by_rank, 1, 1)

    def row(k):
        return rows_ref[k : k + 1, :]

    blur_coefficients(row, taps, spread, coef, 2)
    offsets(row, dy_ref, 2)

    def own_images(q, carry):
        dx, radius_sq, image, over = images(q, row, dy_ref, 2)
        at = pl.ds(q * PITCH, TILE)
        img_d[0, at, :] = image
        img_d[1, at, :] = over * dx
        img_d[2, at, :] = over * dy_ref[2, 0]
        img_d[3, at, :] = over * radius_sq - row(SLOPE) * image
        return carry

    lax.fori_loop(0, TILE, own_images, 0, unroll=2)

    def own_blur(first, count):
        blur(first, count, lambda image: 2, img_d, img_e, img_d, coef, parts, even_acc)

    own_blur(0, 1)
    if remote:
        pl.semaphore_wait(barrier, bricks - 1 + blocks - 1)

        def message(k):
            to = around(me, k, bricks)
            return pltpu.make_async_remote_copy(
                src_ref=out_rows.at[to], dst_ref=in_rows.at[me],
                send_sem=send_sem.at[k], recv_sem=recv_sem.at[k],
                device_id={"brick": to}, device_id_type=MESH,
            )

        def start_message(k, carry):
            message(k).start()
            return carry

        lax.fori_loop(1, bricks, start_message, 0, unroll=7)
        in_rows[me] = out_rows[me]
    else:
        in_rows[...] = out_rows[...]

    own_blur(1, 2)
    cells = exposure_ref.shape[0]
    for k in range(PIXELS // LANES):
        part = exposure_ref[:, k * LANES : (k + 1) * LANES].T
        exposure_t[k * LANES : (k + 1) * LANES, :] = jnp.concatenate([part, part], axis=1)

    if remote:

        def await_message(k, carry):
            message(k).wait_send()
            message(k).wait_recv()
            return carry

        lax.fori_loop(1, bricks, await_message, 0, unroll=7)

    received = in_rows[:, 0, :]
    stacked = jnp.concatenate([received, pltpu.roll(received, LANES // 2, 1)], axis=0).T
    slots_ref[:, :LANES] = stacked[:VALS]
    slots_ref[:, LANES:] = stacked[VALS : 2 * VALS]

    def slot_rows(half):
        return lambda k: slots_ref[k : k + 1, half * LANES : (half + 1) * LANES]

    for half in range(2):
        slot = slot_rows(half)
        blur_coefficients(slot, taps, spread, coef, half)
        offsets(slot, dy_ref, half)

        def slot_images(q, carry, slot=slot, half=half):
            dx, radius_sq, image, over = images(q, slot, dy_ref, half)
            at = pl.ds(q * PITCH, TILE)
            img_a[half, at, :] = image
            img_b[half, at, :] = over
            return carry

        lax.fori_loop(0, TILE, slot_images, 0, unroll=4)
    blur(0, 2, lambda image: image, img_a, img_e, img_c, coef, parts, even_acc)
    cells_at = lax.broadcasted_iota(jnp.int32, (cells, WIDE), 0).astype(F32) + 1.0
    chosen = jnp.where(cells_at == slots_ref[CELL : CELL + 1, :], 1.0, 0.0)
    pick = jnp.concatenate([chosen, chosen], axis=0).astype(BF16)
    pick_wide = jnp.concatenate([pick, pick], axis=1)
    noise = noise_ref[...]
    weights = noise * noise
    weights_twice = jnp.concatenate([weights, weights], axis=1)
    is_high = lax.broadcasted_iota(jnp.int32, (1, 2 * cells), 1) < cells

    def lines_of(ref, half, t):
        lines = [ref[half, pl.ds((t * 8 + k) * PITCH, TILE), :] for k in range(8)]
        return jnp.concatenate(lines, axis=0)

    def residual(t, chi):
        tiles = jnp.concatenate([lines_of(img_c, half, t) for half in range(2)], axis=1)
        model = product(jnp.concatenate(split(tiles), axis=1), pick_wide, 1)
        at = pl.ds(pl.multiple_of(t * 8 * TILE, 8 * TILE), 8 * TILE)
        misfit = exposure_t[at, :] - model
        weighted = weights_twice * misfit
        high = weighted.astype(BF16).astype(F32)
        weighted_ref[at, :] = jnp.where(is_high, high, weighted - high).astype(BF16)
        return chi + jnp.sum((weighted * misfit).reshape(TILE, 8, 2 * cells), axis=0)

    chi = lax.fori_loop(0, 4, residual, jnp.zeros((8, 2 * cells), F32))
    chi = jnp.sum(chi, axis=0, keepdims=True)[:, :cells]
    chi = jnp.concatenate([chi, jnp.zeros((1, LANES - cells), F32)], axis=1)
    chi_out[0, :, :] = chi
    chi_in[0, :, :] = chi
    if remote:

        def chi_message(k):
            return pltpu.make_async_remote_copy(
                src_ref=chi_out.at[0], dst_ref=chi_in.at[k],
                send_sem=chi_send_sem.at[k], recv_sem=chi_recv_sem.at[k],
                device_id={"blk": around(lane, k, blocks)}, device_id_type=MESH,
            )

        def start_chi(k, carry):
            chi_message(k).start()
            return carry

        lax.fori_loop(1, blocks, start_chi, 0)

    def gather(t, carry):
        at = pl.ds(pl.multiple_of(t * 8 * TILE, 8 * TILE), 8 * TILE)
        tiles = product(weighted_ref[at, :], pick)
        for half in range(2):
            for k in range(8):
                line = tiles[k * TILE : (k + 1) * TILE, half * LANES : (half + 1) * LANES]
                img_c[half, pl.ds((t * 8 + k) * PITCH, TILE), :] = line
        return carry

    lax.fori_loop(0, 4, gather, 0)
    blur(0, 2, lambda image: image, img_c, img_e, img_c, coef, parts, even_acc)
    halves = []
    for half in range(2):
        slot = slot_rows(half)

        def project(q, sums, slot=slot, half=half):
            at = pl.ds(q * PITCH, TILE)
            dx = column(q, slot)
            adjoint = img_c[half, at, :]
            over = img_b[half, at, :] * adjoint
            plain = img_a[half, at, :] * adjoint
            moment = over * dy_ref[half, 0]
            second = moment * dy_ref[half, 0]
            plain, over, moment, second = (
                x[0:8] + x[8:16] + (x[16:24] + x[24:32]) for x in (plain, over, moment, second)
            )
            over = over * dx
            return sums[0] + plain, sums[1] + over, sums[2] + moment, sums[3] + (second + over * dx)

        sums = lax.fori_loop(0, TILE, project, tuple(jnp.zeros((8, LANES), F32) for _ in range(4)), unroll=4)
        sums = [jnp.sum(s, axis=0, keepdims=True) for s in sums]
        sums[3] = sums[3] - slot(SLOPE) * sums[0]
        halves.append(jnp.concatenate(sums, axis=0))
    sums = [jnp.concatenate(halves, axis=1)]
    weight = dot(jnp.broadcast_to(weights, (8, cells)), chosen)[0:1]
    back = jnp.concatenate(sums + [weight, jnp.zeros((VALS - 5, WIDE), F32)], axis=0)
    back = jnp.concatenate([back[:, :LANES], back[:, LANES:], jnp.zeros((LANES - 2 * VALS, LANES), F32)], axis=0).T
    out_sums[:, 0, :] = back[0:bricks] + pltpu.roll(back[bricks:], LANES // 2, 1)

    if remote:

        def answer(k):
            to = around(me, k, bricks)
            return pltpu.make_async_remote_copy(
                src_ref=out_sums.at[to], dst_ref=in_sums.at[me],
                send_sem=back_send_sem.at[k], recv_sem=back_recv_sem.at[k],
                device_id={"brick": to}, device_id_type=MESH,
            )

        def start_answer(k, carry):
            answer(k).start()
            return carry

        def await_answer(k, carry):
            answer(k).wait_send()
            answer(k).wait_recv()
            return carry

        def await_chi(k, carry):
            chi_message(k).wait_send()
            chi_message(k).wait_recv()
            return carry

        lax.fori_loop(1, bricks, start_answer, 0, unroll=7)
        in_sums[me] = out_sums[me]
    else:
        in_sums[...] = out_sums[...]

    own_blur(3, 1)
    pairs = [(i, j) for i in range(4) for j in range(i, 4)]

    def gram(p, sums):
        for t in range(TILE // 8):
            at = pl.ds(p * PITCH + t * 8, 8)
            own = [img_d[k, at, :] for k in range(4)]
            sums = tuple(s + own[i] * own[j] for s, (i, j) in zip(sums, pairs))
        return sums

    sums = lax.fori_loop(0, TILE, gram, tuple(jnp.zeros((8, LANES), F32) for _ in pairs))
    for k, s in enumerate(sums):
        gram_ref[k : k + 1, :] = jnp.sum(s, axis=0, keepdims=True)

    if remote:
        lax.fori_loop(1, blocks, await_chi, 0)
        lax.fori_loop(1, bricks, await_answer, 0, unroll=7)

    group = chi_in[0]
    if remote:
        for k in range(1, blocks):
            group = group + chi_in[k]
    group_chi = jnp.sum(group, axis=1, keepdims=True)
    damping = BASE_DAMPING + MISFIT_SCALE * group_chi / pixel_total
    by_rank = dot(in_sums[:, 0, :].T, hits_ref[...])
    rank = rank_ref[...]
    mine = None
    for r in range(CAP):
        part = jnp.where(rank == float(r), by_rank[r * VALS : r * VALS + 8], 0.0)
        mine = part if mine is None else mine + part
    extended = jnp.where(flag_ref[...] == 1, 0.0, 1.0)
    per_flux = 1.0 / values_ref[0:1, :]
    scale = [per_flux, 1.0, 1.0, extended]
    weight = mine[4:5]
    gradient = [scale[k] * mine[k : k + 1] for k in range(4)]
    curvature = [[None] * 4 for _ in range(4)]
    for k, (i, j) in enumerate(pairs):
        entry = gram_ref[k : k + 1, :] * (scale[i] * scale[j]) * weight
        curvature[i][j] = entry
        curvature[j][i] = entry
    delta = damped_solve(curvature, gradient, jnp.broadcast_to(damping, (1, LANES)))
    out_ref[...] = values_ref[...] + jnp.concatenate(delta, axis=0)


def step(bricks, blocks, remote, parameters, sersic, psf_width, point_flag, owner_brick, cell_index, exposure, inv_noise):
    sources, cells = parameters.shape[1], exposure.shape[0]
    vmem = pl.BlockSpec(memory_space=pltpu.VMEM)
    dma = pltpu.SemaphoreType.DMA
    params = dict(vmem_limit_bytes=60000 * 1024)
    if remote:
        params.update(collective_id=0, has_side_effects=True)
    return pl.pallas_call(
        functools.partial(kernel, bricks, blocks, blocks * cells * PIXELS, remote),
        out_shape=jax.ShapeDtypeStruct((4, sources), F32),
        in_specs=[vmem] * 8,
        out_specs=vmem,
        scratch_shapes=[
            pltpu.VMEM((VALS, LANES), F32),
            pltpu.VMEM((bricks, LANES), F32),
            pltpu.VMEM((1, LANES), F32),
            pltpu.VMEM((VALS, WIDE), F32),
            pltpu.VMEM((16, LANES), F32),
            pltpu.VMEM((TILE, LANES), F32),
            pltpu.VMEM((2 * TILE, 8, LANES), F32),
            pltpu.VMEM((3, 2, HALF, HALF, 8, LANES), F32),
            pltpu.VMEM((2, HALF, 2, 8, LANES), F32),
            pltpu.VMEM((2, 2, 8, 8, LANES), F32),
            pltpu.VMEM((3, 2, TILE, LANES), F32),
            pltpu.VMEM((2, LINES, LANES), F32),
            pltpu.VMEM((2, LINES, LANES), F32),
            pltpu.VMEM((2, LINES, LANES), F32),
            pltpu.VMEM((4, LINES, LANES), F32),
            pltpu.VMEM((4, LINES, LANES), F32),
            pltpu.VMEM((PIXELS, 2 * cells), F32),
            pltpu.VMEM((PIXELS, 2 * cells), BF16),
            pltpu.VMEM((bricks, 1, LANES), F32),
            pltpu.VMEM((bricks, 1, LANES), F32),
            pltpu.VMEM((bricks, 1, LANES), F32),
            pltpu.VMEM((bricks, 1, LANES), F32),
            pltpu.VMEM((1, 1, LANES), F32),
            pltpu.VMEM((blocks, 1, LANES), F32),
            dma((bricks,)),
            dma((bricks,)),
            dma((bricks,)),
            dma((bricks,)),
            dma((blocks,)),
            dma((blocks,)),
        ],
        compiler_params=pltpu.CompilerParams(**params),
    )(
        parameters,
        sersic.reshape(1, sources),
        psf_width.reshape(1, sources),
        point_flag.reshape(1, sources),
        owner_brick.reshape(1, sources),
        cell_index.reshape(1, sources),
        exposure,
        inv_noise.reshape(1, cells),
    )


def solution(mesh):
    bricks, blocks = mesh.shape["brick"], mesh.shape["blk"]
    both = ("brick", "blk")
    in_specs = (P(None, both), P(both), P(both), P(both), P(both, None), P(both), P(both, None), P(both))
    return jax.shard_map(
        functools.partial(step, bricks, blocks, True),
        mesh=mesh, in_specs=in_specs, out_specs=P(None, both), check_vma=False,
    )
```

```python
import functools
import math

import jax
import jax.numpy as jnp
from jax import lax
from jax.experimental import pallas as pl
from jax.experimental.pallas import tpu as pltpu
from jax.sharding import PartitionSpec as P

TILE = 32
PIXELS = TILE * TILE
HALF = TILE // 2
PITCH = TILE + 1
LINES = 1096
SERIES = 96
CAP = 4
VALS = 32
BACK = 8
SIDE = 8
LANES = 128
ZERO_POINT = 30.0
BASE_DAMPING = 0.1
MISFIT_SCALE = 0.05
HIGHEST = lax.Precision.HIGHEST
MESH = pl.DeviceIdType.MESH
F32 = jnp.float32
BF16 = jnp.bfloat16

CX, CY, C1, C0, LN, INVN, ITV, NORM, SLOPE, CELL = range(10)


def peer_offsets():
    def hops(offset):
        return sum(min(step, SIDE - step) for step in offset)

    return sorted(((z, y) for z in range(SIDE) for y in range(SIDE)), key=lambda offset: (hops(offset), offset))


def dot(a, b, ca=1, cb=0):
    return lax.dot_general(
        a, b, (((ca,), (cb,)), ((), ())), precision=HIGHEST, preferred_element_type=F32
    )


def series(shape_value, cutoff):
    chain = SERIES // 8
    at = lax.broadcasted_iota(jnp.int32, (8, LANES), 0) * chain
    total = jnp.zeros((8, LANES), F32)
    product = jnp.ones((8, LANES), F32)
    for step in reversed(range(chain)):
        k = at + (step + 1)
        ratio = cutoff / (shape_value + k.astype(F32))
        live = k < SERIES
        total = jnp.where(live, ratio * (1.0 + total), 0.0)
        product = jnp.where(live, product * ratio, product)
    whole = total[7:8]
    last = product[7:8]
    for j in reversed(range(7)):
        whole = total[j : j + 1] + product[j : j + 1] * whole
        last = last * product[j : j + 1]
    return 1.0 + whole, last


def source_rows(values, sersic, psf_width, point, cell):
    flux, shift_x, shift_y, log_radius = (values[k : k + 1] for k in range(4))
    inverse_index = 1.0 / sersic
    bfactor = 2.0 * sersic - 1.0 / 3.0 + 4.0 / (405.0 * sersic)
    cutoff = bfactor * jnp.exp((math.log(0.5 * TILE) - log_radius) * inverse_index)
    total, last = series(2.0 * sersic, cutoff)
    log_norm = math.log(math.pi * 0.25 * TILE * TILE) - cutoff + jnp.log(total)
    slope = 2.0 - (2.0 * sersic - cutoff * last) * inverse_index / total
    inv_two_var = 0.5 / (psf_width * psf_width)
    norm_psf = 1.0 / (math.sqrt(2.0 * math.pi) * psf_width)
    is_point = point == 1
    log_itv = jnp.log(inv_two_var)
    rows = [None] * VALS
    rows[CX] = shift_x
    rows[CY] = shift_y
    rows[C1] = jnp.where(is_point, 1.0, 0.5 * inverse_index)
    rows[C0] = jnp.where(is_point, log_itv, jnp.log(bfactor) - log_radius * inverse_index)
    rows[LN] = jnp.where(is_point, math.log(math.pi) - log_itv, log_norm) - jnp.log(ZERO_POINT * flux)
    rows[INVN] = jnp.where(is_point, 2.0, inverse_index)
    rows[ITV] = jnp.where(is_point, 1.0e4, inv_two_var)
    rows[NORM] = jnp.where(is_point, 1.0, norm_psf)
    rows[SLOPE] = slope
    rows[CELL] = (cell + 1).astype(F32)
    zero = jnp.zeros_like(flux)
    return jnp.concatenate([zero if row is None else row for row in rows], axis=0)


def split(x):
    high = x.astype(BF16)
    return high, (x - high.astype(F32)).astype(BF16)


def product(a, b, cb=0):
    return lax.dot_general(a, b, (((1,), (cb,)), ((), ())), preferred_element_type=F32)


def blur_coefficients(row, taps, spread, coef, at):
    apart = lax.broadcasted_iota(jnp.int32, (TILE, LANES), 0).astype(F32)
    taps[...] = jnp.exp(-(apart * apart) * row(ITV)) * (0.5 * row(NORM))
    for d in range(TILE):
        value = jnp.broadcast_to(taps[d : d + 1, :], (8, LANES))
        spread[TILE - 1 + d] = value
        spread[TILE - 1 - d] = value
    for q in range(HALF):
        near = spread[TILE - 1 - q : TILE - 1 - q + HALF]
        far = spread[q : q + HALF]
        coef[at, 0, q] = near + far
        coef[at, 1, q] = near - far


def blur_lines(load, store, coef, at, parts, even_acc):
    for q in range(HALF):
        low, high = load(q), load(TILE - 1 - q)
        parts[0, q] = low + high
        parts[1, q] = low - high
    for parity in range(2):
        for group in range(2):
            span = slice(group * 8, group * 8 + 8)
            acc = None
            for q in range(HALF):
                term = coef[at, parity, q, span][None] * parts[parity, q][:, None]
                acc = term if acc is None else acc + term
            if parity == 0:
                even_acc[group] = acc
            else:
                even = even_acc[group]
                for k in range(8):
                    store(group * 8 + k, even[:, k] + acc[:, k])
                    store(TILE - 1 - group * 8 - k, even[:, k] - acc[:, k])


def blur(first, count, at_of, src, mid, dst, coef, parts, even_acc):
    def along_major(step, carry):
        image, start = first + step // 2, (step % 2) * 16

        def load(q):
            return src[image, pl.ds(q * PITCH + start, 16), :].reshape(2, 8, LANES)

        def store(q, value):
            mid[image, pl.ds(q * PITCH + start, 16), :] = value.reshape(16, LANES)

        blur_lines(load, store, coef, at_of(image), parts, even_acc)
        return carry

    def along_minor(step, carry):
        image, start = first + step // 2, (step % 2) * 16

        def load(p):
            return mid[image, pl.ds(start * PITCH + p, 16, stride=PITCH), :].reshape(2, 8, LANES)

        def store(p, value):
            dst[image, pl.ds(p * PITCH + start, 16), :] = value.reshape(16, LANES)

        blur_lines(load, store, coef, at_of(image), parts, even_acc)
        return carry

    lax.fori_loop(0, 2 * count, along_major, 0)
    lax.fori_loop(0, 2 * count, along_minor, 0)


def offsets(row, dy_ref, at):
    t_p = lax.broadcasted_iota(jnp.int32, (TILE, LANES), 0).astype(F32) + (0.5 - 0.5 * TILE)
    dy = t_p - row(CY)
    dy_ref[at, 0] = dy
    dy_ref[at, 1] = dy * dy


def column(q, row):
    return q.astype(F32) + (0.5 - 0.5 * TILE) - row(CX)


def images(q, row, dy_ref, at):
    dx = column(q, row)
    radius_sq = dy_ref[at, 1] + dx * dx
    power = jnp.exp(row(C1) * jnp.log(radius_sq) + row(C0))
    image = jnp.exp(-power - row(LN))
    over = image * (power * row(INVN)) / radius_sq
    return dx, radius_sq, image, over


def damped_solve(curvature, gradient, damping):
    system = [[curvature[first][second] for second in range(4)] for first in range(4)]
    for first in range(4):
        system[first][first] = system[first][first] + damping * (1.0 + curvature[first][first])
    factor = [[None for second in range(4)] for first in range(4)]
    for column in range(4):
        pivot = system[column][column]
        for inner in range(column):
            pivot = pivot - factor[column][inner] * factor[column][inner]
        pivot = jnp.sqrt(pivot)
        factor[column][column] = pivot
        for lower_row in range(column + 1, 4):
            entry = system[lower_row][column]
            for inner in range(column):
                entry = entry - factor[lower_row][inner] * factor[column][inner]
            factor[lower_row][column] = entry / pivot
    forward = []
    for row_at in range(4):
        entry = gradient[row_at]
        for inner in range(row_at):
            entry = entry - factor[row_at][inner] * forward[inner]
        forward.append(entry / factor[row_at][row_at])
    solved = [None, None, None, None]
    for row_at in reversed(range(4)):
        entry = forward[row_at]
        for inner in range(row_at + 1, 4):
            entry = entry - factor[inner][row_at] * solved[inner]
        solved[row_at] = entry / factor[row_at][row_at]
    return solved


def kernel(
    blocks, pixel_total, remote,
    values_hbm, sersic_hbm, psf_hbm, flag_hbm, owner_hbm, cell_hbm, exposure_hbm, noise_hbm,
    out_ref,
    values_ref, sersic_ref, psf_ref, flag_ref, owner_ref, cell_ref, exposure_ref, noise_ref,
    rows_ref, hits_ref, rank_ref, slots_ref, gram_ref, taps, spread, coef, parts, even_acc, dy_ref,
    img_a, img_b, img_c, img_d, img_e, exposure_t, weighted_ref,
    out_rows, in_rows, out_sums, in_sums, chi_out, chi_in,
    input_sem, send_sem, near_sem, far_sem, back_send_sem, back_sem, chi_send_sem, chi_sem,
):
    inputs = [
        pltpu.make_async_copy(source, target, input_sem.at[k])
        for k, (source, target) in enumerate(
            (
                (values_hbm, values_ref),
                (sersic_hbm, sersic_ref),
                (psf_hbm, psf_ref),
                (flag_hbm, flag_ref),
                (owner_hbm, owner_ref),
                (cell_hbm, cell_ref),
                (exposure_hbm, exposure_ref),
                (noise_hbm, noise_ref),
            )
        )
    ]
    for copy in inputs:
        copy.start()
    offsets_of = peer_offsets()
    peers = len(offsets_of)
    near = peers // 2
    if remote:
        me = lax.axis_index("brick")
        lane = lax.axis_index("blk")
        barrier = pltpu.get_barrier_semaphore()
        my_z, my_y = me // SIDE, me % SIDE
        plus_z = [((my_z + k) % SIDE) * SIDE for k in range(SIDE)]
        plus_y = [(my_y + k) % SIDE for k in range(SIDE)]

        def ahead(j):
            return plus_z[offsets_of[j][0]] + plus_y[offsets_of[j][1]]

        def behind(j):
            return plus_z[-offsets_of[j][0] % SIDE] + plus_y[-offsets_of[j][1] % SIDE]

        def around(k):
            return jnp.where(lane + k >= blocks, lane + k - blocks, lane + k)

        for j in reversed(range(1, peers)):
            pl.semaphore_signal(barrier, inc=1, device_id={"brick": ahead(j)}, device_id_type=MESH)
        for k in range(1, blocks):
            pl.semaphore_signal(barrier, inc=1, device_id={"blk": around(k)}, device_id_type=MESH)
    else:
        my_z, my_y = 0, 0
    for copy in inputs[:6]:
        copy.wait()

    rows = source_rows(values_ref[...], sersic_ref[...], psf_ref[...], flag_ref[...], cell_ref[...])
    rows_ref[...] = rows
    owner = owner_ref[...].astype(F32)
    owner_all = jnp.broadcast_to(owner, (LANES, LANES))
    earlier = lax.broadcasted_iota(jnp.int32, (LANES, LANES), 0) < lax.broadcasted_iota(jnp.int32, (LANES, LANES), 1)
    same = jnp.where((owner_all.T == owner_all) & earlier, 1.0, 0.0)
    rank = jnp.sum(same, axis=0, keepdims=True)
    rank_ref[...] = rank
    place = owner_ref[...]
    ahead_of_me = (((place >> 3) - my_z) & (SIDE - 1)) * SIDE + (((place & (SIDE - 1)) - my_y) & (SIDE - 1))
    for j, (z, y) in enumerate(offsets_of):
        hits_ref[j : j + 1, :] = jnp.where(ahead_of_me == z * SIDE + y, 1.0, 0.0)
    by_rank = jnp.concatenate([jnp.where(rank == float(r), rows, 0.0) for r in range(CAP)], axis=0)
    out_rows[:, 0, :] = dot(hits_ref[...], by_rank, 1, 1)

    def row(k):
        return rows_ref[k : k + 1, :]

    blur_coefficients(row, taps, spread, coef, 2)
    offsets(row, dy_ref, 2)

    def own_images(q, carry):
        dx, radius_sq, image, over = images(q, row, dy_ref, 2)
        at = pl.ds(q * PITCH, TILE)
        img_d[0, at, :] = image
        img_d[1, at, :] = over * dx
        img_d[2, at, :] = over * dy_ref[2, 0]
        img_d[3, at, :] = over * radius_sq - row(SLOPE) * image
        return carry

    lax.fori_loop(0, TILE, own_images, 0, unroll=4)

    def own_blur(first, count):
        blur(first, count, lambda image: 2, img_d, img_e, img_d, coef, parts, even_acc)

    own_blur(0, 2)
    if remote:
        pl.semaphore_wait(barrier, peers - 1 + blocks - 1)

        def send_row(source, target, j, to, sent, landed):
            pltpu.make_async_remote_copy(
                src_ref=source.at[j], dst_ref=target.at[j], send_sem=sent, recv_sem=landed,
                device_id={"brick": to}, device_id_type=MESH,
            ).start()

        def await_rows(ref, count, sem):
            pltpu.make_async_copy(ref.at[0:count], ref.at[0:count], sem).wait()

        for j in reversed(range(1, peers)):
            send_row(out_rows, in_rows, j, ahead(j), send_sem.at[0], (near_sem if j < near else far_sem).at[0])
        in_rows[0] = out_rows[0]
    else:
        in_rows[...] = out_rows[...]

    own_blur(2, 1)
    for copy in inputs[6:]:
        copy.wait()
    cells = exposure_ref.shape[0]
    for k in range(PIXELS // LANES):
        part = exposure_ref[:, k * LANES : (k + 1) * LANES].T
        exposure_t[k * LANES : (k + 1) * LANES, :] = jnp.concatenate([part, part], axis=1)

    cells_at = lax.broadcasted_iota(jnp.int32, (cells, LANES), 0).astype(F32) + 1.0
    picks = []

    def slot_rows(half):
        return lambda k: slots_ref[half, k : k + 1, :]

    def render(half):
        received = in_rows[half * near : (half + 1) * near, 0, :]
        turned = [received] + [pltpu.roll(received, LANES - r * VALS, 1) for r in range(1, CAP)]
        slots_ref[half] = jnp.concatenate(turned, axis=0).T[:VALS]
        slot = slot_rows(half)
        blur_coefficients(slot, taps, spread, coef, half)
        offsets(slot, dy_ref, half)

        def slot_images(q, carry):
            dx, radius_sq, image, over = images(q, slot, dy_ref, half)
            at = pl.ds(q * PITCH, TILE)
            img_a[half, at, :] = image
            img_b[half, at, :] = over
            return carry

        lax.fori_loop(0, TILE, slot_images, 0, unroll=8)
        blur(half, 1, lambda image: half, img_a, img_e, img_c, coef, parts, even_acc)
        chosen = jnp.where(cells_at == slot(CELL), 1.0, 0.0)
        picks.append(chosen)

    def lines_of(half, t):
        lines = [img_c[half, pl.ds((t * 8 + k) * PITCH, TILE), :] for k in range(8)]
        pick = jnp.concatenate([picks[half], picks[half]], axis=0).astype(BF16)
        tiles = jnp.concatenate(split(jnp.concatenate(lines, axis=0)), axis=1)
        return product(tiles, jnp.concatenate([pick, pick], axis=1), 1)

    def subtract_near(t, carry):
        at = pl.ds(pl.multiple_of(t * 8 * TILE, 8 * TILE), 8 * TILE)
        exposure_t[at, :] = exposure_t[at, :] - lines_of(0, t)
        return carry

    if remote:
        await_rows(in_rows, near - 1, near_sem.at[0])
    render(0)
    lax.fori_loop(0, 4, subtract_near, 0)
    if remote:
        await_rows(in_rows, peers - near, far_sem.at[0])
    render(1)
    noise = noise_ref[...]
    weights = noise * noise
    weights_twice = jnp.concatenate([weights, weights], axis=1)
    is_high = lax.broadcasted_iota(jnp.int32, (1, 2 * cells), 1) < cells

    def residual(t, chi):
        at = pl.ds(pl.multiple_of(t * 8 * TILE, 8 * TILE), 8 * TILE)
        misfit = exposure_t[at, :] - lines_of(1, t)
        weighted = weights_twice * misfit
        high = weighted.astype(BF16).astype(F32)
        weighted_ref[at, :] = jnp.where(is_high, high, weighted - high).astype(BF16)
        return chi + jnp.sum((weighted * misfit).reshape(TILE, 8, 2 * cells), axis=0)

    chi = lax.fori_loop(0, 4, residual, jnp.zeros((8, 2 * cells), F32))
    chi = jnp.sum(chi, axis=0, keepdims=True)[:, :cells]
    chi = jnp.concatenate([chi, jnp.zeros((1, LANES - cells), F32)], axis=1)
    chi_out[0, :, :] = chi
    chi_in[0, :, :] = chi
    if remote:

        for k in range(1, blocks):
            pltpu.make_async_remote_copy(
                src_ref=chi_out.at[0], dst_ref=chi_in.at[k], send_sem=chi_send_sem.at[0], recv_sem=chi_sem.at[0],
                device_id={"blk": around(k)}, device_id_type=MESH,
            ).start()

    def answer(half):
        slot = slot_rows(half)
        pick = jnp.concatenate([picks[half], picks[half]], axis=0).astype(BF16)

        def gather(t, carry):
            at = pl.ds(pl.multiple_of(t * 8 * TILE, 8 * TILE), 8 * TILE)
            tiles = product(weighted_ref[at, :], pick)
            for k in range(8):
                img_c[half, pl.ds((t * 8 + k) * PITCH, TILE), :] = tiles[k * TILE : (k + 1) * TILE]
            return carry

        def project(q, sums):
            at = pl.ds(q * PITCH, TILE)
            dx = column(q, slot)
            adjoint = img_c[half, at, :]
            over = img_b[half, at, :] * adjoint
            plain = img_a[half, at, :] * adjoint
            moment = over * dy_ref[half, 0]
            second = moment * dy_ref[half, 0]
            plain, over, moment, second = (
                x[0:8] + x[8:16] + (x[16:24] + x[24:32]) for x in (plain, over, moment, second)
            )
            over = over * dx
            return sums[0] + plain, sums[1] + over, sums[2] + moment, sums[3] + (second + over * dx)

        lax.fori_loop(0, 4, gather, 0)
        blur(half, 1, lambda image: half, img_c, img_e, img_c, coef, parts, even_acc)
        sums = lax.fori_loop(0, TILE, project, tuple(jnp.zeros((8, LANES), F32) for _ in range(4)), unroll=4)
        sums = [jnp.sum(s, axis=0, keepdims=True) for s in sums]
        sums[3] = sums[3] - slot(SLOPE) * sums[0]
        weight = dot(jnp.broadcast_to(weights, (8, cells)), picks[half])[0:1]
        back = jnp.concatenate(sums + [weight, jnp.zeros((LANES - 5, LANES), F32)], axis=0).T
        packed = back[0:near]
        for r in range(1, CAP):
            packed = packed + pltpu.roll(back[r * near : (r + 1) * near], r * BACK, 1)
        out_sums[half * near : (half + 1) * near, 0, :] = packed

    answer(1)
    if remote:
        for j in reversed(range(near, peers)):
            send_row(out_sums, in_sums, j, behind(j), back_send_sem.at[0], back_sem.at[0])
    answer(0)
    if remote:
        for j in reversed(range(1, near)):
            send_row(out_sums, in_sums, j, behind(j), back_send_sem.at[0], back_sem.at[0])
        in_sums[0] = out_sums[0]
    else:
        in_sums[...] = out_sums[...]

    own_blur(3, 1)
    pairs = [(i, j) for i in range(4) for j in range(i, 4)]

    def gram(p, sums):
        for t in range(TILE // 8):
            at = pl.ds(p * PITCH + t * 8, 8)
            own = [img_d[k, at, :] for k in range(4)]
            sums = tuple(s + own[i] * own[j] for s, (i, j) in zip(sums, pairs))
        return sums

    sums = lax.fori_loop(0, TILE, gram, tuple(jnp.zeros((8, LANES), F32) for _ in pairs))
    for k, s in enumerate(sums):
        gram_ref[k : k + 1, :] = jnp.sum(s, axis=0, keepdims=True)

    if remote:
        await_rows(chi_in, blocks - 1, chi_sem.at[0])
        await_rows(in_sums, peers - 1, back_sem.at[0])

    group = chi_in[0]
    if remote:
        for k in range(1, blocks):
            group = group + chi_in[k]
    group_chi = jnp.sum(group, axis=1, keepdims=True)
    damping = BASE_DAMPING + MISFIT_SCALE * group_chi / pixel_total
    by_rank = dot(in_sums[:, 0, :].T[: CAP * BACK], hits_ref[...])
    rank = rank_ref[...]
    mine = None
    for r in range(CAP):
        part = jnp.where(rank == float(r), by_rank[r * BACK : (r + 1) * BACK], 0.0)
        mine = part if mine is None else mine + part
    extended = jnp.where(flag_ref[...] == 1, 0.0, 1.0)
    per_flux = 1.0 / values_ref[0:1, :]
    scale = [per_flux, 1.0, 1.0, extended]
    weight = mine[4:5]
    gradient = [scale[k] * mine[k : k + 1] for k in range(4)]
    curvature = [[None] * 4 for _ in range(4)]
    for k, (i, j) in enumerate(pairs):
        entry = gram_ref[k : k + 1, :] * (scale[i] * scale[j]) * weight
        curvature[i][j] = entry
        curvature[j][i] = entry
    delta = damped_solve(curvature, gradient, jnp.broadcast_to(damping, (1, LANES)))
    out_ref[...] = jnp.concatenate(delta, axis=0)
    if remote:
        await_rows(out_rows, peers - 1, send_sem.at[0])
        await_rows(out_sums, peers - 1, back_send_sem.at[0])
        await_rows(chi_in, blocks - 1, chi_send_sem.at[0])


def step(bricks, blocks, remote, parameters, sersic, psf_width, point_flag, owner_brick, cell_index, exposure, inv_noise):
    sources, cells = parameters.shape[1], exposure.shape[0]
    vmem = pl.BlockSpec(memory_space=pltpu.VMEM)
    dma = pltpu.SemaphoreType.DMA
    params = dict(vmem_limit_bytes=60000 * 1024)
    if remote:
        params.update(collective_id=0, has_side_effects=True)
    delta = pl.pallas_call(
        functools.partial(kernel, blocks, blocks * cells * PIXELS, remote),
        out_shape=jax.ShapeDtypeStruct((4, sources), F32),
        in_specs=[pl.BlockSpec(memory_space=pl.ANY)] * 8,
        out_specs=vmem,
        scratch_shapes=[
            pltpu.VMEM((4, sources), F32),
            pltpu.VMEM((1, sources), F32),
            pltpu.VMEM((1, sources), F32),
            pltpu.VMEM((1, sources), jnp.int32),
            pltpu.VMEM((1, sources), jnp.int32),
            pltpu.VMEM((1, sources), jnp.int32),
            pltpu.VMEM((cells, PIXELS), F32),
            pltpu.VMEM((1, cells), F32),
            pltpu.VMEM((VALS, LANES), F32),
            pltpu.VMEM((bricks, LANES), F32),
            pltpu.VMEM((1, LANES), F32),
            pltpu.VMEM((2, VALS, LANES), F32),
            pltpu.VMEM((16, LANES), F32),
            pltpu.VMEM((TILE, LANES), F32),
            pltpu.VMEM((2 * TILE, 8, LANES), F32),
            pltpu.VMEM((3, 2, HALF, HALF, 8, LANES), F32),
            pltpu.VMEM((2, HALF, 2, 8, LANES), F32),
            pltpu.VMEM((2, 2, 8, 8, LANES), F32),
            pltpu.VMEM((3, 2, TILE, LANES), F32),
            pltpu.VMEM((2, LINES, LANES), F32),
            pltpu.VMEM((2, LINES, LANES), F32),
            pltpu.VMEM((2, LINES, LANES), F32),
            pltpu.VMEM((4, LINES, LANES), F32),
            pltpu.VMEM((4, LINES, LANES), F32),
            pltpu.VMEM((PIXELS, 2 * cells), F32),
            pltpu.VMEM((PIXELS, 2 * cells), BF16),
            pltpu.VMEM((bricks, 1, LANES), F32),
            pltpu.VMEM((bricks, 1, LANES), F32),
            pltpu.VMEM((bricks, 1, LANES), F32),
            pltpu.VMEM((bricks, 1, LANES), F32),
            pltpu.VMEM((1, 1, LANES), F32),
            pltpu.VMEM((blocks, 1, LANES), F32),
            dma((8,)),
            *[dma((1,))] * 7,
        ],
        compiler_params=pltpu.CompilerParams(**params),
    )(
        parameters,
        sersic.reshape(1, sources),
        psf_width.reshape(1, sources),
        point_flag.reshape(1, sources),
        owner_brick.reshape(1, sources),
        cell_index.reshape(1, sources),
        exposure,
        inv_noise.reshape(1, cells),
    )
    return parameters + delta


def solution(mesh):
    bricks, blocks = mesh.shape["brick"], mesh.shape["blk"]
    both = ("brick", "blk")
    in_specs = (P(None, both), P(both), P(both), P(both), P(both, None), P(both), P(both, None), P(both))
    return jax.shard_map(
        functools.partial(step, bricks, blocks, True),
        mesh=mesh, in_specs=in_specs, out_specs=P(None, both), check_vma=False,
    )
```

```python
import functools
import math

import jax
import jax.numpy as jnp
from jax import lax
from jax.experimental import pallas as pl
from jax.experimental.pallas import tpu as pltpu
from jax.sharding import PartitionSpec as P

TILE = 32
PIXELS = TILE * TILE
HALF = TILE // 2
PITCH = TILE + 1
LINES = 1096
SERIES = 96
CAP = 4
VALS = 32
BACK = 8
SIDE = 8
LANES = 128
ZERO_POINT = 30.0
BASE_DAMPING = 0.1
MISFIT_SCALE = 0.05
HIGHEST = lax.Precision.HIGHEST
MESH = pl.DeviceIdType.MESH
F32 = jnp.float32
BF16 = jnp.bfloat16

CX, CY, C1, C0, LN, INVN, ITV, NORM, SLOPE, CELL, WEIGHT = range(11)


def peer_offsets():
    return [(z, y) for z in sorted(range(SIDE), key=lambda step: (min(step, SIDE - step), step)) for y in range(SIDE)]


def dot(a, b, ca=1, cb=0):
    return lax.dot_general(
        a, b, (((ca,), (cb,)), ((), ())), precision=HIGHEST, preferred_element_type=F32
    )


def series(shape_value, cutoff):
    chain = SERIES // 8
    at = lax.broadcasted_iota(jnp.int32, (8, LANES), 0) * chain
    total = jnp.zeros((8, LANES), F32)
    product = jnp.ones((8, LANES), F32)
    for step in reversed(range(chain)):
        k = at + (step + 1)
        ratio = cutoff / (shape_value + k.astype(F32))
        live = k < SERIES
        total = jnp.where(live, ratio * (1.0 + total), 0.0)
        product = jnp.where(live, product * ratio, product)
    whole = total[7:8]
    last = product[7:8]
    for j in reversed(range(7)):
        whole = total[j : j + 1] + product[j : j + 1] * whole
        last = last * product[j : j + 1]
    return 1.0 + whole, last


def source_rows(values, sersic, psf_width, point, cell):
    flux, shift_x, shift_y, log_radius = (values[k : k + 1] for k in range(4))
    inverse_index = 1.0 / sersic
    bfactor = 2.0 * sersic - 1.0 / 3.0 + 4.0 / (405.0 * sersic)
    cutoff = bfactor * jnp.exp((math.log(0.5 * TILE) - log_radius) * inverse_index)
    total, last = series(2.0 * sersic, cutoff)
    log_norm = math.log(math.pi * 0.25 * TILE * TILE) - cutoff + jnp.log(total)
    slope = 2.0 - (2.0 * sersic - cutoff * last) * inverse_index / total
    inv_two_var = 0.5 / (psf_width * psf_width)
    norm_psf = 1.0 / (math.sqrt(2.0 * math.pi) * psf_width)
    is_point = point == 1
    log_itv = jnp.log(inv_two_var)
    rows = [None] * VALS
    rows[CX] = shift_x
    rows[CY] = shift_y
    rows[C1] = jnp.where(is_point, 1.0, 0.5 * inverse_index)
    rows[C0] = jnp.where(is_point, log_itv, jnp.log(bfactor) - log_radius * inverse_index)
    rows[LN] = jnp.where(is_point, math.log(math.pi) - log_itv, log_norm) - jnp.log(ZERO_POINT * flux)
    rows[INVN] = jnp.where(is_point, 2.0, inverse_index)
    rows[ITV] = jnp.where(is_point, 1.0e4, inv_two_var)
    rows[NORM] = jnp.where(is_point, 1.0, norm_psf)
    rows[SLOPE] = slope
    rows[CELL] = (cell + 1).astype(F32)
    zero = jnp.zeros_like(flux)
    return jnp.concatenate([zero if row is None else row for row in rows], axis=0)


def split(x):
    high = x.astype(BF16)
    return high, (x - high.astype(F32)).astype(BF16)


def product(a, b, cb=0):
    return lax.dot_general(a, b, (((1,), (cb,)), ((), ())), preferred_element_type=F32)


def blur_coefficients(row, taps, spread, coef, at):
    apart = lax.broadcasted_iota(jnp.int32, (TILE, LANES), 0).astype(F32)
    taps[...] = jnp.exp(-(apart * apart) * row(ITV)) * (0.5 * row(NORM))
    for d in range(TILE):
        value = jnp.broadcast_to(taps[d : d + 1, :], (8, LANES))
        spread[TILE - 1 + d] = value
        spread[TILE - 1 - d] = value
    for q in range(HALF):
        near = spread[TILE - 1 - q : TILE - 1 - q + HALF]
        far = spread[q : q + HALF]
        coef[at, 0, q] = near + far
        coef[at, 1, q] = near - far


def blur_lines(load, store, coef, at, parts, even_acc):
    for q in range(HALF):
        low, high = load(q), load(TILE - 1 - q)
        parts[0, q] = low + high
        parts[1, q] = low - high
    for parity in range(2):
        for group in range(2):
            span = slice(group * 8, group * 8 + 8)
            acc = None
            for q in range(HALF):
                term = coef[at, parity, q, span][None] * parts[parity, q][:, None]
                acc = term if acc is None else acc + term
            if parity == 0:
                even_acc[group] = acc
            else:
                even = even_acc[group]
                for k in range(8):
                    store(group * 8 + k, even[:, k] + acc[:, k])
                    store(TILE - 1 - group * 8 - k, even[:, k] - acc[:, k])


def blur(first, count, at_of, src, mid, dst, coef, parts, even_acc):
    def along_major(step, carry):
        image, start = first + step // 2, (step % 2) * 16

        def load(q):
            return src[image, pl.ds(q * PITCH + start, 16), :].reshape(2, 8, LANES)

        def store(q, value):
            mid[image, pl.ds(q * PITCH + start, 16), :] = value.reshape(16, LANES)

        blur_lines(load, store, coef, at_of(image), parts, even_acc)
        return carry

    def along_minor(step, carry):
        image, start = first + step // 2, (step % 2) * 16

        def load(p):
            return mid[image, pl.ds(start * PITCH + p, 16, stride=PITCH), :].reshape(2, 8, LANES)

        def store(p, value):
            dst[image, pl.ds(p * PITCH + start, 16), :] = value.reshape(16, LANES)

        blur_lines(load, store, coef, at_of(image), parts, even_acc)
        return carry

    lax.fori_loop(0, 2 * count, along_major, 0)
    lax.fori_loop(0, 2 * count, along_minor, 0)


def offsets(row, dy_ref, at):
    t_p = lax.broadcasted_iota(jnp.int32, (TILE, LANES), 0).astype(F32) + (0.5 - 0.5 * TILE)
    dy = t_p - row(CY)
    dy_ref[at, 0] = dy
    dy_ref[at, 1] = dy * dy


def column(q, row):
    return q.astype(F32) + (0.5 - 0.5 * TILE) - row(CX)


def images(q, row, dy_ref, at):
    dx = column(q, row)
    radius_sq = dy_ref[at, 1] + dx * dx
    power = jnp.exp(row(C1) * jnp.log(radius_sq) + row(C0))
    image = jnp.exp(-power - row(LN))
    over = image * (power * row(INVN)) / radius_sq
    return dx, radius_sq, image, over


def damped_solve(curvature, gradient, damping):
    system = [[curvature[first][second] for second in range(4)] for first in range(4)]
    for first in range(4):
        system[first][first] = system[first][first] + damping * (1.0 + curvature[first][first])
    factor = [[None for second in range(4)] for first in range(4)]
    for column in range(4):
        pivot = system[column][column]
        for inner in range(column):
            pivot = pivot - factor[column][inner] * factor[column][inner]
        pivot = jnp.sqrt(pivot)
        factor[column][column] = pivot
        for lower_row in range(column + 1, 4):
            entry = system[lower_row][column]
            for inner in range(column):
                entry = entry - factor[lower_row][inner] * factor[column][inner]
            factor[lower_row][column] = entry / pivot
    forward = []
    for row_at in range(4):
        entry = gradient[row_at]
        for inner in range(row_at):
            entry = entry - factor[row_at][inner] * forward[inner]
        forward.append(entry / factor[row_at][row_at])
    solved = [None, None, None, None]
    for row_at in reversed(range(4)):
        entry = forward[row_at]
        for inner in range(row_at + 1, 4):
            entry = entry - factor[inner][row_at] * solved[inner]
        solved[row_at] = entry / factor[row_at][row_at]
    return solved


def kernel(
    blocks, pixel_total, remote,
    values_hbm, sersic_hbm, psf_hbm, flag_hbm, owner_hbm, cell_hbm, exposure_hbm, noise_hbm,
    out_ref,
    values_ref, sersic_ref, psf_ref, flag_ref, owner_ref, cell_ref, exposure_ref, noise_ref,
    rows_ref, hits_ref, rank_ref, slots_ref, gram_ref, taps, spread, coef, parts, even_acc, dy_ref,
    img_a, img_b, img_c, img_d, img_e, exposure_t, weighted_ref,
    out_rows, mid_rows, in_rows, out_sums, in_sums, chi_out, chi_in,
    input_sem, send_sem, mid_sem, pass_sem, near_sem, far_sem, back_send_sem, back_sem, chi_send_sem, chi_sem,
):
    inputs = [
        pltpu.make_async_copy(source, target, input_sem.at[k])
        for k, (source, target) in enumerate(
            (
                (values_hbm, values_ref),
                (sersic_hbm, sersic_ref),
                (psf_hbm, psf_ref),
                (flag_hbm, flag_ref),
                (owner_hbm, owner_ref),
                (cell_hbm, cell_ref),
                (exposure_hbm, exposure_ref),
                (noise_hbm, noise_ref),
            )
        )
    ]
    for copy in inputs:
        copy.start()
    offsets_of = peer_offsets()
    peers = len(offsets_of)
    near = peers // 2
    if remote:
        me = lax.axis_index("brick")
        lane = lax.axis_index("blk")
        barrier = pltpu.get_barrier_semaphore()
        my_z, my_y = me // SIDE, me % SIDE
        plus_z = [((my_z + k) % SIDE) * SIDE for k in range(SIDE)]
        plus_y = [(my_y + k) % SIDE for k in range(SIDE)]

        def ahead(j):
            return plus_z[offsets_of[j][0]] + plus_y[offsets_of[j][1]]

        def behind(j):
            return plus_z[-offsets_of[j][0] % SIDE] + plus_y[-offsets_of[j][1] % SIDE]

        def around(k):
            return jnp.where(lane + k >= blocks, lane + k - blocks, lane + k)

        for k in reversed(range(1, SIDE)):
            pl.semaphore_signal(barrier, inc=1, device_id={"brick": ahead(k)}, device_id_type=MESH)
            pl.semaphore_signal(barrier, inc=1, device_id={"brick": ahead(k * SIDE)}, device_id_type=MESH)
        for k in range(1, blocks):
            pl.semaphore_signal(barrier, inc=1, device_id={"blk": around(k)}, device_id_type=MESH)
    else:
        my_z, my_y = 0, 0
    for copy in inputs[:6]:
        copy.wait()

    rows = source_rows(values_ref[...], sersic_ref[...], psf_ref[...], flag_ref[...], cell_ref[...])
    rows_ref[...] = rows
    owner = owner_ref[...].astype(F32)
    owner_all = jnp.broadcast_to(owner, (LANES, LANES))
    earlier = lax.broadcasted_iota(jnp.int32, (LANES, LANES), 0) < lax.broadcasted_iota(jnp.int32, (LANES, LANES), 1)
    same = jnp.where((owner_all.T == owner_all) & earlier, 1.0, 0.0)
    rank = jnp.sum(same, axis=0, keepdims=True)
    rank_ref[...] = rank
    place = owner_ref[...]
    ahead_of_me = (((place >> 3) - my_z) & (SIDE - 1)) * SIDE + (((place & (SIDE - 1)) - my_y) & (SIDE - 1))
    for j, (z, y) in enumerate(offsets_of):
        hits_ref[j : j + 1, :] = jnp.where(ahead_of_me == z * SIDE + y, 1.0, 0.0)
    by_rank = jnp.concatenate([jnp.where(rank == float(r), rows, 0.0) for r in range(CAP)], axis=0)
    out_rows[:, :, 0, :] = dot(hits_ref[...], by_rank, 1, 1).reshape(SIDE, SIDE, LANES)

    def row(k):
        return rows_ref[k : k + 1, :]

    blur_coefficients(row, taps, spread, coef, 2)
    offsets(row, dy_ref, 2)

    def own_images(q, carry):
        dx, radius_sq, image, over = images(q, row, dy_ref, 2)
        at = pl.ds(q * PITCH, TILE)
        img_d[0, at, :] = image
        img_d[1, at, :] = over * dx
        img_d[2, at, :] = over * dy_ref[2, 0]
        img_d[3, at, :] = over * radius_sq - row(SLOPE) * image
        return carry

    lax.fori_loop(0, TILE, own_images, 0, unroll=4)

    def own_blur(first, count):
        blur(first, count, lambda image: 2, img_d, img_e, img_d, coef, parts, even_acc)

    if remote:
        pl.semaphore_wait(barrier, 2 * (SIDE - 1) + blocks - 1)

        def send(source, target, to, sent, landed):
            pltpu.make_async_remote_copy(
                src_ref=source, dst_ref=target, send_sem=sent, recv_sem=landed,
                device_id={"brick": to}, device_id_type=MESH,
            ).start()

        def await_rows(ref, count, sem):
            pltpu.make_async_copy(ref.at[0:count], ref.at[0:count], sem).wait()

        for k in range(1, SIDE):
            send(out_rows.at[:, k], mid_rows.at[:, k], ahead(k), send_sem.at[0], mid_sem.at[0])
    mid_rows[:, 0] = out_rows[:, 0]
    own_blur(0, 2)
    if remote:
        await_rows(mid_rows, SIDE - 1, mid_sem.at[0])
        for k in reversed(range(1, SIDE)):
            landed = (near_sem if k < SIDE // 2 else far_sem).at[0]
            send(mid_rows.at[k], in_rows.at[k], ahead(k * SIDE), pass_sem.at[0], landed)
        in_rows[0] = mid_rows[0]
    else:
        in_rows[...] = out_rows[...]

    own_blur(2, 1)
    for copy in inputs[6:]:
        copy.wait()
    cells = exposure_ref.shape[0]
    for k in range(PIXELS // LANES):
        part = exposure_ref[:, k * LANES : (k + 1) * LANES].T
        exposure_t[k * LANES : (k + 1) * LANES, :] = jnp.concatenate([part, part], axis=1)

    noise = noise_ref[...]
    weights = noise * noise
    cells_at = lax.broadcasted_iota(jnp.int32, (cells, LANES), 0).astype(F32) + 1.0
    picks = []

    def slot_rows(half):
        return lambda k: slots_ref[half, k : k + 1, :]

    def render(half):
        received = in_rows[half * SIDE // 2 : (half + 1) * SIDE // 2, :, 0, :].reshape(near, LANES)
        turned = [received] + [pltpu.roll(received, LANES - r * VALS, 1) for r in range(1, CAP)]
        slots_ref[half] = jnp.concatenate(turned, axis=0).T[:VALS]
        slot = slot_rows(half)
        blur_coefficients(slot, taps, spread, coef, half)
        offsets(slot, dy_ref, half)

        def slot_images(q, carry):
            dx, radius_sq, image, over = images(q, slot, dy_ref, half)
            at = pl.ds(q * PITCH, TILE)
            img_a[half, at, :] = image
            img_b[half, at, :] = over
            return carry

        lax.fori_loop(0, TILE, slot_images, 0, unroll=8)
        blur(half, 1, lambda image: half, img_a, img_e, img_c, coef, parts, even_acc)
        chosen = jnp.where(cells_at == slot(CELL), 1.0, 0.0)
        picks.append(chosen)
        slots_ref[half, WEIGHT : WEIGHT + 1, :] = dot(jnp.broadcast_to(weights, (8, cells)), chosen)[0:1]

    def lines_of(half, t):
        lines = [img_c[half, pl.ds((t * 8 + k) * PITCH, TILE), :] for k in range(8)]
        pick = jnp.concatenate([picks[half], picks[half]], axis=0).astype(BF16)
        tiles = jnp.concatenate(split(jnp.concatenate(lines, axis=0)), axis=1)
        return product(tiles, jnp.concatenate([pick, pick], axis=1), 1)

    def subtract_near(t, carry):
        at = pl.ds(pl.multiple_of(t * 8 * TILE, 8 * TILE), 8 * TILE)
        exposure_t[at, :] = exposure_t[at, :] - lines_of(0, t)
        return carry

    if remote:
        await_rows(in_rows, SIDE // 2 - 1, near_sem.at[0])
    render(0)
    lax.fori_loop(0, 4, subtract_near, 0, unroll=2)
    if remote:
        await_rows(in_rows, SIDE // 2, far_sem.at[0])
    render(1)
    weights_twice = jnp.concatenate([weights, weights], axis=1)
    is_high = lax.broadcasted_iota(jnp.int32, (1, 2 * cells), 1) < cells

    def residual(t, chi):
        at = pl.ds(pl.multiple_of(t * 8 * TILE, 8 * TILE), 8 * TILE)
        misfit = exposure_t[at, :] - lines_of(1, t)
        weighted = weights_twice * misfit
        high = weighted.astype(BF16).astype(F32)
        weighted_ref[at, :] = jnp.where(is_high, high, weighted - high).astype(BF16)
        return chi + jnp.sum((weighted * misfit).reshape(TILE, 8, 2 * cells), axis=0)

    chi = lax.fori_loop(0, 4, residual, jnp.zeros((8, 2 * cells), F32), unroll=2)
    chi = jnp.sum(chi, axis=0, keepdims=True)[:, :cells]
    chi = jnp.concatenate([chi, jnp.zeros((1, LANES - cells), F32)], axis=1)
    chi_out[0, :, :] = chi
    chi_in[0, :, :] = chi
    if remote:

        for k in range(1, blocks):
            pltpu.make_async_remote_copy(
                src_ref=chi_out.at[0], dst_ref=chi_in.at[k], send_sem=chi_send_sem.at[0], recv_sem=chi_sem.at[0],
                device_id={"blk": around(k)}, device_id_type=MESH,
            ).start()

    def answer(half):
        slot = slot_rows(half)
        pick = jnp.concatenate([picks[half], picks[half]], axis=0).astype(BF16)

        def gather(t, carry):
            at = pl.ds(pl.multiple_of(t * 8 * TILE, 8 * TILE), 8 * TILE)
            tiles = product(weighted_ref[at, :], pick)
            for k in range(8):
                img_c[half, pl.ds((t * 8 + k) * PITCH, TILE), :] = tiles[k * TILE : (k + 1) * TILE]
            return carry

        def project(q, sums):
            at = pl.ds(q * PITCH, TILE)
            dx = column(q, slot)
            adjoint = img_c[half, at, :]
            over = img_b[half, at, :] * adjoint
            plain = img_a[half, at, :] * adjoint
            moment = over * dy_ref[half, 0]
            second = moment * dy_ref[half, 0]
            plain, over, moment, second = (
                x[0:8] + x[8:16] + (x[16:24] + x[24:32]) for x in (plain, over, moment, second)
            )
            over = over * dx
            return sums[0] + plain, sums[1] + over, sums[2] + moment, sums[3] + (second + over * dx)

        lax.fori_loop(0, 4, gather, 0, unroll=2)
        blur(half, 1, lambda image: half, img_c, img_e, img_c, coef, parts, even_acc)
        sums = lax.fori_loop(0, TILE, project, tuple(jnp.zeros((8, LANES), F32) for _ in range(4)), unroll=4)
        sums = [jnp.sum(s, axis=0, keepdims=True) for s in sums]
        sums[3] = sums[3] - slot(SLOPE) * sums[0]
        back = jnp.concatenate(sums + [slots_ref[half, WEIGHT : WEIGHT + 1, :], jnp.zeros((LANES - 5, LANES), F32)], axis=0).T
        packed = back[0:near]
        for r in range(1, CAP):
            packed = packed + pltpu.roll(back[r * near : (r + 1) * near], r * BACK, 1)
        out_sums[half * near : (half + 1) * near, 0, :] = packed

    answer(1)
    if remote:
        for j in reversed(range(near, peers)):
            send(out_sums.at[j], in_sums.at[j], behind(j), back_send_sem.at[0], back_sem.at[0])
    answer(0)
    if remote:
        for j in reversed(range(1, near)):
            send(out_sums.at[j], in_sums.at[j], behind(j), back_send_sem.at[0], back_sem.at[0])
        in_sums[0] = out_sums[0]
    else:
        in_sums[...] = out_sums[...]

    own_blur(3, 1)
    pairs = [(i, j) for i in range(4) for j in range(i, 4)]

    def gram(p, sums):
        for t in range(TILE // 8):
            at = pl.ds(p * PITCH + t * 8, 8)
            own = [img_d[k, at, :] for k in range(4)]
            sums = tuple(s + own[i] * own[j] for s, (i, j) in zip(sums, pairs))
        return sums

    sums = lax.fori_loop(0, TILE, gram, tuple(jnp.zeros((8, LANES), F32) for _ in pairs))
    for k, s in enumerate(sums):
        gram_ref[k : k + 1, :] = jnp.sum(s, axis=0, keepdims=True)

    if remote:
        await_rows(chi_in, blocks - 1, chi_sem.at[0])
        await_rows(in_sums, peers - 1, back_sem.at[0])

    group = chi_in[0]
    if remote:
        for k in range(1, blocks):
            group = group + chi_in[k]
    group_chi = jnp.sum(group, axis=1, keepdims=True)
    damping = BASE_DAMPING + MISFIT_SCALE * group_chi / pixel_total
    by_rank = dot(in_sums[:, 0, :].T[: CAP * BACK], hits_ref[...])
    rank = rank_ref[...]
    mine = None
    for r in range(CAP):
        part = jnp.where(rank == float(r), by_rank[r * BACK : (r + 1) * BACK], 0.0)
        mine = part if mine is None else mine + part
    extended = jnp.where(flag_ref[...] == 1, 0.0, 1.0)
    per_flux = 1.0 / values_ref[0:1, :]
    scale = [per_flux, 1.0, 1.0, extended]
    weight = mine[4:5]
    gradient = [scale[k] * mine[k : k + 1] for k in range(4)]
    curvature = [[None] * 4 for _ in range(4)]
    for k, (i, j) in enumerate(pairs):
        entry = gram_ref[k : k + 1, :] * (scale[i] * scale[j]) * weight
        curvature[i][j] = entry
        curvature[j][i] = entry
    delta = damped_solve(curvature, gradient, jnp.broadcast_to(damping, (1, LANES)))
    out_ref[...] = jnp.concatenate(delta, axis=0)
    if remote:
        await_rows(out_rows, SIDE - 1, send_sem.at[0])
        await_rows(mid_rows, SIDE - 1, pass_sem.at[0])
        await_rows(out_sums, peers - 1, back_send_sem.at[0])
        await_rows(chi_in, blocks - 1, chi_send_sem.at[0])


def step(bricks, blocks, remote, parameters, sersic, psf_width, point_flag, owner_brick, cell_index, exposure, inv_noise):
    sources, cells = parameters.shape[1], exposure.shape[0]
    vmem = pl.BlockSpec(memory_space=pltpu.VMEM)
    dma = pltpu.SemaphoreType.DMA
    params = dict(vmem_limit_bytes=24 << 20)
    if remote:
        params.update(collective_id=0, has_side_effects=True)
    delta = pl.pallas_call(
        functools.partial(kernel, blocks, blocks * cells * PIXELS, remote),
        out_shape=jax.ShapeDtypeStruct((4, sources), F32),
        in_specs=[pl.BlockSpec(memory_space=pltpu.HBM)] * 8,
        out_specs=vmem,
        scratch_shapes=[
            pltpu.VMEM((4, sources), F32),
            pltpu.VMEM((1, sources), F32),
            pltpu.VMEM((1, sources), F32),
            pltpu.VMEM((1, sources), jnp.int32),
            pltpu.VMEM((1, sources), jnp.int32),
            pltpu.VMEM((1, sources), jnp.int32),
            pltpu.VMEM((cells, PIXELS), F32),
            pltpu.VMEM((1, cells), F32),
            pltpu.VMEM((VALS, LANES), F32),
            pltpu.VMEM((bricks, LANES), F32),
            pltpu.VMEM((1, LANES), F32),
            pltpu.VMEM((2, VALS, LANES), F32),
            pltpu.VMEM((16, LANES), F32),
            pltpu.VMEM((TILE, LANES), F32),
            pltpu.VMEM((2 * TILE, 8, LANES), F32),
            pltpu.VMEM((3, 2, HALF, HALF, 8, LANES), F32),
            pltpu.VMEM((2, HALF, 2, 8, LANES), F32),
            pltpu.VMEM((2, 2, 8, 8, LANES), F32),
            pltpu.VMEM((3, 2, TILE, LANES), F32),
            pltpu.VMEM((2, LINES, LANES), F32),
            pltpu.VMEM((2, LINES, LANES), F32),
            pltpu.VMEM((2, LINES, LANES), F32),
            pltpu.VMEM((4, LINES, LANES), F32),
            pltpu.VMEM((4, LINES, LANES), F32),
            pltpu.VMEM((PIXELS, 2 * cells), F32),
            pltpu.VMEM((PIXELS, 2 * cells), BF16),
            *[pltpu.VMEM((SIDE, SIDE, 1, LANES), F32)] * 3,
            *[pltpu.VMEM((bricks, 1, LANES), F32)] * 2,
            pltpu.VMEM((1, 1, LANES), F32),
            pltpu.VMEM((blocks, 1, LANES), F32),
            dma((8,)),
            *[dma((1,))] * 9,
        ],
        compiler_params=pltpu.CompilerParams(**params),
    )(*[pltpu.with_memory_space_constraint(x, pltpu.HBM) for x in (
        parameters,
        sersic.reshape(1, sources),
        psf_width.reshape(1, sources),
        point_flag.reshape(1, sources),
        owner_brick.reshape(1, sources),
        cell_index.reshape(1, sources),
        exposure,
        inv_noise.reshape(1, cells),
    )])
    return parameters + delta


def solution(mesh):
    bricks, blocks = mesh.shape["brick"], mesh.shape["blk"]
    both = ("brick", "blk")
    in_specs = (P(None, both), P(both), P(both), P(both), P(both, None), P(both), P(both, None), P(both))
    return jax.shard_map(
        functools.partial(step, bricks, blocks, True),
        mesh=mesh, in_specs=in_specs, out_specs=P(None, both), check_vma=False,
    )
```

```python
import functools
import math

import jax
import jax.numpy as jnp
from jax import lax
from jax.experimental import pallas as pl
from jax.experimental.pallas import tpu as pltpu
from jax.sharding import PartitionSpec as P

TILE = 32
PIXELS = TILE * TILE
HALF = TILE // 2
PITCH = TILE + 1
LINES = 1096
SERIES = 96
CAP = 4
VALS = 32
BACK = 8
SIDE = 8
LANES = 128
ZERO_POINT = 30.0
BASE_DAMPING = 0.1
MISFIT_SCALE = 0.05
HIGHEST = lax.Precision.HIGHEST
MESH = pl.DeviceIdType.MESH
F32 = jnp.float32
BF16 = jnp.bfloat16

CX, CY, C1, C0, LN, LNN, ITV, NORM, SLOPE, CELL, WEIGHT = range(11)


def peer_offsets():
    return [(z, y) for z in sorted(range(SIDE), key=lambda step: (min(step, SIDE - step), step)) for y in range(SIDE)]


def dot(a, b, ca=1, cb=0):
    return lax.dot_general(
        a, b, (((ca,), (cb,)), ((), ())), precision=HIGHEST, preferred_element_type=F32
    )


def series(shape_value, cutoff):
    chain = SERIES // 8
    at = lax.broadcasted_iota(jnp.int32, (8, LANES), 0) * chain
    total = jnp.zeros((8, LANES), F32)
    product = jnp.ones((8, LANES), F32)
    for step in reversed(range(chain)):
        k = at + (step + 1)
        ratio = cutoff / (shape_value + k.astype(F32))
        live = k < SERIES
        total = jnp.where(live, ratio * (1.0 + total), 0.0)
        product = jnp.where(live, product * ratio, product)
    whole = total[7:8]
    last = product[7:8]
    for j in reversed(range(7)):
        whole = total[j : j + 1] + product[j : j + 1] * whole
        last = last * product[j : j + 1]
    return 1.0 + whole, last


def source_rows(values, sersic, psf_width, point, cell):
    flux, shift_x, shift_y, log_radius = (values[k : k + 1] for k in range(4))
    inverse_index = 1.0 / sersic
    bfactor = 2.0 * sersic - 1.0 / 3.0 + 4.0 / (405.0 * sersic)
    cutoff = bfactor * jnp.exp((math.log(0.5 * TILE) - log_radius) * inverse_index)
    total, last = series(2.0 * sersic, cutoff)
    log_norm = math.log(math.pi * 0.25 * TILE * TILE) - cutoff + jnp.log(total)
    slope = 2.0 - (2.0 * sersic - cutoff * last) * inverse_index / total
    inv_two_var = 0.5 / (psf_width * psf_width)
    norm_psf = 1.0 / (math.sqrt(2.0 * math.pi) * psf_width)
    is_point = point == 1
    log_itv = jnp.log(inv_two_var)
    rows = [None] * VALS
    rows[CX] = shift_x
    rows[CY] = shift_y
    rows[C1] = jnp.where(is_point, 1.0, 0.5 * inverse_index)
    rows[C0] = jnp.where(is_point, log_itv, jnp.log(bfactor) - log_radius * inverse_index)
    rows[LN] = jnp.where(is_point, math.log(math.pi) - log_itv, log_norm) - jnp.log(ZERO_POINT * flux)
    rows[LNN] = jnp.where(is_point, -math.log(2.0), jnp.log(sersic))
    rows[ITV] = jnp.where(is_point, 1.0e4, inv_two_var)
    rows[NORM] = jnp.where(is_point, 1.0, norm_psf)
    rows[SLOPE] = slope
    rows[CELL] = (cell + 1).astype(F32)
    zero = jnp.zeros_like(flux)
    return jnp.concatenate([zero if row is None else row for row in rows], axis=0)


def split(x):
    high = x.astype(BF16)
    return high, (x - high.astype(F32)).astype(BF16)


def product(a, b, cb=0):
    return lax.dot_general(a, b, (((1,), (cb,)), ((), ())), preferred_element_type=F32)


def spread_taps(row, taps, spread):
    apart = lax.broadcasted_iota(jnp.int32, (TILE, LANES), 0).astype(F32)
    taps[...] = jnp.exp(-(apart * apart) * row(ITV)) * (0.5 * row(NORM))
    for d in range(TILE):
        value = jnp.broadcast_to(taps[d : d + 1, :], (8, LANES))
        spread[TILE - 1 + d] = value
        if d:
            spread[TILE - 1 - d] = value


def blur_column(q, spread, coef, at):
    near = spread[pl.ds(TILE - 1 - q, HALF)]
    far = spread[pl.ds(q, HALF)]
    coef[at, 0, q] = near + far
    coef[at, 1, q] = near - far


def blur_lines(load, store, coef, at, parts, even_acc):
    for q in range(HALF):
        low, high = load(q), load(TILE - 1 - q)
        parts[0, q] = low + high
        parts[1, q] = low - high
    for parity in range(2):
        for group in range(2):
            span = slice(group * 8, group * 8 + 8)
            acc = None
            for q in range(HALF):
                term = coef[at, parity, q, span][None] * parts[parity, q][:, None]
                acc = term if acc is None else acc + term
            if parity == 0:
                even_acc[group] = acc
            else:
                even = even_acc[group]
                for k in range(8):
                    store(group * 8 + k, even[:, k] + acc[:, k])
                    store(TILE - 1 - group * 8 - k, even[:, k] - acc[:, k])


def blur(first, count, at_of, src, mid, dst, coef, parts, even_acc):
    def along_major(step, carry):
        image, start = first + step // 2, (step % 2) * 16

        def load(q):
            return src[image, pl.ds(q * PITCH + start, 16), :].reshape(2, 8, LANES)

        def store(q, value):
            mid[image, pl.ds(q * PITCH + start, 16), :] = value.reshape(16, LANES)

        blur_lines(load, store, coef, at_of(image), parts, even_acc)
        return carry

    def along_minor(step, carry):
        image, start = first + step // 2, (step % 2) * 16

        def load(p):
            return mid[image, pl.ds(start * PITCH + p, 16, stride=PITCH), :].reshape(2, 8, LANES)

        def store(p, value):
            dst[image, pl.ds(p * PITCH + start, 16), :] = value.reshape(16, LANES)

        blur_lines(load, store, coef, at_of(image), parts, even_acc)
        return carry

    lax.fori_loop(0, 2 * count, along_major, 0)
    lax.fori_loop(0, 2 * count, along_minor, 0)


def offsets(row, dy_ref, at):
    t_p = lax.broadcasted_iota(jnp.int32, (TILE, LANES), 0).astype(F32) + (0.5 - 0.5 * TILE)
    dy = t_p - row(CY)
    dy_ref[at, 0] = dy
    dy_ref[at, 1] = dy * dy


def column(q, row):
    return q.astype(F32) + (0.5 - 0.5 * TILE) - row(CX)


def images(q, row, dy_ref, at):
    dx = column(q, row)
    radius_sq = dy_ref[at, 1] + dx * dx
    log_r2 = jnp.log(radius_sq)
    log_power = row(C1) * log_r2 + row(C0)
    log_image = -jnp.exp(log_power) - row(LN)
    over = jnp.exp(log_image + log_power - (log_r2 + row(LNN)))
    return dx, radius_sq, jnp.exp(log_image), over


def damped_solve(curvature, gradient, damping):
    system = [[curvature[first][second] for second in range(4)] for first in range(4)]
    for first in range(4):
        system[first][first] = system[first][first] + damping * (1.0 + curvature[first][first])
    factor = [[None for second in range(4)] for first in range(4)]
    for column in range(4):
        pivot = system[column][column]
        for inner in range(column):
            pivot = pivot - factor[column][inner] * factor[column][inner]
        pivot = jnp.sqrt(pivot)
        factor[column][column] = pivot
        for lower_row in range(column + 1, 4):
            entry = system[lower_row][column]
            for inner in range(column):
                entry = entry - factor[lower_row][inner] * factor[column][inner]
            factor[lower_row][column] = entry / pivot
    forward = []
    for row_at in range(4):
        entry = gradient[row_at]
        for inner in range(row_at):
            entry = entry - factor[row_at][inner] * forward[inner]
        forward.append(entry / factor[row_at][row_at])
    solved = [None, None, None, None]
    for row_at in reversed(range(4)):
        entry = forward[row_at]
        for inner in range(row_at + 1, 4):
            entry = entry - factor[inner][row_at] * solved[inner]
        solved[row_at] = entry / factor[row_at][row_at]
    return solved


def kernel(
    blocks, pixel_total, remote,
    values_hbm, sersic_hbm, psf_hbm, flag_hbm, owner_hbm, cell_hbm, exposure_hbm, noise_hbm,
    out_ref,
    values_ref, sersic_ref, psf_ref, flag_ref, owner_ref, cell_ref, exposure_ref, noise_ref,
    rows_ref, hits_ref, rank_ref, slots_ref, gram_ref, taps, spread, coef, parts, even_acc, dy_ref,
    img_a, img_b, img_c, img_d, img_e, exposure_t, weighted_ref,
    out_rows, mid_rows, in_rows, out_sums, in_sums, chi_out, chi_in,
    input_sem, send_sem, mid_sem, pass_sem, near_sem, far_sem, back_send_sem, back_sem, chi_send_sem, chi_sem,
):
    inputs = [
        pltpu.make_async_copy(source, target, input_sem.at[k])
        for k, (source, target) in enumerate(
            (
                (values_hbm, values_ref),
                (sersic_hbm, sersic_ref),
                (psf_hbm, psf_ref),
                (flag_hbm, flag_ref),
                (owner_hbm, owner_ref),
                (cell_hbm, cell_ref),
                (exposure_hbm, exposure_ref),
                (noise_hbm, noise_ref),
            )
        )
    ]
    for copy in inputs:
        copy.start()
    offsets_of = peer_offsets()
    peers = len(offsets_of)
    near = peers // 2
    if remote:
        me = lax.axis_index("brick")
        lane = lax.axis_index("blk")
        barrier = pltpu.get_barrier_semaphore()
        my_z, my_y = me // SIDE, me % SIDE
        plus_z = [((my_z + k) % SIDE) * SIDE for k in range(SIDE)]
        plus_y = [(my_y + k) % SIDE for k in range(SIDE)]

        def ahead(j):
            return plus_z[offsets_of[j][0]] + plus_y[offsets_of[j][1]]

        def behind(j):
            return plus_z[-offsets_of[j][0] % SIDE] + plus_y[-offsets_of[j][1] % SIDE]

        def around(k):
            return jnp.where(lane + k >= blocks, lane + k - blocks, lane + k)

        for k in reversed(range(1, SIDE)):
            pl.semaphore_signal(barrier, inc=1, device_id={"brick": ahead(k)}, device_id_type=MESH)
            pl.semaphore_signal(barrier, inc=1, device_id={"brick": ahead(k * SIDE)}, device_id_type=MESH)
        for k in range(1, blocks):
            pl.semaphore_signal(barrier, inc=1, device_id={"blk": around(k)}, device_id_type=MESH)
    else:
        my_z, my_y = 0, 0
    for copy in inputs[:6]:
        copy.wait()

    rows = source_rows(values_ref[...], sersic_ref[...], psf_ref[...], flag_ref[...], cell_ref[...])
    rows_ref[...] = rows
    owner = owner_ref[...].astype(F32)
    owner_all = jnp.broadcast_to(owner, (LANES, LANES))
    earlier = lax.broadcasted_iota(jnp.int32, (LANES, LANES), 0) < lax.broadcasted_iota(jnp.int32, (LANES, LANES), 1)
    same = jnp.where((owner_all.T == owner_all) & earlier, 1.0, 0.0)
    rank = jnp.sum(same, axis=0, keepdims=True)
    rank_ref[...] = rank
    place = owner_ref[...]
    ahead_of_me = (((place >> 3) - my_z) & (SIDE - 1)) * SIDE + (((place & (SIDE - 1)) - my_y) & (SIDE - 1))
    for j, (z, y) in enumerate(offsets_of):
        hits_ref[j : j + 1, :] = jnp.where(ahead_of_me == z * SIDE + y, 1.0, 0.0)
    by_rank = jnp.concatenate([jnp.where(rank == float(r), rows, 0.0) for r in range(CAP)], axis=0)
    out_rows[:, :, 0, :] = dot(hits_ref[...], by_rank, 1, 1).reshape(SIDE, SIDE, LANES)

    def row(k):
        return rows_ref[k : k + 1, :]

    spread_taps(row, taps, spread)
    offsets(row, dy_ref, 2)

    def own_images(step, carry):
        for k in range(8):
            q = step * 8 + k
            dx, radius_sq, image, over = images(q, row, dy_ref, 2)
            at = pl.ds(q * PITCH, TILE)
            img_d[0, at, :] = image
            img_d[1, at, :] = over * dx
            img_d[2, at, :] = over * dy_ref[2, 0]
            img_d[3, at, :] = over * radius_sq - row(SLOPE) * image
        for k in range(4):
            blur_column(step * 4 + k, spread, coef, 2)
        return carry

    lax.fori_loop(0, TILE // 8, own_images, 0)

    def own_blur(first, count):
        blur(first, count, lambda image: 2, img_d, img_e, img_d, coef, parts, even_acc)

    if remote:
        pl.semaphore_wait(barrier, 2 * (SIDE - 1) + blocks - 1)

        def send(source, target, to, sent, landed):
            pltpu.make_async_remote_copy(
                src_ref=source, dst_ref=target, send_sem=sent, recv_sem=landed,
                device_id={"brick": to}, device_id_type=MESH,
            ).start()

        def await_rows(ref, count, sem):
            pltpu.make_async_copy(ref.at[0:count], ref.at[0:count], sem).wait()

        for k in range(1, SIDE):
            send(out_rows.at[:, k], mid_rows.at[:, k], ahead(k), send_sem.at[0], mid_sem.at[0])
    mid_rows[:, 0] = out_rows[:, 0]
    own_blur(0, 2)
    if remote:
        await_rows(mid_rows, SIDE - 1, mid_sem.at[0])
        for k in reversed(range(1, SIDE)):
            landed = (near_sem if k < SIDE // 2 else far_sem).at[0]
            send(mid_rows.at[k], in_rows.at[k], ahead(k * SIDE), pass_sem.at[0], landed)
        in_rows[0] = mid_rows[0]
    else:
        in_rows[...] = out_rows[...]

    own_blur(2, 1)
    for copy in inputs[6:]:
        copy.wait()
    cells = exposure_ref.shape[0]
    for k in range(PIXELS // LANES):
        part = exposure_ref[:, k * LANES : (k + 1) * LANES].T
        exposure_t[k * LANES : (k + 1) * LANES, :] = jnp.concatenate([part, part], axis=1)

    noise = noise_ref[...]
    weights = noise * noise
    cells_at = lax.broadcasted_iota(jnp.int32, (cells, LANES), 0).astype(F32) + 1.0
    picks = []

    def slot_rows(half):
        return lambda k: slots_ref[half, k : k + 1, :]

    def render(half):
        received = in_rows[half * SIDE // 2 : (half + 1) * SIDE // 2, :, 0, :].reshape(near, LANES)
        turned = [received] + [pltpu.roll(received, LANES - r * VALS, 1) for r in range(1, CAP)]
        slots_ref[half] = jnp.concatenate(turned, axis=0).T[:VALS]
        slot = slot_rows(half)
        spread_taps(slot, taps, spread)
        offsets(slot, dy_ref, half)

        def slot_images(step, carry):
            for k in range(8):
                q = step * 8 + k
                dx, radius_sq, image, over = images(q, slot, dy_ref, half)
                at = pl.ds(q * PITCH, TILE)
                img_a[half, at, :] = image
                img_b[half, at, :] = over
            for k in range(4):
                blur_column(step * 4 + k, spread, coef, half)
            return carry

        lax.fori_loop(0, TILE // 8, slot_images, 0)
        blur(half, 1, lambda image: half, img_a, img_e, img_c, coef, parts, even_acc)
        chosen = jnp.where(cells_at == slot(CELL), 1.0, 0.0)
        picks.append(chosen)
        slots_ref[half, WEIGHT : WEIGHT + 1, :] = dot(jnp.broadcast_to(weights, (8, cells)), chosen)[0:1]

    def lines_of(half, t):
        lines = [img_c[half, pl.ds((t * 8 + k) * PITCH, TILE), :] for k in range(8)]
        pick = jnp.concatenate([picks[half], picks[half]], axis=0).astype(BF16)
        tiles = jnp.concatenate(split(jnp.concatenate(lines, axis=0)), axis=1)
        return product(tiles, jnp.concatenate([pick, pick], axis=1), 1)

    def subtract_near(t, carry):
        at = pl.ds(pl.multiple_of(t * 8 * TILE, 8 * TILE), 8 * TILE)
        exposure_t[at, :] = exposure_t[at, :] - lines_of(0, t)
        return carry

    if remote:
        await_rows(in_rows, SIDE // 2 - 1, near_sem.at[0])
    render(0)
    lax.fori_loop(0, 4, subtract_near, 0, unroll=2)
    if remote:
        await_rows(in_rows, SIDE // 2, far_sem.at[0])
    render(1)
    weights_twice = jnp.concatenate([weights, weights], axis=1)
    is_high = lax.broadcasted_iota(jnp.int32, (1, 2 * cells), 1) < cells

    def residual(t, chi):
        at = pl.ds(pl.multiple_of(t * 8 * TILE, 8 * TILE), 8 * TILE)
        misfit = exposure_t[at, :] - lines_of(1, t)
        weighted = weights_twice * misfit
        high = weighted.astype(BF16).astype(F32)
        weighted_ref[at, :] = jnp.where(is_high, high, weighted - high).astype(BF16)
        return chi + jnp.sum((weighted * misfit).reshape(TILE, 8, 2 * cells), axis=0)

    chi = lax.fori_loop(0, 4, residual, jnp.zeros((8, 2 * cells), F32), unroll=2)
    chi = jnp.sum(chi, axis=0, keepdims=True)[:, :cells]
    chi = jnp.concatenate([chi, jnp.zeros((1, LANES - cells), F32)], axis=1)
    chi_out[0, :, :] = chi
    chi_in[0, :, :] = chi
    if remote:

        for k in range(1, blocks):
            pltpu.make_async_remote_copy(
                src_ref=chi_out.at[0], dst_ref=chi_in.at[k], send_sem=chi_send_sem.at[0], recv_sem=chi_sem.at[0],
                device_id={"blk": around(k)}, device_id_type=MESH,
            ).start()

    def answer(half):
        slot = slot_rows(half)
        pick = jnp.concatenate([picks[half], picks[half]], axis=0).astype(BF16)

        def gather(t, carry):
            at = pl.ds(pl.multiple_of(t * 8 * TILE, 8 * TILE), 8 * TILE)
            tiles = product(weighted_ref[at, :], pick)
            for k in range(8):
                img_c[half, pl.ds((t * 8 + k) * PITCH, TILE), :] = tiles[k * TILE : (k + 1) * TILE]
            return carry

        def project(q, sums):
            at = pl.ds(q * PITCH, TILE)
            dx = column(q, slot)
            adjoint = img_c[half, at, :]
            over = img_b[half, at, :] * adjoint
            plain = img_a[half, at, :] * adjoint
            moment = over * dy_ref[half, 0]
            second = moment * dy_ref[half, 0]
            plain, over, moment, second = (
                x[0:8] + x[8:16] + (x[16:24] + x[24:32]) for x in (plain, over, moment, second)
            )
            over = over * dx
            return sums[0] + plain, sums[1] + over, sums[2] + moment, sums[3] + (second + over * dx)

        lax.fori_loop(0, 4, gather, 0, unroll=2)
        blur(half, 1, lambda image: half, img_c, img_e, img_c, coef, parts, even_acc)
        sums = lax.fori_loop(0, TILE, project, tuple(jnp.zeros((8, LANES), F32) for _ in range(4)), unroll=4)
        sums = [jnp.sum(s, axis=0, keepdims=True) for s in sums]
        sums[3] = sums[3] - slot(SLOPE) * sums[0]
        back = jnp.concatenate(sums + [slots_ref[half, WEIGHT : WEIGHT + 1, :], jnp.zeros((LANES - 5, LANES), F32)], axis=0).T
        packed = back[0:near]
        for r in range(1, CAP):
            packed = packed + pltpu.roll(back[r * near : (r + 1) * near], r * BACK, 1)
        out_sums[half * near : (half + 1) * near, 0, :] = packed

    answer(1)
    if remote:
        for j in reversed(range(near, peers)):
            send(out_sums.at[j], in_sums.at[j], behind(j), back_send_sem.at[0], back_sem.at[0])
    answer(0)
    if remote:
        for j in reversed(range(1, near)):
            send(out_sums.at[j], in_sums.at[j], behind(j), back_send_sem.at[0], back_sem.at[0])
        in_sums[0] = out_sums[0]
    else:
        in_sums[...] = out_sums[...]

    own_blur(3, 1)
    pairs = [(i, j) for i in range(4) for j in range(i, 4)]

    def gram(p, sums):
        for t in range(TILE // 8):
            at = pl.ds(p * PITCH + t * 8, 8)
            own = [img_d[k, at, :] for k in range(4)]
            sums = tuple(s + own[i] * own[j] for s, (i, j) in zip(sums, pairs))
        return sums

    sums = lax.fori_loop(0, TILE, gram, tuple(jnp.zeros((8, LANES), F32) for _ in pairs))
    for k, s in enumerate(sums):
        gram_ref[k : k + 1, :] = jnp.sum(s, axis=0, keepdims=True)

    if remote:
        await_rows(chi_in, blocks - 1, chi_sem.at[0])
        await_rows(in_sums, peers - 1, back_sem.at[0])

    group = chi_in[0]
    if remote:
        for k in range(1, blocks):
            group = group + chi_in[k]
    group_chi = jnp.sum(group, axis=1, keepdims=True)
    damping = BASE_DAMPING + MISFIT_SCALE * group_chi / pixel_total
    by_rank = dot(in_sums[:, 0, :].T[: CAP * BACK], hits_ref[...])
    rank = rank_ref[...]
    mine = None
    for r in range(CAP):
        part = jnp.where(rank == float(r), by_rank[r * BACK : (r + 1) * BACK], 0.0)
        mine = part if mine is None else mine + part
    extended = jnp.where(flag_ref[...] == 1, 0.0, 1.0)
    per_flux = 1.0 / values_ref[0:1, :]
    scale = [per_flux, 1.0, 1.0, extended]
    weight = mine[4:5]
    gradient = [scale[k] * mine[k : k + 1] for k in range(4)]
    curvature = [[None] * 4 for _ in range(4)]
    for k, (i, j) in enumerate(pairs):
        entry = gram_ref[k : k + 1, :] * (scale[i] * scale[j]) * weight
        curvature[i][j] = entry
        curvature[j][i] = entry
    delta = damped_solve(curvature, gradient, jnp.broadcast_to(damping, (1, LANES)))
    out_ref[...] = jnp.concatenate(delta, axis=0)
    if remote:
        await_rows(out_rows, SIDE - 1, send_sem.at[0])
        await_rows(mid_rows, SIDE - 1, pass_sem.at[0])
        await_rows(out_sums, peers - 1, back_send_sem.at[0])
        await_rows(chi_in, blocks - 1, chi_send_sem.at[0])


def step(bricks, blocks, remote, parameters, sersic, psf_width, point_flag, owner_brick, cell_index, exposure, inv_noise):
    sources, cells = parameters.shape[1], exposure.shape[0]
    vmem = pl.BlockSpec(memory_space=pltpu.VMEM)
    dma = pltpu.SemaphoreType.DMA
    params = dict(vmem_limit_bytes=24 << 20)
    if remote:
        params.update(collective_id=0, has_side_effects=True)
    delta = pl.pallas_call(
        functools.partial(kernel, blocks, blocks * cells * PIXELS, remote),
        out_shape=jax.ShapeDtypeStruct((4, sources), F32),
        in_specs=[pl.BlockSpec(memory_space=pltpu.HBM)] * 8,
        out_specs=vmem,
        scratch_shapes=[
            pltpu.VMEM((4, sources), F32),
            pltpu.VMEM((1, sources), F32),
            pltpu.VMEM((1, sources), F32),
            pltpu.VMEM((1, sources), jnp.int32),
            pltpu.VMEM((1, sources), jnp.int32),
            pltpu.VMEM((1, sources), jnp.int32),
            pltpu.VMEM((cells, PIXELS), F32),
            pltpu.VMEM((1, cells), F32),
            pltpu.VMEM((VALS, LANES), F32),
            pltpu.VMEM((bricks, LANES), F32),
            pltpu.VMEM((1, LANES), F32),
            pltpu.VMEM((2, VALS, LANES), F32),
            pltpu.VMEM((16, LANES), F32),
            pltpu.VMEM((TILE, LANES), F32),
            pltpu.VMEM((2 * TILE, 8, LANES), F32),
            pltpu.VMEM((3, 2, HALF, HALF, 8, LANES), F32),
            pltpu.VMEM((2, HALF, 2, 8, LANES), F32),
            pltpu.VMEM((2, 2, 8, 8, LANES), F32),
            pltpu.VMEM((3, 2, TILE, LANES), F32),
            pltpu.VMEM((2, LINES, LANES), F32),
            pltpu.VMEM((2, LINES, LANES), F32),
            pltpu.VMEM((2, LINES, LANES), F32),
            pltpu.VMEM((4, LINES, LANES), F32),
            pltpu.VMEM((4, LINES, LANES), F32),
            pltpu.VMEM((PIXELS, 2 * cells), F32),
            pltpu.VMEM((PIXELS, 2 * cells), BF16),
            *[pltpu.VMEM((SIDE, SIDE, 1, LANES), F32)] * 3,
            *[pltpu.VMEM((bricks, 1, LANES), F32)] * 2,
            pltpu.VMEM((1, 1, LANES), F32),
            pltpu.VMEM((blocks, 1, LANES), F32),
            dma((8,)),
            *[dma((1,))] * 9,
        ],
        compiler_params=pltpu.CompilerParams(**params),
    )(*[pltpu.with_memory_space_constraint(x, pltpu.HBM) for x in (
        parameters,
        sersic.reshape(1, sources),
        psf_width.reshape(1, sources),
        point_flag.reshape(1, sources),
        owner_brick.reshape(1, sources),
        cell_index.reshape(1, sources),
        exposure,
        inv_noise.reshape(1, cells),
    )])
    return parameters + delta


def solution(mesh):
    bricks, blocks = mesh.shape["brick"], mesh.shape["blk"]
    both = ("brick", "blk")
    in_specs = (P(None, both), P(both), P(both), P(both), P(both, None), P(both), P(both, None), P(both))
    return jax.shard_map(
        functools.partial(step, bricks, blocks, True),
        mesh=mesh, in_specs=in_specs, out_specs=P(None, both), check_vma=False,
    )
```

```python
import functools
import math

import jax
import jax.numpy as jnp
from jax import lax
from jax.experimental import pallas as pl
from jax.experimental.pallas import tpu as pltpu
from jax.sharding import PartitionSpec as P

TILE = 32
PIXELS = TILE * TILE
HALF = TILE // 2
PITCH = TILE + 1
LINES = 1096
SERIES = 96
CAP = 4
VALS = 32
BACK = 8
SIDE = 8
NEAR_Z = 2
LANES = 128
ZERO_POINT = 30.0
BASE_DAMPING = 0.1
MISFIT_SCALE = 0.05
HIGHEST = lax.Precision.HIGHEST
MESH = pl.DeviceIdType.MESH
F32 = jnp.float32
BF16 = jnp.bfloat16

CX, CY, C1, C0, LN, LNN, ITV, NORM, SLOPE, CELL, WEIGHT = range(11)


def hops(step):
    return min(step, SIDE - step)


def peer_offsets():
    return [(z, y) for z in sorted(range(SIDE), key=lambda step: (hops(step), step)) for y in range(SIDE)]


def slot_peers():
    def far(j):
        z, y = (hops(step) for step in peer_offsets()[j])
        return z + y + (SIDE if z > NEAR_Z else 0)

    ordered = sorted(range(SIDE * SIDE), key=lambda j: (far(j), j))
    half = len(ordered) // 2
    return ordered[:half], ordered[half:]


def dot(a, b, ca=1, cb=0):
    return lax.dot_general(
        a, b, (((ca,), (cb,)), ((), ())), precision=HIGHEST, preferred_element_type=F32
    )


def series(shape_value, cutoff):
    chain = SERIES // 8
    at = lax.broadcasted_iota(jnp.int32, (8, LANES), 0) * chain
    total = jnp.zeros((8, LANES), F32)
    product = jnp.ones((8, LANES), F32)
    for step in reversed(range(chain)):
        k = at + (step + 1)
        ratio = cutoff / (shape_value + k.astype(F32))
        live = k < SERIES
        total = jnp.where(live, ratio * (1.0 + total), 0.0)
        product = jnp.where(live, product * ratio, product)
    whole = total[7:8]
    last = product[7:8]
    for j in reversed(range(7)):
        whole = total[j : j + 1] + product[j : j + 1] * whole
        last = last * product[j : j + 1]
    return 1.0 + whole, last


def source_rows(values, sersic, psf_width, point, cell):
    flux, shift_x, shift_y, log_radius = (values[k : k + 1] for k in range(4))
    inverse_index = 1.0 / sersic
    bfactor = 2.0 * sersic - 1.0 / 3.0 + 4.0 / (405.0 * sersic)
    cutoff = bfactor * jnp.exp((math.log(0.5 * TILE) - log_radius) * inverse_index)
    total, last = series(2.0 * sersic, cutoff)
    log_norm = math.log(math.pi * 0.25 * TILE * TILE) - cutoff + jnp.log(total)
    slope = 2.0 - (2.0 * sersic - cutoff * last) * inverse_index / total
    inv_two_var = 0.5 / (psf_width * psf_width)
    norm_psf = 1.0 / (math.sqrt(2.0 * math.pi) * psf_width)
    is_point = point == 1
    log_itv = jnp.log(inv_two_var)
    rows = [None] * VALS
    rows[CX] = shift_x
    rows[CY] = shift_y
    rows[C1] = jnp.where(is_point, 1.0, 0.5 * inverse_index)
    rows[C0] = jnp.where(is_point, log_itv, jnp.log(bfactor) - log_radius * inverse_index)
    rows[LN] = jnp.where(is_point, math.log(math.pi) - log_itv, log_norm) - jnp.log(ZERO_POINT * flux)
    rows[LNN] = jnp.where(is_point, -math.log(2.0), jnp.log(sersic))
    rows[ITV] = jnp.where(is_point, 1.0e4, inv_two_var)
    rows[NORM] = jnp.where(is_point, 1.0, norm_psf)
    rows[SLOPE] = slope
    rows[CELL] = (cell + 1).astype(F32)
    zero = jnp.zeros_like(flux)
    return jnp.concatenate([zero if row is None else row for row in rows], axis=0)


def split(x):
    high = x.astype(BF16)
    return high, (x - high.astype(F32)).astype(BF16)


def product(a, b, cb=0):
    return lax.dot_general(a, b, (((1,), (cb,)), ((), ())), preferred_element_type=F32)


def spread_taps(row, taps, spread):
    apart = lax.broadcasted_iota(jnp.int32, (TILE, LANES), 0).astype(F32)
    taps[...] = jnp.exp(-(apart * apart) * row(ITV)) * (0.5 * row(NORM))
    for d in range(TILE):
        value = jnp.broadcast_to(taps[d : d + 1, :], (8, LANES))
        spread[TILE - 1 + d] = value
        if d:
            spread[TILE - 1 - d] = value


def blur_column(q, spread, coef, at):
    near = spread[pl.ds(TILE - 1 - q, HALF)]
    far = spread[pl.ds(q, HALF)]
    coef[at, 0, q] = near + far
    coef[at, 1, q] = near - far


def blur_lines(load, store, coef, at, parts, even_acc):
    for q in range(HALF):
        low, high = load(q), load(TILE - 1 - q)
        parts[0, q] = low + high
        parts[1, q] = low - high
    for parity in range(2):
        for group in range(2):
            span = slice(group * 8, group * 8 + 8)
            acc = None
            for q in range(HALF):
                term = coef[at, parity, q, span][None] * parts[parity, q][:, None]
                acc = term if acc is None else acc + term
            if parity == 0:
                even_acc[group] = acc
            else:
                even = even_acc[group]
                for k in range(8):
                    store(group * 8 + k, even[:, k] + acc[:, k])
                    store(TILE - 1 - group * 8 - k, even[:, k] - acc[:, k])


def blur(first, count, at_of, src, mid, dst, coef, parts, even_acc):
    def along_major(step, carry):
        image, start = first + step // 2, (step % 2) * 16

        def load(q):
            return src[image, pl.ds(q * PITCH + start, 16), :].reshape(2, 8, LANES)

        def store(q, value):
            mid[image, pl.ds(q * PITCH + start, 16), :] = value.reshape(16, LANES)

        blur_lines(load, store, coef, at_of(image), parts, even_acc)
        return carry

    def along_minor(step, carry):
        image, start = first + step // 2, (step % 2) * 16

        def load(p):
            return mid[image, pl.ds(start * PITCH + p, 16, stride=PITCH), :].reshape(2, 8, LANES)

        def store(p, value):
            dst[image, pl.ds(p * PITCH + start, 16), :] = value.reshape(16, LANES)

        blur_lines(load, store, coef, at_of(image), parts, even_acc)
        return carry

    lax.fori_loop(0, 2 * count, along_major, 0)
    lax.fori_loop(0, 2 * count, along_minor, 0)


def offsets(row, dy_ref, at):
    t_p = lax.broadcasted_iota(jnp.int32, (TILE, LANES), 0).astype(F32) + (0.5 - 0.5 * TILE)
    dy = t_p - row(CY)
    dy_ref[at, 0] = dy
    dy_ref[at, 1] = dy * dy


def column(q, row):
    return q.astype(F32) + (0.5 - 0.5 * TILE) - row(CX)


def images(q, row, dy_ref, at):
    dx = column(q, row)
    radius_sq = dy_ref[at, 1] + dx * dx
    log_r2 = jnp.log(radius_sq)
    log_power = row(C1) * log_r2 + row(C0)
    log_image = -jnp.exp(log_power) - row(LN)
    over = jnp.exp(log_image + log_power - (log_r2 + row(LNN)))
    return dx, radius_sq, jnp.exp(log_image), over


def damped_solve(curvature, gradient, damping):
    system = [[curvature[first][second] for second in range(4)] for first in range(4)]
    for first in range(4):
        system[first][first] = system[first][first] + damping * (1.0 + curvature[first][first])
    factor = [[None for second in range(4)] for first in range(4)]
    for column in range(4):
        pivot = system[column][column]
        for inner in range(column):
            pivot = pivot - factor[column][inner] * factor[column][inner]
        pivot = jnp.sqrt(pivot)
        factor[column][column] = pivot
        for lower_row in range(column + 1, 4):
            entry = system[lower_row][column]
            for inner in range(column):
                entry = entry - factor[lower_row][inner] * factor[column][inner]
            factor[lower_row][column] = entry / pivot
    forward = []
    for row_at in range(4):
        entry = gradient[row_at]
        for inner in range(row_at):
            entry = entry - factor[row_at][inner] * forward[inner]
        forward.append(entry / factor[row_at][row_at])
    solved = [None, None, None, None]
    for row_at in reversed(range(4)):
        entry = forward[row_at]
        for inner in range(row_at + 1, 4):
            entry = entry - factor[inner][row_at] * solved[inner]
        solved[row_at] = entry / factor[row_at][row_at]
    return solved


def kernel(
    blocks, pixel_total, remote,
    values_hbm, sersic_hbm, psf_hbm, flag_hbm, owner_hbm, cell_hbm, exposure_hbm, noise_hbm,
    out_ref,
    values_ref, sersic_ref, psf_ref, flag_ref, owner_ref, cell_ref, exposure_ref, noise_ref,
    rows_ref, hits_ref, rank_ref, slots_ref, gram_ref, taps, spread, coef, parts, even_acc, dy_ref,
    img_a, img_b, img_c, img_d, img_e, exposure_t, weighted_ref,
    out_rows, mid_rows, in_rows, out_sums, in_sums, chi_out, chi_in,
    input_sem, send_sem, mid_sem, pass_sem, near_sem, far_sem, back_send_sem, back_sem, chi_send_sem, chi_sem,
):
    offsets_of = peer_offsets()
    peers = len(offsets_of)
    near = peers // 2
    held = slot_peers()
    near_z = 2 * NEAR_Z + 1
    far_first = sorted(range(1, SIDE), key=lambda step: -hops(step))
    if remote:
        me = lax.axis_index("brick")
        lane = lax.axis_index("blk")
        barrier = pltpu.get_barrier_semaphore()
        my_z, my_y = me // SIDE, me % SIDE
        plus_z = [((my_z + k) % SIDE) * SIDE for k in range(SIDE)]
        plus_y = [(my_y + k) % SIDE for k in range(SIDE)]

        def ahead(j):
            return plus_z[offsets_of[j][0]] + plus_y[offsets_of[j][1]]

        def behind(j):
            return plus_z[-offsets_of[j][0] % SIDE] + plus_y[-offsets_of[j][1] % SIDE]

        def around(k):
            return jnp.where(lane + k >= blocks, lane + k - blocks, lane + k)

        for k in far_first:
            pl.semaphore_signal(barrier, inc=1, device_id={"brick": ahead(k)}, device_id_type=MESH)
        for k in reversed(range(1, SIDE)):
            pl.semaphore_signal(barrier, inc=1, device_id={"brick": ahead(k * SIDE)}, device_id_type=MESH)
        for k in range(1, blocks):
            pl.semaphore_signal(barrier, inc=1, device_id={"blk": around(k)}, device_id_type=MESH)
    else:
        my_z, my_y = 0, 0
    inputs = [
        pltpu.make_async_copy(source, target, input_sem.at[k])
        for k, (source, target) in enumerate(
            (
                (values_hbm, values_ref),
                (sersic_hbm, sersic_ref),
                (psf_hbm, psf_ref),
                (flag_hbm, flag_ref),
                (owner_hbm, owner_ref),
                (cell_hbm, cell_ref),
                (exposure_hbm, exposure_ref),
                (noise_hbm, noise_ref),
            )
        )
    ]
    for copy in inputs:
        copy.start()
    for copy in inputs[:6]:
        copy.wait()

    rows = source_rows(values_ref[...], sersic_ref[...], psf_ref[...], flag_ref[...], cell_ref[...])
    rows_ref[...] = rows
    owner = owner_ref[...].astype(F32)
    owner_all = jnp.broadcast_to(owner, (LANES, LANES))
    earlier = lax.broadcasted_iota(jnp.int32, (LANES, LANES), 0) < lax.broadcasted_iota(jnp.int32, (LANES, LANES), 1)
    same = jnp.where((owner_all.T == owner_all) & earlier, 1.0, 0.0)
    rank = jnp.sum(same, axis=0, keepdims=True)
    rank_ref[...] = rank
    place = owner_ref[...]
    ahead_of_me = (((place >> 3) - my_z) & (SIDE - 1)) * SIDE + (((place & (SIDE - 1)) - my_y) & (SIDE - 1))
    for j, (z, y) in enumerate(offsets_of):
        hits_ref[j : j + 1, :] = jnp.where(ahead_of_me == z * SIDE + y, 1.0, 0.0)
    by_rank = jnp.concatenate([jnp.where(rank == float(r), rows, 0.0) for r in range(CAP)], axis=0)
    out_rows[:, :, 0, :] = dot(hits_ref[...], by_rank, 1, 1).reshape(SIDE, SIDE, LANES)

    def row(k):
        return rows_ref[k : k + 1, :]

    spread_taps(row, taps, spread)
    offsets(row, dy_ref, 2)

    def own_images(step, carry):
        for k in range(8):
            q = step * 8 + k
            dx, radius_sq, image, over = images(q, row, dy_ref, 2)
            at = pl.ds(q * PITCH, TILE)
            img_d[0, at, :] = image
            img_d[1, at, :] = over * dx
            img_d[2, at, :] = over * dy_ref[2, 0]
            img_d[3, at, :] = over * radius_sq - row(SLOPE) * image
        for k in range(4):
            blur_column(step * 4 + k, spread, coef, 2)
        return carry

    lax.fori_loop(0, TILE // 8, own_images, 0)

    def own_blur(first, count):
        blur(first, count, lambda image: 2, img_d, img_e, img_d, coef, parts, even_acc)

    if remote:
        pl.semaphore_wait(barrier, 2 * (SIDE - 1) + blocks - 1)

        def send(source, target, to, sent, landed):
            pltpu.make_async_remote_copy(
                src_ref=source, dst_ref=target, send_sem=sent, recv_sem=landed,
                device_id={"brick": to}, device_id_type=MESH,
            ).start()

        def await_rows(ref, count, sem):
            pltpu.make_async_copy(ref.at[0:count], ref.at[0:count], sem).wait()

        for k in far_first:
            send(out_rows.at[:, k], mid_rows.at[:, k], ahead(k), send_sem.at[0], mid_sem.at[0])
    mid_rows[:, 0] = out_rows[:, 0]
    own_blur(0, 2)
    if remote:
        await_rows(mid_rows, SIDE - 1, mid_sem.at[0])
        for k in reversed(range(1, SIDE)):
            landed = (near_sem if k < near_z else far_sem).at[0]
            send(mid_rows.at[k], in_rows.at[k], ahead(k * SIDE), pass_sem.at[0], landed)
        in_rows[0] = mid_rows[0]
    else:
        in_rows[...] = out_rows[...]

    own_blur(2, 1)
    for copy in inputs[6:]:
        copy.wait()
    cells = exposure_ref.shape[0]
    for k in range(PIXELS // LANES):
        part = exposure_ref[:, k * LANES : (k + 1) * LANES].T
        exposure_t[k * LANES : (k + 1) * LANES, :] = jnp.concatenate([part, part], axis=1)

    noise = noise_ref[...]
    weights = noise * noise
    cells_at = lax.broadcasted_iota(jnp.int32, (cells, LANES), 0).astype(F32) + 1.0
    picks = []

    def slot_rows(half):
        return lambda k: slots_ref[half, k : k + 1, :]

    def render(half):
        received = jnp.concatenate([in_rows[j // SIDE, j % SIDE] for j in held[half]], axis=0)
        turned = [received] + [pltpu.roll(received, LANES - r * VALS, 1) for r in range(1, CAP)]
        slots_ref[half] = jnp.concatenate(turned, axis=0).T[:VALS]
        slot = slot_rows(half)
        spread_taps(slot, taps, spread)
        offsets(slot, dy_ref, half)

        def slot_images(step, carry):
            for k in range(8):
                q = step * 8 + k
                dx, radius_sq, image, over = images(q, slot, dy_ref, half)
                at = pl.ds(q * PITCH, TILE)
                img_a[half, at, :] = image
                img_b[half, at, :] = over
            for k in range(4):
                blur_column(step * 4 + k, spread, coef, half)
            return carry

        lax.fori_loop(0, TILE // 8, slot_images, 0)
        blur(half, 1, lambda image: half, img_a, img_e, img_c, coef, parts, even_acc)
        chosen = jnp.where(cells_at == slot(CELL), 1.0, 0.0)
        picks.append(chosen)
        slots_ref[half, WEIGHT : WEIGHT + 1, :] = dot(jnp.broadcast_to(weights, (8, cells)), chosen)[0:1]

    def lines_of(half, t):
        lines = [img_c[half, pl.ds((t * 8 + k) * PITCH, TILE), :] for k in range(8)]
        pick = jnp.concatenate([picks[half], picks[half]], axis=0).astype(BF16)
        tiles = jnp.concatenate(split(jnp.concatenate(lines, axis=0)), axis=1)
        return product(tiles, jnp.concatenate([pick, pick], axis=1), 1)

    def subtract_near(t, carry):
        at = pl.ds(pl.multiple_of(t * 8 * TILE, 8 * TILE), 8 * TILE)
        exposure_t[at, :] = exposure_t[at, :] - lines_of(0, t)
        return carry

    if remote:
        await_rows(in_rows, near_z - 1, near_sem.at[0])
    render(0)
    lax.fori_loop(0, 4, subtract_near, 0, unroll=2)
    if remote:
        await_rows(in_rows, SIDE - near_z, far_sem.at[0])
    render(1)
    weights_twice = jnp.concatenate([weights, weights], axis=1)
    is_high = lax.broadcasted_iota(jnp.int32, (1, 2 * cells), 1) < cells

    def residual(t, chi):
        at = pl.ds(pl.multiple_of(t * 8 * TILE, 8 * TILE), 8 * TILE)
        misfit = exposure_t[at, :] - lines_of(1, t)
        weighted = weights_twice * misfit
        high = weighted.astype(BF16).astype(F32)
        weighted_ref[at, :] = jnp.where(is_high, high, weighted - high).astype(BF16)
        return chi + jnp.sum((weighted * misfit).reshape(TILE, 8, 2 * cells), axis=0)

    chi = lax.fori_loop(0, 4, residual, jnp.zeros((8, 2 * cells), F32), unroll=2)
    chi = jnp.sum(chi, axis=0, keepdims=True)[:, :cells]
    chi = jnp.concatenate([chi, jnp.zeros((1, LANES - cells), F32)], axis=1)
    chi_out[0, :, :] = chi
    chi_in[0, :, :] = chi
    if remote:

        for k in range(1, blocks):
            pltpu.make_async_remote_copy(
                src_ref=chi_out.at[0], dst_ref=chi_in.at[k], send_sem=chi_send_sem.at[0], recv_sem=chi_sem.at[0],
                device_id={"blk": around(k)}, device_id_type=MESH,
            ).start()

    def answer(half):
        slot = slot_rows(half)
        pick = jnp.concatenate([picks[half], picks[half]], axis=0).astype(BF16)

        def gather(t, carry):
            at = pl.ds(pl.multiple_of(t * 8 * TILE, 8 * TILE), 8 * TILE)
            tiles = product(weighted_ref[at, :], pick)
            for k in range(8):
                img_c[half, pl.ds((t * 8 + k) * PITCH, TILE), :] = tiles[k * TILE : (k + 1) * TILE]
            return carry

        def project(q, sums):
            at = pl.ds(q * PITCH, TILE)
            dx = column(q, slot)
            adjoint = img_c[half, at, :]
            over = img_b[half, at, :] * adjoint
            plain = img_a[half, at, :] * adjoint
            moment = over * dy_ref[half, 0]
            second = moment * dy_ref[half, 0]
            plain, over, moment, second = (
                x[0:8] + x[8:16] + (x[16:24] + x[24:32]) for x in (plain, over, moment, second)
            )
            over = over * dx
            return sums[0] + plain, sums[1] + over, sums[2] + moment, sums[3] + (second + over * dx)

        lax.fori_loop(0, 4, gather, 0, unroll=2)
        blur(half, 1, lambda image: half, img_c, img_e, img_c, coef, parts, even_acc)
        sums = lax.fori_loop(0, TILE, project, tuple(jnp.zeros((8, LANES), F32) for _ in range(4)), unroll=4)
        sums = [jnp.sum(s, axis=0, keepdims=True) for s in sums]
        sums[3] = sums[3] - slot(SLOPE) * sums[0]
        back = jnp.concatenate(sums + [slots_ref[half, WEIGHT : WEIGHT + 1, :], jnp.zeros((LANES - 5, LANES), F32)], axis=0).T
        packed = back[0:near]
        for r in range(1, CAP):
            packed = packed + pltpu.roll(back[r * near : (r + 1) * near], r * BACK, 1)
        out_sums[half * near : (half + 1) * near, 0, :] = packed

    def send_answers(half):
        for k in reversed(range(near)):
            j = held[half][k]
            if j:
                send(out_sums.at[half * near + k], in_sums.at[j], behind(j), back_send_sem.at[0], back_sem.at[0])

    answer(1)
    if remote:
        send_answers(1)
    answer(0)
    if remote:
        send_answers(0)
        in_sums[0] = out_sums[0]
    else:
        for half in range(2):
            for k in range(near):
                in_sums[held[half][k]] = out_sums[half * near + k]

    own_blur(3, 1)
    pairs = [(i, j) for i in range(4) for j in range(i, 4)]

    def gram(p, sums):
        for t in range(TILE // 8):
            at = pl.ds(p * PITCH + t * 8, 8)
            own = [img_d[k, at, :] for k in range(4)]
            sums = tuple(s + own[i] * own[j] for s, (i, j) in zip(sums, pairs))
        return sums

    sums = lax.fori_loop(0, TILE, gram, tuple(jnp.zeros((8, LANES), F32) for _ in pairs))
    for k, s in enumerate(sums):
        gram_ref[k : k + 1, :] = jnp.sum(s, axis=0, keepdims=True)

    if remote:
        await_rows(chi_in, blocks - 1, chi_sem.at[0])
        await_rows(in_sums, peers - 1, back_sem.at[0])

    group = chi_in[0]
    if remote:
        for k in range(1, blocks):
            group = group + chi_in[k]
    group_chi = jnp.sum(group, axis=1, keepdims=True)
    damping = BASE_DAMPING + MISFIT_SCALE * group_chi / pixel_total
    by_rank = dot(in_sums[:, 0, :].T[: CAP * BACK], hits_ref[...])
    rank = rank_ref[...]
    mine = None
    for r in range(CAP):
        part = jnp.where(rank == float(r), by_rank[r * BACK : (r + 1) * BACK], 0.0)
        mine = part if mine is None else mine + part
    extended = jnp.where(flag_ref[...] == 1, 0.0, 1.0)
    per_flux = 1.0 / values_ref[0:1, :]
    scale = [per_flux, 1.0, 1.0, extended]
    weight = mine[4:5]
    gradient = [scale[k] * mine[k : k + 1] for k in range(4)]
    curvature = [[None] * 4 for _ in range(4)]
    for k, (i, j) in enumerate(pairs):
        entry = gram_ref[k : k + 1, :] * (scale[i] * scale[j]) * weight
        curvature[i][j] = entry
        curvature[j][i] = entry
    delta = damped_solve(curvature, gradient, jnp.broadcast_to(damping, (1, LANES)))
    out_ref[...] = jnp.concatenate(delta, axis=0)
    if remote:
        await_rows(out_rows, SIDE - 1, send_sem.at[0])
        await_rows(mid_rows, SIDE - 1, pass_sem.at[0])
        await_rows(out_sums, peers - 1, back_send_sem.at[0])
        await_rows(chi_in, blocks - 1, chi_send_sem.at[0])


def step(bricks, blocks, remote, parameters, sersic, psf_width, point_flag, owner_brick, cell_index, exposure, inv_noise):
    sources, cells = parameters.shape[1], exposure.shape[0]
    vmem = pl.BlockSpec(memory_space=pltpu.VMEM)
    dma = pltpu.SemaphoreType.DMA
    params = dict(vmem_limit_bytes=24 << 20)
    if remote:
        params.update(collective_id=0, has_side_effects=True)
    delta = pl.pallas_call(
        functools.partial(kernel, blocks, blocks * cells * PIXELS, remote),
        out_shape=jax.ShapeDtypeStruct((4, sources), F32),
        in_specs=[pl.BlockSpec(memory_space=pltpu.HBM)] * 8,
        out_specs=vmem,
        scratch_shapes=[
            pltpu.VMEM((4, sources), F32),
            pltpu.VMEM((1, sources), F32),
            pltpu.VMEM((1, sources), F32),
            pltpu.VMEM((1, sources), jnp.int32),
            pltpu.VMEM((1, sources), jnp.int32),
            pltpu.VMEM((1, sources), jnp.int32),
            pltpu.VMEM((cells, PIXELS), F32),
            pltpu.VMEM((1, cells), F32),
            pltpu.VMEM((VALS, LANES), F32),
            pltpu.VMEM((bricks, LANES), F32),
            pltpu.VMEM((1, LANES), F32),
            pltpu.VMEM((2, VALS, LANES), F32),
            pltpu.VMEM((16, LANES), F32),
            pltpu.VMEM((TILE, LANES), F32),
            pltpu.VMEM((2 * TILE, 8, LANES), F32),
            pltpu.VMEM((3, 2, HALF, HALF, 8, LANES), F32),
            pltpu.VMEM((2, HALF, 2, 8, LANES), F32),
            pltpu.VMEM((2, 2, 8, 8, LANES), F32),
            pltpu.VMEM((3, 2, TILE, LANES), F32),
            pltpu.VMEM((2, LINES, LANES), F32),
            pltpu.VMEM((2, LINES, LANES), F32),
            pltpu.VMEM((2, LINES, LANES), F32),
            pltpu.VMEM((4, LINES, LANES), F32),
            pltpu.VMEM((4, LINES, LANES), F32),
            pltpu.VMEM((PIXELS, 2 * cells), F32),
            pltpu.VMEM((PIXELS, 2 * cells), BF16),
            *[pltpu.VMEM((SIDE, SIDE, 1, LANES), F32)] * 3,
            *[pltpu.VMEM((bricks, 1, LANES), F32)] * 2,
            pltpu.VMEM((1, 1, LANES), F32),
            pltpu.VMEM((blocks, 1, LANES), F32),
            dma((8,)),
            *[dma((1,))] * 9,
        ],
        compiler_params=pltpu.CompilerParams(**params),
    )(*[pltpu.with_memory_space_constraint(x, pltpu.HBM) for x in (
        parameters,
        sersic.reshape(1, sources),
        psf_width.reshape(1, sources),
        point_flag.reshape(1, sources),
        owner_brick.reshape(1, sources),
        cell_index.reshape(1, sources),
        exposure,
        inv_noise.reshape(1, cells),
    )])
    return parameters + delta


def solution(mesh):
    bricks, blocks = mesh.shape["brick"], mesh.shape["blk"]
    both = ("brick", "blk")
    in_specs = (P(None, both), P(both), P(both), P(both), P(both, None), P(both), P(both, None), P(both))
    return jax.shard_map(
        functools.partial(step, bricks, blocks, True),
        mesh=mesh, in_specs=in_specs, out_specs=P(None, both), check_vma=False,
    )
```

```python
import functools
import math

import jax
import jax.numpy as jnp
from jax import lax
from jax.experimental import pallas as pl
from jax.experimental.pallas import tpu as pltpu
from jax.sharding import PartitionSpec as P

TILE = 32
PIXELS = TILE * TILE
HALF = TILE // 2
PITCH = TILE + 1
LINES = 1096
SERIES = 96
CAP = 4
VALS = 32
BACK = 8
SIDE = 8
NEAR_Z = 2
LANES = 128
ZERO_POINT = 30.0
BASE_DAMPING = 0.1
MISFIT_SCALE = 0.05
HIGHEST = lax.Precision.HIGHEST
MESH = pl.DeviceIdType.MESH
F32 = jnp.float32
BF16 = jnp.bfloat16

CX, CY, C1, C0, LN, LNN, ITV, NORM, SLOPE, CELL, WEIGHT = range(11)


def hops(step):
    return min(step, SIDE - step)


def peer_offsets():
    return [(z, y) for z in sorted(range(SIDE), key=lambda step: (hops(step), step)) for y in range(SIDE)]


def slot_peers():
    def far(j):
        z, y = (hops(step) for step in peer_offsets()[j])
        return z + y + (SIDE if z > NEAR_Z else 0)

    ordered = sorted(range(SIDE * SIDE), key=lambda j: (far(j), j))
    half = len(ordered) // 2
    return ordered[:half], ordered[half:]


def dot(a, b, ca=1, cb=0):
    return lax.dot_general(
        a, b, (((ca,), (cb,)), ((), ())), precision=HIGHEST, preferred_element_type=F32
    )


def series(shape_value, cutoff):
    chain = SERIES // 8
    at = lax.broadcasted_iota(jnp.int32, (8, LANES), 0) * chain
    total = jnp.zeros((8, LANES), F32)
    product = jnp.ones((8, LANES), F32)
    for step in reversed(range(chain)):
        k = at + (step + 1)
        ratio = cutoff / (shape_value + k.astype(F32))
        live = k < SERIES
        total = jnp.where(live, ratio * (1.0 + total), 0.0)
        product = jnp.where(live, product * ratio, product)
    whole = total[7:8]
    last = product[7:8]
    for j in reversed(range(7)):
        whole = total[j : j + 1] + product[j : j + 1] * whole
        last = last * product[j : j + 1]
    return 1.0 + whole, last


def source_rows(values, sersic, psf_width, point, cell):
    flux, shift_x, shift_y, log_radius = (values[k : k + 1] for k in range(4))
    inverse_index = 1.0 / sersic
    bfactor = 2.0 * sersic - 1.0 / 3.0 + 4.0 / (405.0 * sersic)
    cutoff = bfactor * jnp.exp((math.log(0.5 * TILE) - log_radius) * inverse_index)
    total, last = series(2.0 * sersic, cutoff)
    log_norm = math.log(math.pi * 0.25 * TILE * TILE) - cutoff + jnp.log(total)
    slope = 2.0 - (2.0 * sersic - cutoff * last) * inverse_index / total
    inv_two_var = 0.5 / (psf_width * psf_width)
    norm_psf = 1.0 / (math.sqrt(2.0 * math.pi) * psf_width)
    is_point = point == 1
    log_itv = jnp.log(inv_two_var)
    rows = [None] * VALS
    rows[CX] = shift_x
    rows[CY] = shift_y
    rows[C1] = jnp.where(is_point, 1.0, 0.5 * inverse_index)
    rows[C0] = jnp.where(is_point, log_itv, jnp.log(bfactor) - log_radius * inverse_index)
    rows[LN] = jnp.where(is_point, math.log(math.pi) - log_itv, log_norm) - jnp.log(ZERO_POINT * flux)
    rows[LNN] = jnp.where(is_point, -math.log(2.0), jnp.log(sersic))
    rows[ITV] = jnp.where(is_point, 1.0e4, inv_two_var)
    rows[NORM] = jnp.where(is_point, 1.0, norm_psf)
    rows[SLOPE] = slope
    rows[CELL] = (cell + 1).astype(F32)
    zero = jnp.zeros_like(flux)
    return jnp.concatenate([zero if row is None else row for row in rows], axis=0)


def split(x):
    high = x.astype(BF16)
    return high, (x - high.astype(F32)).astype(BF16)


def product(a, b, cb=0):
    return lax.dot_general(a, b, (((1,), (cb,)), ((), ())), preferred_element_type=F32)


def spread_taps(row, taps, spread):
    apart = lax.broadcasted_iota(jnp.int32, (TILE, LANES), 0).astype(F32)
    taps[...] = jnp.exp(-(apart * apart) * row(ITV)) * (0.5 * row(NORM))
    for d in range(TILE):
        value = jnp.broadcast_to(taps[d : d + 1, :], (8, LANES))
        spread[TILE - 1 + d] = value
        if d:
            spread[TILE - 1 - d] = value


def blur_column(q, spread, coef, at):
    near = spread[pl.ds(TILE - 1 - q, HALF)]
    far = spread[pl.ds(q, HALF)]
    coef[at, 0, q] = near + far
    coef[at, 1, q] = near - far


def blur_lines(load, store, coef, at, parts, even_acc):
    for q in range(HALF):
        low, high = load(q), load(TILE - 1 - q)
        parts[0, q] = low + high
        parts[1, q] = low - high
    for parity in range(2):
        for group in range(2):
            span = slice(group * 8, group * 8 + 8)
            acc = None
            for q in range(HALF):
                term = coef[at, parity, q, span][None] * parts[parity, q][:, None]
                acc = term if acc is None else acc + term
            if parity == 0:
                even_acc[group] = acc
            else:
                even = even_acc[group]
                for k in range(8):
                    store(group * 8 + k, even[:, k] + acc[:, k])
                    store(TILE - 1 - group * 8 - k, even[:, k] - acc[:, k])


def blur(first, count, at_of, src, mid, dst, coef, parts, even_acc):
    def along_major(k, carry):
        image = first + k
        for part in range(2):
            start = part * 16

            def load(q, start=start):
                return src[image, pl.ds(q * PITCH + start, 16), :].reshape(2, 8, LANES)

            def store(q, value, start=start):
                mid[image, pl.ds(q * PITCH + start, 16), :] = value.reshape(16, LANES)

            blur_lines(load, store, coef, at_of(image), parts.at[part], even_acc.at[part])
        return carry

    def along_minor(k, carry):
        image = first + k
        for part in range(2):
            start = part * 16

            def load(p, start=start):
                return mid[image, pl.ds(start * PITCH + p, 16, stride=PITCH), :].reshape(2, 8, LANES)

            def store(p, value, start=start):
                dst[image, pl.ds(p * PITCH + start, 16), :] = value.reshape(16, LANES)

            blur_lines(load, store, coef, at_of(image), parts.at[part], even_acc.at[part])
        return carry

    if count == 1:
        along_major(0, 0)
        along_minor(0, 0)
    else:
        lax.fori_loop(0, count, along_major, 0)
        lax.fori_loop(0, count, along_minor, 0)


def offsets(row, dy_ref, at):
    t_p = lax.broadcasted_iota(jnp.int32, (TILE, LANES), 0).astype(F32) + (0.5 - 0.5 * TILE)
    dy = t_p - row(CY)
    dy_ref[at, 0] = dy
    dy_ref[at, 1] = dy * dy


def column(q, row):
    return q.astype(F32) + (0.5 - 0.5 * TILE) - row(CX)


def images(q, row, dy_ref, at):
    dx = column(q, row)
    radius_sq = dy_ref[at, 1] + dx * dx
    log_r2 = jnp.log(radius_sq)
    log_power = row(C1) * log_r2 + row(C0)
    log_image = -jnp.exp(log_power) - row(LN)
    over = jnp.exp(log_image + log_power - (log_r2 + row(LNN)))
    return dx, radius_sq, jnp.exp(log_image), over


def damped_solve(curvature, gradient, damping):
    system = [[curvature[first][second] for second in range(4)] for first in range(4)]
    for first in range(4):
        system[first][first] = system[first][first] + damping * (1.0 + curvature[first][first])
    factor = [[None for second in range(4)] for first in range(4)]
    for column in range(4):
        pivot = system[column][column]
        for inner in range(column):
            pivot = pivot - factor[column][inner] * factor[column][inner]
        pivot = jnp.sqrt(pivot)
        factor[column][column] = pivot
        for lower_row in range(column + 1, 4):
            entry = system[lower_row][column]
            for inner in range(column):
                entry = entry - factor[lower_row][inner] * factor[column][inner]
            factor[lower_row][column] = entry / pivot
    forward = []
    for row_at in range(4):
        entry = gradient[row_at]
        for inner in range(row_at):
            entry = entry - factor[row_at][inner] * forward[inner]
        forward.append(entry / factor[row_at][row_at])
    solved = [None, None, None, None]
    for row_at in reversed(range(4)):
        entry = forward[row_at]
        for inner in range(row_at + 1, 4):
            entry = entry - factor[inner][row_at] * solved[inner]
        solved[row_at] = entry / factor[row_at][row_at]
    return solved


def kernel(
    blocks, pixel_total, remote,
    values_hbm, sersic_hbm, psf_hbm, flag_hbm, owner_hbm, cell_hbm, exposure_hbm, noise_hbm,
    out_ref,
    values_ref, sersic_ref, psf_ref, flag_ref, owner_ref, cell_ref, exposure_ref, noise_ref,
    rows_ref, hits_ref, rank_ref, slots_ref, gram_ref, taps, spread, coef, parts, even_acc, dy_ref,
    img_a, img_b, img_c, img_d, img_e, exposure_t, weighted_ref,
    out_rows, mid_rows, in_rows, out_sums, in_sums, chi_out, chi_in,
    input_sem, send_sem, mid_sem, pass_sem, near_sem, far_sem, back_send_sem, back_sem, chi_send_sem, chi_sem,
):
    offsets_of = peer_offsets()
    peers = len(offsets_of)
    near = peers // 2
    held = slot_peers()
    near_z = 2 * NEAR_Z + 1
    far_first = sorted(range(1, SIDE), key=lambda step: -hops(step))
    if remote:
        me = lax.axis_index("brick")
        lane = lax.axis_index("blk")
        barrier = pltpu.get_barrier_semaphore()
        my_z, my_y = me // SIDE, me % SIDE
        plus_z = [((my_z + k) % SIDE) * SIDE for k in range(SIDE)]
        plus_y = [(my_y + k) % SIDE for k in range(SIDE)]

        def ahead(j):
            return plus_z[offsets_of[j][0]] + plus_y[offsets_of[j][1]]

        def behind(j):
            return plus_z[-offsets_of[j][0] % SIDE] + plus_y[-offsets_of[j][1] % SIDE]

        def around(k):
            return jnp.where(lane + k >= blocks, lane + k - blocks, lane + k)

        for k in far_first:
            pl.semaphore_signal(barrier, inc=1, device_id={"brick": ahead(k)}, device_id_type=MESH)
        for k in reversed(range(1, SIDE)):
            pl.semaphore_signal(barrier, inc=1, device_id={"brick": ahead(k * SIDE)}, device_id_type=MESH)
        for k in range(1, blocks):
            pl.semaphore_signal(barrier, inc=1, device_id={"blk": around(k)}, device_id_type=MESH)
    else:
        my_z, my_y = 0, 0
    inputs = [
        pltpu.make_async_copy(source, target, input_sem.at[k])
        for k, (source, target) in enumerate(
            (
                (values_hbm, values_ref),
                (sersic_hbm, sersic_ref),
                (psf_hbm, psf_ref),
                (flag_hbm, flag_ref),
                (owner_hbm, owner_ref),
                (cell_hbm, cell_ref),
                (exposure_hbm, exposure_ref),
                (noise_hbm, noise_ref),
            )
        )
    ]
    for copy in inputs:
        copy.start()
    for copy in inputs[:6]:
        copy.wait()

    rows = source_rows(values_ref[...], sersic_ref[...], psf_ref[...], flag_ref[...], cell_ref[...])
    rows_ref[...] = rows
    owner = owner_ref[...].astype(F32)
    owner_all = jnp.broadcast_to(owner, (LANES, LANES))
    earlier = lax.broadcasted_iota(jnp.int32, (LANES, LANES), 0) < lax.broadcasted_iota(jnp.int32, (LANES, LANES), 1)
    same = jnp.where((owner_all.T == owner_all) & earlier, 1.0, 0.0)
    rank = jnp.sum(same, axis=0, keepdims=True)
    rank_ref[...] = rank
    place = owner_ref[...]
    ahead_of_me = (((place >> 3) - my_z) & (SIDE - 1)) * SIDE + (((place & (SIDE - 1)) - my_y) & (SIDE - 1))
    for j, (z, y) in enumerate(offsets_of):
        hits_ref[j : j + 1, :] = jnp.where(ahead_of_me == z * SIDE + y, 1.0, 0.0)
    by_rank = jnp.concatenate([jnp.where(rank == float(r), rows, 0.0) for r in range(CAP)], axis=0)
    out_rows[:, :, 0, :] = dot(hits_ref[...], by_rank, 1, 1).reshape(SIDE, SIDE, LANES)

    def row(k):
        return rows_ref[k : k + 1, :]

    spread_taps(row, taps, spread)
    offsets(row, dy_ref, 2)

    def own_images(step, carry):
        for k in range(8):
            q = step * 8 + k
            dx, radius_sq, image, over = images(q, row, dy_ref, 2)
            at = pl.ds(q * PITCH, TILE)
            img_d[0, at, :] = image
            img_d[1, at, :] = over * dx
            img_d[2, at, :] = over * dy_ref[2, 0]
            img_d[3, at, :] = over * radius_sq - row(SLOPE) * image
        for k in range(4):
            blur_column(step * 4 + k, spread, coef, 2)
        return carry

    lax.fori_loop(0, TILE // 8, own_images, 0)

    def own_blur(first, count):
        blur(first, count, lambda image: 2, img_d, img_e, img_d, coef, parts, even_acc)

    if remote:
        pl.semaphore_wait(barrier, 2 * (SIDE - 1) + blocks - 1)

        def send(source, target, to, sent, landed):
            pltpu.make_async_remote_copy(
                src_ref=source, dst_ref=target, send_sem=sent, recv_sem=landed,
                device_id={"brick": to}, device_id_type=MESH,
            ).start()

        def await_rows(ref, count, sem):
            pltpu.make_async_copy(ref.at[0:count], ref.at[0:count], sem).wait()

        for k in far_first:
            send(out_rows.at[:, k], mid_rows.at[:, k], ahead(k), send_sem.at[0], mid_sem.at[0])
    mid_rows[:, 0] = out_rows[:, 0]
    own_blur(0, 2)
    if remote:
        await_rows(mid_rows, SIDE - 1, mid_sem.at[0])
        for k in reversed(range(1, SIDE)):
            landed = (near_sem if k < near_z else far_sem).at[0]
            send(mid_rows.at[k], in_rows.at[k], ahead(k * SIDE), pass_sem.at[0], landed)
        in_rows[0] = mid_rows[0]
    else:
        in_rows[...] = out_rows[...]

    own_blur(2, 1)
    for copy in inputs[6:]:
        copy.wait()
    cells = exposure_ref.shape[0]
    for k in range(PIXELS // LANES):
        part = exposure_ref[:, k * LANES : (k + 1) * LANES].T
        exposure_t[k * LANES : (k + 1) * LANES, :] = jnp.concatenate([part, part], axis=1)

    noise = noise_ref[...]
    weights = noise * noise
    cells_at = lax.broadcasted_iota(jnp.int32, (cells, LANES), 0).astype(F32) + 1.0
    picks = []

    def slot_rows(half):
        return lambda k: slots_ref[half, k : k + 1, :]

    def render(half):
        received = jnp.concatenate([in_rows[j // SIDE, j % SIDE] for j in held[half]], axis=0)
        turned = [received] + [pltpu.roll(received, LANES - r * VALS, 1) for r in range(1, CAP)]
        slots_ref[half] = jnp.concatenate(turned, axis=0).T[:VALS]
        slot = slot_rows(half)
        spread_taps(slot, taps, spread)
        offsets(slot, dy_ref, half)

        def slot_images(step, carry):
            for k in range(8):
                q = step * 8 + k
                dx, radius_sq, image, over = images(q, slot, dy_ref, half)
                at = pl.ds(q * PITCH, TILE)
                img_a[half, at, :] = image
                img_b[half, at, :] = over
            for k in range(4):
                blur_column(step * 4 + k, spread, coef, half)
            return carry

        lax.fori_loop(0, TILE // 8, slot_images, 0)
        blur(half, 1, lambda image: half, img_a, img_e, img_c, coef, parts, even_acc)
        chosen = jnp.where(cells_at == slot(CELL), 1.0, 0.0)
        picks.append(chosen)
        slots_ref[half, WEIGHT : WEIGHT + 1, :] = dot(jnp.broadcast_to(weights, (8, cells)), chosen)[0:1]

    def lines_of(half, t):
        lines = [img_c[half, pl.ds((t * 8 + k) * PITCH, TILE), :] for k in range(8)]
        pick = jnp.concatenate([picks[half], picks[half]], axis=0).astype(BF16)
        tiles = jnp.concatenate(split(jnp.concatenate(lines, axis=0)), axis=1)
        return product(tiles, jnp.concatenate([pick, pick], axis=1), 1)

    def subtract_near(t, carry):
        at = pl.ds(pl.multiple_of(t * 8 * TILE, 8 * TILE), 8 * TILE)
        exposure_t[at, :] = exposure_t[at, :] - lines_of(0, t)
        return carry

    if remote:
        await_rows(in_rows, near_z - 1, near_sem.at[0])
    render(0)
    lax.fori_loop(0, 4, subtract_near, 0, unroll=4)
    if remote:
        await_rows(in_rows, SIDE - near_z, far_sem.at[0])
    render(1)
    weights_twice = jnp.concatenate([weights, weights], axis=1)
    is_high = lax.broadcasted_iota(jnp.int32, (1, 2 * cells), 1) < cells

    def residual(t, chi):
        at = pl.ds(pl.multiple_of(t * 8 * TILE, 8 * TILE), 8 * TILE)
        misfit = exposure_t[at, :] - lines_of(1, t)
        weighted = weights_twice * misfit
        high = weighted.astype(BF16).astype(F32)
        weighted_ref[at, :] = jnp.where(is_high, high, weighted - high).astype(BF16)
        return chi + jnp.sum((weighted * misfit).reshape(TILE, 8, 2 * cells), axis=0)

    chi = lax.fori_loop(0, 4, residual, jnp.zeros((8, 2 * cells), F32), unroll=4)
    chi = jnp.sum(chi, axis=0, keepdims=True)[:, :cells]
    chi = jnp.concatenate([chi, jnp.zeros((1, LANES - cells), F32)], axis=1)
    chi_out[0, :, :] = chi
    chi_in[0, :, :] = chi
    if remote:

        for k in range(1, blocks):
            pltpu.make_async_remote_copy(
                src_ref=chi_out.at[0], dst_ref=chi_in.at[k], send_sem=chi_send_sem.at[0], recv_sem=chi_sem.at[0],
                device_id={"blk": around(k)}, device_id_type=MESH,
            ).start()

    def answer(half):
        slot = slot_rows(half)
        pick = jnp.concatenate([picks[half], picks[half]], axis=0).astype(BF16)

        def gather(t, carry):
            at = pl.ds(pl.multiple_of(t * 8 * TILE, 8 * TILE), 8 * TILE)
            tiles = product(weighted_ref[at, :], pick)
            for k in range(8):
                img_c[half, pl.ds((t * 8 + k) * PITCH, TILE), :] = tiles[k * TILE : (k + 1) * TILE]
            return carry

        def project(q, sums):
            at = pl.ds(q * PITCH, TILE)
            dx = column(q, slot)
            adjoint = img_c[half, at, :]
            over = img_b[half, at, :] * adjoint
            plain = img_a[half, at, :] * adjoint
            moment = over * dy_ref[half, 0]
            second = moment * dy_ref[half, 0]
            plain, over, moment, second = (
                x[0:8] + x[8:16] + (x[16:24] + x[24:32]) for x in (plain, over, moment, second)
            )
            over = over * dx
            return sums[0] + plain, sums[1] + over, sums[2] + moment, sums[3] + (second + over * dx)

        lax.fori_loop(0, 4, gather, 0, unroll=4)
        blur(half, 1, lambda image: half, img_c, img_e, img_c, coef, parts, even_acc)
        sums = lax.fori_loop(0, TILE, project, tuple(jnp.zeros((8, LANES), F32) for _ in range(4)), unroll=8)
        sums = [jnp.sum(s, axis=0, keepdims=True) for s in sums]
        sums[3] = sums[3] - slot(SLOPE) * sums[0]
        back = jnp.concatenate(sums + [slots_ref[half, WEIGHT : WEIGHT + 1, :], jnp.zeros((LANES - 5, LANES), F32)], axis=0).T
        packed = back[0:near]
        for r in range(1, CAP):
            packed = packed + pltpu.roll(back[r * near : (r + 1) * near], r * BACK, 1)
        out_sums[half * near : (half + 1) * near, 0, :] = packed

    def send_answers(half):
        for k in reversed(range(near)):
            j = held[half][k]
            if j:
                send(out_sums.at[half * near + k], in_sums.at[j], behind(j), back_send_sem.at[0], back_sem.at[0])

    answer(1)
    if remote:
        send_answers(1)
    answer(0)
    if remote:
        send_answers(0)
        in_sums[0] = out_sums[0]
    else:
        for half in range(2):
            for k in range(near):
                in_sums[held[half][k]] = out_sums[half * near + k]

    own_blur(3, 1)
    pairs = [(i, j) for i in range(4) for j in range(i, 4)]

    def gram(p, sums):
        for t in range(TILE // 8):
            at = pl.ds(p * PITCH + t * 8, 8)
            own = [img_d[k, at, :] for k in range(4)]
            sums = tuple(s + own[i] * own[j] for s, (i, j) in zip(sums, pairs))
        return sums

    sums = lax.fori_loop(0, TILE, gram, tuple(jnp.zeros((8, LANES), F32) for _ in pairs))
    for k, s in enumerate(sums):
        gram_ref[k : k + 1, :] = jnp.sum(s, axis=0, keepdims=True)

    if remote:
        await_rows(chi_in, blocks - 1, chi_sem.at[0])
        await_rows(in_sums, peers - 1, back_sem.at[0])

    group = chi_in[0]
    if remote:
        for k in range(1, blocks):
            group = group + chi_in[k]
    group_chi = jnp.sum(group, axis=1, keepdims=True)
    damping = BASE_DAMPING + MISFIT_SCALE * group_chi / pixel_total
    by_rank = dot(in_sums[:, 0, :].T[: CAP * BACK], hits_ref[...])
    rank = rank_ref[...]
    mine = None
    for r in range(CAP):
        part = jnp.where(rank == float(r), by_rank[r * BACK : (r + 1) * BACK], 0.0)
        mine = part if mine is None else mine + part
    extended = jnp.where(flag_ref[...] == 1, 0.0, 1.0)
    per_flux = 1.0 / values_ref[0:1, :]
    scale = [per_flux, 1.0, 1.0, extended]
    weight = mine[4:5]
    gradient = [scale[k] * mine[k : k + 1] for k in range(4)]
    curvature = [[None] * 4 for _ in range(4)]
    for k, (i, j) in enumerate(pairs):
        entry = gram_ref[k : k + 1, :] * (scale[i] * scale[j]) * weight
        curvature[i][j] = entry
        curvature[j][i] = entry
    delta = damped_solve(curvature, gradient, jnp.broadcast_to(damping, (1, LANES)))
    out_ref[...] = jnp.concatenate(delta, axis=0)
    if remote:
        await_rows(out_rows, SIDE - 1, send_sem.at[0])
        await_rows(mid_rows, SIDE - 1, pass_sem.at[0])
        await_rows(out_sums, peers - 1, back_send_sem.at[0])
        await_rows(chi_in, blocks - 1, chi_send_sem.at[0])


def step(bricks, blocks, remote, parameters, sersic, psf_width, point_flag, owner_brick, cell_index, exposure, inv_noise):
    sources, cells = parameters.shape[1], exposure.shape[0]
    vmem = pl.BlockSpec(memory_space=pltpu.VMEM)
    dma = pltpu.SemaphoreType.DMA
    params = dict(vmem_limit_bytes=24 << 20)
    if remote:
        params.update(collective_id=0, has_side_effects=True)
    delta = pl.pallas_call(
        functools.partial(kernel, blocks, blocks * cells * PIXELS, remote),
        out_shape=jax.ShapeDtypeStruct((4, sources), F32),
        in_specs=[pl.BlockSpec(memory_space=pltpu.HBM)] * 8,
        out_specs=vmem,
        scratch_shapes=[
            pltpu.VMEM((4, sources), F32),
            pltpu.VMEM((1, sources), F32),
            pltpu.VMEM((1, sources), F32),
            pltpu.VMEM((1, sources), jnp.int32),
            pltpu.VMEM((1, sources), jnp.int32),
            pltpu.VMEM((1, sources), jnp.int32),
            pltpu.VMEM((cells, PIXELS), F32),
            pltpu.VMEM((1, cells), F32),
            pltpu.VMEM((VALS, LANES), F32),
            pltpu.VMEM((bricks, LANES), F32),
            pltpu.VMEM((1, LANES), F32),
            pltpu.VMEM((2, VALS, LANES), F32),
            pltpu.VMEM((16, LANES), F32),
            pltpu.VMEM((TILE, LANES), F32),
            pltpu.VMEM((2 * TILE, 8, LANES), F32),
            pltpu.VMEM((3, 2, HALF, HALF, 8, LANES), F32),
            pltpu.VMEM((2, 2, HALF, 2, 8, LANES), F32),
            pltpu.VMEM((2, 2, 2, 8, 8, LANES), F32),
            pltpu.VMEM((3, 2, TILE, LANES), F32),
            pltpu.VMEM((2, LINES, LANES), F32),
            pltpu.VMEM((2, LINES, LANES), F32),
            pltpu.VMEM((2, LINES, LANES), F32),
            pltpu.VMEM((4, LINES, LANES), F32),
            pltpu.VMEM((4, LINES, LANES), F32),
            pltpu.VMEM((PIXELS, 2 * cells), F32),
            pltpu.VMEM((PIXELS, 2 * cells), BF16),
            *[pltpu.VMEM((SIDE, SIDE, 1, LANES), F32)] * 3,
            *[pltpu.VMEM((bricks, 1, LANES), F32)] * 2,
            pltpu.VMEM((1, 1, LANES), F32),
            pltpu.VMEM((blocks, 1, LANES), F32),
            dma((8,)),
            *[dma((1,))] * 9,
        ],
        compiler_params=pltpu.CompilerParams(**params),
    )(*[pltpu.with_memory_space_constraint(x, pltpu.HBM) for x in (
        parameters,
        sersic.reshape(1, sources),
        psf_width.reshape(1, sources),
        point_flag.reshape(1, sources),
        owner_brick.reshape(1, sources),
        cell_index.reshape(1, sources),
        exposure,
        inv_noise.reshape(1, cells),
    )])
    return parameters + delta


def solution(mesh):
    bricks, blocks = mesh.shape["brick"], mesh.shape["blk"]
    both = ("brick", "blk")
    in_specs = (P(None, both), P(both), P(both), P(both), P(both, None), P(both), P(both, None), P(both))
    return jax.shard_map(
        functools.partial(step, bricks, blocks, True),
        mesh=mesh, in_specs=in_specs, out_specs=P(None, both), check_vma=False,
    )
```

```python
import functools
import math

import jax
import jax.numpy as jnp
from jax import lax
from jax.experimental import pallas as pl
from jax.experimental.pallas import tpu as pltpu
from jax.sharding import PartitionSpec as P

TILE = 32
PIXELS = TILE * TILE
HALF = TILE // 2
PITCH = TILE + 1
LINES = 1096
SERIES = 96
CAP = 4
VALS = 32
BACK = 8
SIDE = 8
NEAR_Z = 2
LANES = 128
ZERO_POINT = 30.0
BASE_DAMPING = 0.1
MISFIT_SCALE = 0.05
HIGHEST = lax.Precision.HIGHEST
MESH = pl.DeviceIdType.MESH
F32 = jnp.float32
BF16 = jnp.bfloat16

CX, CY, C1, C0, LN, LNN, ITV, NORM, SLOPE, CELL, WEIGHT = range(11)


def hops(step):
    return min(step, SIDE - step)


def peer_offsets():
    return [(z, y) for z in sorted(range(SIDE), key=lambda step: (hops(step), step)) for y in range(SIDE)]


def slot_peers():
    def far(j):
        z, y = (hops(step) for step in peer_offsets()[j])
        return z + y + (SIDE if z > NEAR_Z else 0)

    ordered = sorted(range(SIDE * SIDE), key=lambda j: (far(j), j))
    half = len(ordered) // 2
    return ordered[:half], ordered[half:]


def dot(a, b, ca=1, cb=0):
    return lax.dot_general(
        a, b, (((ca,), (cb,)), ((), ())), precision=HIGHEST, preferred_element_type=F32
    )


def series(shape_value, cutoff):
    chain = SERIES // 8
    at = lax.broadcasted_iota(jnp.int32, (8, LANES), 0) * chain
    total = jnp.zeros((8, LANES), F32)
    product = jnp.ones((8, LANES), F32)
    for step in reversed(range(chain)):
        k = at + (step + 1)
        ratio = cutoff / (shape_value + k.astype(F32))
        live = k < SERIES
        total = jnp.where(live, ratio * (1.0 + total), 0.0)
        product = jnp.where(live, product * ratio, product)
    whole = total[7:8]
    last = product[7:8]
    for j in reversed(range(7)):
        whole = total[j : j + 1] + product[j : j + 1] * whole
        last = last * product[j : j + 1]
    return 1.0 + whole, last


def source_rows(values, sersic, psf_width, point, cell):
    flux, shift_x, shift_y, log_radius = (values[k : k + 1] for k in range(4))
    inverse_index = 1.0 / sersic
    bfactor = 2.0 * sersic - 1.0 / 3.0 + 4.0 / (405.0 * sersic)
    cutoff = bfactor * jnp.exp((math.log(0.5 * TILE) - log_radius) * inverse_index)
    total, last = series(2.0 * sersic, cutoff)
    log_norm = math.log(math.pi * 0.25 * TILE * TILE) - cutoff + jnp.log(total)
    slope = 2.0 - (2.0 * sersic - cutoff * last) * inverse_index / total
    inv_two_var = 0.5 / (psf_width * psf_width)
    norm_psf = 1.0 / (math.sqrt(2.0 * math.pi) * psf_width)
    is_point = point == 1
    log_itv = jnp.log(inv_two_var)
    rows = [None] * VALS
    rows[CX] = shift_x
    rows[CY] = shift_y
    rows[C1] = jnp.where(is_point, 1.0, 0.5 * inverse_index)
    rows[C0] = jnp.where(is_point, log_itv, jnp.log(bfactor) - log_radius * inverse_index)
    rows[LN] = jnp.where(is_point, math.log(math.pi) - log_itv, log_norm) - jnp.log(ZERO_POINT * flux)
    rows[LNN] = jnp.where(is_point, -math.log(2.0), jnp.log(sersic))
    rows[ITV] = jnp.where(is_point, 1.0e4, inv_two_var)
    rows[NORM] = jnp.where(is_point, 1.0, norm_psf)
    rows[SLOPE] = slope
    rows[CELL] = (cell + 1).astype(F32)
    zero = jnp.zeros_like(flux)
    return jnp.concatenate([zero if row is None else row for row in rows], axis=0)


def split(x):
    high = x.astype(BF16)
    return high, (x - high.astype(F32)).astype(BF16)


def product(a, b, cb=0):
    return lax.dot_general(a, b, (((1,), (cb,)), ((), ())), preferred_element_type=F32)


def spread_taps(row, taps, spread):
    apart = lax.broadcasted_iota(jnp.int32, (TILE, LANES), 0).astype(F32)
    taps[...] = jnp.exp(-(apart * apart) * row(ITV)) * (0.5 * row(NORM))
    for d in range(TILE):
        value = jnp.broadcast_to(taps[d : d + 1, :], (8, LANES))
        spread[TILE - 1 + d] = value
        if d:
            spread[TILE - 1 - d] = value


def blur_column(q, spread, coef, at):
    near = spread[pl.ds(TILE - 1 - q, HALF)]
    far = spread[pl.ds(q, HALF)]
    coef[at, 0, q] = near + far
    coef[at, 1, q] = near - far


def blur_lines(load, store, coef, at, parts, even_acc):
    for q in range(HALF):
        low, high = load(q), load(TILE - 1 - q)
        parts[0, q] = low + high
        parts[1, q] = low - high
    for parity in range(2):
        for group in range(2):
            span = slice(group * 8, group * 8 + 8)
            acc = None
            for q in range(HALF):
                term = coef[at, parity, q, span][None] * parts[parity, q][:, None]
                acc = term if acc is None else acc + term
            if parity == 0:
                even_acc[group] = acc
            else:
                even = even_acc[group]
                for k in range(8):
                    store(group * 8 + k, even[:, k] + acc[:, k])
                    store(TILE - 1 - group * 8 - k, even[:, k] - acc[:, k])


def blur(first, count, at_of, src, mid, dst, coef, parts, even_acc):
    def along_major(k, carry):
        image = first + k
        for part in range(2):
            start = part * 16

            def load(q, start=start):
                return src[image, pl.ds(q * PITCH + start, 16), :].reshape(2, 8, LANES)

            def store(q, value, start=start):
                mid[image, pl.ds(q * PITCH + start, 16), :] = value.reshape(16, LANES)

            blur_lines(load, store, coef, at_of(image), parts.at[part], even_acc.at[part])
        return carry

    def along_minor(k, carry):
        image = first + k
        for part in range(2):
            start = part * 16

            def load(p, start=start):
                return mid[image, pl.ds(start * PITCH + p, 16, stride=PITCH), :].reshape(2, 8, LANES)

            def store(p, value, start=start):
                dst[image, pl.ds(p * PITCH + start, 16), :] = value.reshape(16, LANES)

            blur_lines(load, store, coef, at_of(image), parts.at[part], even_acc.at[part])
        return carry

    if count == 1:
        along_major(0, 0)
        along_minor(0, 0)
    else:
        lax.fori_loop(0, count, along_major, 0)
        lax.fori_loop(0, count, along_minor, 0)


def offsets(row, dy_ref, at):
    t_p = lax.broadcasted_iota(jnp.int32, (TILE, LANES), 0).astype(F32) + (0.5 - 0.5 * TILE)
    dy = t_p - row(CY)
    dy_ref[at, 0] = dy
    dy_ref[at, 1] = dy * dy


def column(q, row):
    return q.astype(F32) + (0.5 - 0.5 * TILE) - row(CX)


def images(q, row, dy_ref, at):
    dx = column(q, row)
    radius_sq = dy_ref[at, 1] + dx * dx
    log_r2 = jnp.log(radius_sq)
    log_power = row(C1) * log_r2 + row(C0)
    log_image = -jnp.exp(log_power) - row(LN)
    over = jnp.exp(log_image + log_power - (log_r2 + row(LNN)))
    return dx, radius_sq, jnp.exp(log_image), over


def damped_solve(curvature, gradient, damping):
    system = [[curvature[first][second] for second in range(4)] for first in range(4)]
    for first in range(4):
        system[first][first] = system[first][first] + damping * (1.0 + curvature[first][first])
    factor = [[None for second in range(4)] for first in range(4)]
    for column in range(4):
        pivot = system[column][column]
        for inner in range(column):
            pivot = pivot - factor[column][inner] * factor[column][inner]
        pivot = jnp.sqrt(pivot)
        factor[column][column] = pivot
        for lower_row in range(column + 1, 4):
            entry = system[lower_row][column]
            for inner in range(column):
                entry = entry - factor[lower_row][inner] * factor[column][inner]
            factor[lower_row][column] = entry / pivot
    forward = []
    for row_at in range(4):
        entry = gradient[row_at]
        for inner in range(row_at):
            entry = entry - factor[row_at][inner] * forward[inner]
        forward.append(entry / factor[row_at][row_at])
    solved = [None, None, None, None]
    for row_at in reversed(range(4)):
        entry = forward[row_at]
        for inner in range(row_at + 1, 4):
            entry = entry - factor[inner][row_at] * solved[inner]
        solved[row_at] = entry / factor[row_at][row_at]
    return solved


def kernel(
    blocks, pixel_total, remote,
    values_hbm, sersic_hbm, psf_hbm, flag_hbm, owner_hbm, cell_hbm, exposure_hbm, noise_hbm,
    out_ref,
    values_ref, sersic_ref, psf_ref, flag_ref, owner_ref, cell_ref, exposure_ref, noise_ref,
    rows_ref, hits_ref, rank_ref, slots_ref, gram_ref, taps, spread, coef, parts, even_acc, dy_ref,
    img_a, img_b, img_c, img_d, img_e, exposure_t, weighted_ref,
    out_rows, mid_rows, in_rows, out_sums, in_sums, chi_out, chi_in,
    input_sem, send_sem, mid_sem, pass_sem, near_sem, far_sem, back_send_sem, back_sem, chi_send_sem, chi_sem,
):
    offsets_of = peer_offsets()
    peers = len(offsets_of)
    near = peers // 2
    held = slot_peers()
    near_z = 2 * NEAR_Z + 1
    far_first = sorted(range(1, SIDE), key=lambda step: -hops(step))
    if remote:
        me = lax.axis_index("brick")
        lane = lax.axis_index("blk")
        barrier = pltpu.get_barrier_semaphore()
        my_z, my_y = me // SIDE, me % SIDE
        plus_z = [((my_z + k) % SIDE) * SIDE for k in range(SIDE)]
        plus_y = [(my_y + k) % SIDE for k in range(SIDE)]

        def ahead(j):
            return plus_z[offsets_of[j][0]] + plus_y[offsets_of[j][1]]

        def behind(j):
            return plus_z[-offsets_of[j][0] % SIDE] + plus_y[-offsets_of[j][1] % SIDE]

        def around(k):
            return jnp.where(lane + k >= blocks, lane + k - blocks, lane + k)

        for k in far_first:
            pl.semaphore_signal(barrier, inc=1, device_id={"brick": ahead(k)}, device_id_type=MESH)
        for k in reversed(range(1, SIDE)):
            pl.semaphore_signal(barrier, inc=1, device_id={"brick": ahead(k * SIDE)}, device_id_type=MESH)
        for k in range(1, blocks):
            pl.semaphore_signal(barrier, inc=1, device_id={"blk": around(k)}, device_id_type=MESH)
    else:
        my_z, my_y = 0, 0
    inputs = [
        pltpu.make_async_copy(source, target, input_sem.at[k])
        for k, (source, target) in enumerate(
            (
                (values_hbm, values_ref),
                (sersic_hbm, sersic_ref),
                (psf_hbm, psf_ref),
                (flag_hbm, flag_ref),
                (owner_hbm, owner_ref),
                (cell_hbm, cell_ref),
                (exposure_hbm, exposure_ref),
                (noise_hbm, noise_ref),
            )
        )
    ]
    for copy in inputs:
        copy.start()
    for copy in inputs[:6]:
        copy.wait()

    rows = source_rows(values_ref[...], sersic_ref[...], psf_ref[...], flag_ref[...], cell_ref[...])
    rows_ref[...] = rows
    owner = owner_ref[...].astype(F32)
    owner_all = jnp.broadcast_to(owner, (LANES, LANES))
    earlier = lax.broadcasted_iota(jnp.int32, (LANES, LANES), 0) < lax.broadcasted_iota(jnp.int32, (LANES, LANES), 1)
    same = jnp.where((owner_all.T == owner_all) & earlier, 1.0, 0.0)
    rank = jnp.sum(same, axis=0, keepdims=True)
    rank_ref[...] = rank
    place = owner_ref[...]
    ahead_of_me = (((place >> 3) - my_z) & (SIDE - 1)) * SIDE + (((place & (SIDE - 1)) - my_y) & (SIDE - 1))
    for j, (z, y) in enumerate(offsets_of):
        hits_ref[j : j + 1, :] = jnp.where(ahead_of_me == z * SIDE + y, 1.0, 0.0)
    by_rank = jnp.concatenate([jnp.where(rank == float(r), rows, 0.0) for r in range(CAP)], axis=0)
    out_rows[:, :, 0, :] = dot(hits_ref[...], by_rank, 1, 1).reshape(SIDE, SIDE, LANES)

    def row(k):
        return rows_ref[k : k + 1, :]

    spread_taps(row, taps, spread)
    offsets(row, dy_ref, 2)

    def own_images(step, carry):
        for k in range(8):
            q = step * 8 + k
            dx, radius_sq, image, over = images(q, row, dy_ref, 2)
            at = pl.ds(q * PITCH, TILE)
            img_d[0, at, :] = image
            img_d[1, at, :] = over * dx
            img_d[2, at, :] = over * dy_ref[2, 0]
            img_d[3, at, :] = over * radius_sq - row(SLOPE) * image
        for k in range(4):
            blur_column(step * 4 + k, spread, coef, 2)
        return carry

    lax.fori_loop(0, TILE // 8, own_images, 0)

    def own_blur(first, count):
        blur(first, count, lambda image: 2, img_d, img_e, img_d, coef, parts, even_acc)

    if remote:
        pl.semaphore_wait(barrier, 2 * (SIDE - 1) + blocks - 1)

        def send(source, target, to, sent, landed):
            pltpu.make_async_remote_copy(
                src_ref=source, dst_ref=target, send_sem=sent, recv_sem=landed,
                device_id={"brick": to}, device_id_type=MESH,
            ).start()

        def await_rows(ref, count, sem):
            pltpu.make_async_copy(ref.at[0:count], ref.at[0:count], sem).wait()

        for k in far_first:
            send(out_rows.at[:, k], mid_rows.at[:, k], ahead(k), send_sem.at[0], mid_sem.at[0])
    mid_rows[:, 0] = out_rows[:, 0]
    own_blur(0, 2)
    if remote:
        await_rows(mid_rows, SIDE - 1, mid_sem.at[0])
        for k in reversed(range(1, SIDE)):
            landed = (near_sem if k < near_z else far_sem).at[0]
            send(mid_rows.at[k], in_rows.at[k], ahead(k * SIDE), pass_sem.at[0], landed)
        in_rows[0] = mid_rows[0]
    else:
        in_rows[...] = out_rows[...]

    own_blur(2, 1)
    for copy in inputs[6:]:
        copy.wait()
    cells = exposure_ref.shape[0]
    for k in range(PIXELS // LANES):
        part = exposure_ref[:, k * LANES : (k + 1) * LANES].T
        exposure_t[k * LANES : (k + 1) * LANES, :] = jnp.concatenate([part, part], axis=1)

    noise = noise_ref[...]
    weights = noise * noise
    cells_at = lax.broadcasted_iota(jnp.int32, (cells, LANES), 0).astype(F32) + 1.0
    picks = []

    def slot_rows(half):
        return lambda k: slots_ref[half, k : k + 1, :]

    def render(half):
        received = jnp.concatenate([in_rows[j // SIDE, j % SIDE] for j in held[half]], axis=0)
        turned = [received] + [pltpu.roll(received, LANES - r * VALS, 1) for r in range(1, CAP)]
        slots_ref[half] = jnp.concatenate(turned, axis=0).T[:VALS]
        slot = slot_rows(half)
        spread_taps(slot, taps, spread)
        offsets(slot, dy_ref, half)

        def slot_images(step, carry):
            for k in range(8):
                q = step * 8 + k
                dx, radius_sq, image, over = images(q, slot, dy_ref, half)
                at = pl.ds(q * PITCH, TILE)
                img_a[half, at, :] = image
                img_b[half, at, :] = over
            for k in range(4):
                blur_column(step * 4 + k, spread, coef, half)
            return carry

        lax.fori_loop(0, TILE // 8, slot_images, 0, unroll=4)
        blur(half, 1, lambda image: half, img_a, img_e, img_c, coef, parts, even_acc)
        chosen = jnp.where(cells_at == slot(CELL), 1.0, 0.0)
        picks.append(chosen)
        slots_ref[half, WEIGHT : WEIGHT + 1, :] = dot(jnp.broadcast_to(weights, (8, cells)), chosen)[0:1]

    def lines_of(half, t):
        lines = [img_c[half, pl.ds((t * 8 + k) * PITCH, TILE), :] for k in range(8)]
        pick = jnp.concatenate([picks[half], picks[half]], axis=0).astype(BF16)
        tiles = jnp.concatenate(split(jnp.concatenate(lines, axis=0)), axis=1)
        return product(tiles, jnp.concatenate([pick, pick], axis=1), 1)

    def subtract_near(t, carry):
        at = pl.ds(pl.multiple_of(t * 8 * TILE, 8 * TILE), 8 * TILE)
        exposure_t[at, :] = exposure_t[at, :] - lines_of(0, t)
        return carry

    if remote:
        await_rows(in_rows, near_z - 1, near_sem.at[0])
    render(0)
    lax.fori_loop(0, 4, subtract_near, 0, unroll=4)
    if remote:
        await_rows(in_rows, SIDE - near_z, far_sem.at[0])
    render(1)
    weights_twice = jnp.concatenate([weights, weights], axis=1)
    is_high = lax.broadcasted_iota(jnp.int32, (1, 2 * cells), 1) < cells

    def residual(t, chi):
        at = pl.ds(pl.multiple_of(t * 8 * TILE, 8 * TILE), 8 * TILE)
        misfit = exposure_t[at, :] - lines_of(1, t)
        weighted = weights_twice * misfit
        high = weighted.astype(BF16).astype(F32)
        weighted_ref[at, :] = jnp.where(is_high, high, weighted - high).astype(BF16)
        return chi + jnp.sum((weighted * misfit).reshape(TILE, 8, 2 * cells), axis=0)

    chi = lax.fori_loop(0, 4, residual, jnp.zeros((8, 2 * cells), F32), unroll=4)
    def answer(half):
        slot = slot_rows(half)
        pick = jnp.concatenate([picks[half], picks[half]], axis=0).astype(BF16)

        def gather(t, carry):
            at = pl.ds(pl.multiple_of(t * 8 * TILE, 8 * TILE), 8 * TILE)
            tiles = product(weighted_ref[at, :], pick)
            for k in range(8):
                img_c[half, pl.ds((t * 8 + k) * PITCH, TILE), :] = tiles[k * TILE : (k + 1) * TILE]
            return carry

        def project(q, sums):
            at = pl.ds(q * PITCH, TILE)
            dx = column(q, slot)
            adjoint = img_c[half, at, :]
            over = img_b[half, at, :] * adjoint
            plain = img_a[half, at, :] * adjoint
            moment = over * dy_ref[half, 0]
            second = moment * dy_ref[half, 0]
            plain, over, moment, second = (
                x[0:8] + x[8:16] + (x[16:24] + x[24:32]) for x in (plain, over, moment, second)
            )
            over = over * dx
            return sums[0] + plain, sums[1] + over, sums[2] + moment, sums[3] + (second + over * dx)

        lax.fori_loop(0, 4, gather, 0, unroll=4)
        blur(half, 1, lambda image: half, img_c, img_e, img_c, coef, parts, even_acc)
        sums = lax.fori_loop(0, TILE, project, tuple(jnp.zeros((8, LANES), F32) for _ in range(4)), unroll=16)
        sums = [jnp.sum(s, axis=0, keepdims=True) for s in sums]
        sums[3] = sums[3] - slot(SLOPE) * sums[0]
        back = jnp.concatenate(sums + [slots_ref[half, WEIGHT : WEIGHT + 1, :], jnp.zeros((LANES - 5, LANES), F32)], axis=0).T
        packed = back[0:near]
        for r in range(1, CAP):
            packed = packed + pltpu.roll(back[r * near : (r + 1) * near], r * BACK, 1)
        out_sums[half * near : (half + 1) * near, 0, :] = packed

    def send_answers(half):
        for k in reversed(range(near)):
            j = held[half][k]
            if j:
                send(out_sums.at[half * near + k], in_sums.at[j], behind(j), back_send_sem.at[0], back_sem.at[0])

    answer(1)
    if remote:
        send_answers(1)
    chi = jnp.sum(chi, axis=0, keepdims=True)[:, :cells]
    chi = jnp.concatenate([chi, jnp.zeros((1, LANES - cells), F32)], axis=1)
    chi_out[0, :, :] = chi
    chi_in[0, :, :] = chi
    if remote:

        for k in range(1, blocks):
            pltpu.make_async_remote_copy(
                src_ref=chi_out.at[0], dst_ref=chi_in.at[k], send_sem=chi_send_sem.at[0], recv_sem=chi_sem.at[0],
                device_id={"blk": around(k)}, device_id_type=MESH,
            ).start()
    answer(0)
    if remote:
        send_answers(0)
        in_sums[0] = out_sums[0]
    else:
        for half in range(2):
            for k in range(near):
                in_sums[held[half][k]] = out_sums[half * near + k]

    own_blur(3, 1)
    pairs = [(i, j) for i in range(4) for j in range(i, 4)]

    def gram(p, sums):
        for t in range(TILE // 8):
            at = pl.ds(p * PITCH + t * 8, 8)
            own = [img_d[k, at, :] for k in range(4)]
            sums = tuple(s + own[i] * own[j] for s, (i, j) in zip(sums, pairs))
        return sums

    sums = lax.fori_loop(0, TILE, gram, tuple(jnp.zeros((8, LANES), F32) for _ in pairs))
    for k, s in enumerate(sums):
        gram_ref[k : k + 1, :] = jnp.sum(s, axis=0, keepdims=True)

    if remote:
        await_rows(chi_in, blocks - 1, chi_sem.at[0])
        await_rows(in_sums, peers - 1, back_sem.at[0])

    group = chi_in[0]
    if remote:
        for k in range(1, blocks):
            group = group + chi_in[k]
    group_chi = jnp.sum(group, axis=1, keepdims=True)
    damping = BASE_DAMPING + MISFIT_SCALE * group_chi / pixel_total
    by_rank = dot(in_sums[:, 0, :].T[: CAP * BACK], hits_ref[...])
    rank = rank_ref[...]
    mine = None
    for r in range(CAP):
        part = jnp.where(rank == float(r), by_rank[r * BACK : (r + 1) * BACK], 0.0)
        mine = part if mine is None else mine + part
    extended = jnp.where(flag_ref[...] == 1, 0.0, 1.0)
    per_flux = 1.0 / values_ref[0:1, :]
    scale = [per_flux, 1.0, 1.0, extended]
    weight = mine[4:5]
    gradient = [scale[k] * mine[k : k + 1] for k in range(4)]
    curvature = [[None] * 4 for _ in range(4)]
    for k, (i, j) in enumerate(pairs):
        entry = gram_ref[k : k + 1, :] * (scale[i] * scale[j]) * weight
        curvature[i][j] = entry
        curvature[j][i] = entry
    delta = damped_solve(curvature, gradient, jnp.broadcast_to(damping, (1, LANES)))
    out_ref[...] = jnp.concatenate(delta, axis=0)
    if remote:
        await_rows(out_rows, SIDE - 1, send_sem.at[0])
        await_rows(mid_rows, SIDE - 1, pass_sem.at[0])
        await_rows(out_sums, peers - 1, back_send_sem.at[0])
        await_rows(chi_in, blocks - 1, chi_send_sem.at[0])


def step(bricks, blocks, remote, parameters, sersic, psf_width, point_flag, owner_brick, cell_index, exposure, inv_noise):
    sources, cells = parameters.shape[1], exposure.shape[0]
    vmem = pl.BlockSpec(memory_space=pltpu.VMEM)
    dma = pltpu.SemaphoreType.DMA
    params = dict(vmem_limit_bytes=36 << 20)
    if remote:
        params.update(collective_id=0, has_side_effects=True)
    delta = pl.pallas_call(
        functools.partial(kernel, blocks, blocks * cells * PIXELS, remote),
        out_shape=jax.ShapeDtypeStruct((4, sources), F32),
        in_specs=[pl.BlockSpec(memory_space=pltpu.HBM)] * 8,
        out_specs=vmem,
        scratch_shapes=[
            pltpu.VMEM((4, sources), F32),
            pltpu.VMEM((1, sources), F32),
            pltpu.VMEM((1, sources), F32),
            pltpu.VMEM((1, sources), jnp.int32),
            pltpu.VMEM((1, sources), jnp.int32),
            pltpu.VMEM((1, sources), jnp.int32),
            pltpu.VMEM((cells, PIXELS), F32),
            pltpu.VMEM((1, cells), F32),
            pltpu.VMEM((VALS, LANES), F32),
            pltpu.VMEM((bricks, LANES), F32),
            pltpu.VMEM((1, LANES), F32),
            pltpu.VMEM((2, VALS, LANES), F32),
            pltpu.VMEM((16, LANES), F32),
            pltpu.VMEM((TILE, LANES), F32),
            pltpu.VMEM((2 * TILE, 8, LANES), F32),
            pltpu.VMEM((3, 2, HALF, HALF, 8, LANES), F32),
            pltpu.VMEM((2, 2, HALF, 2, 8, LANES), F32),
            pltpu.VMEM((2, 2, 2, 8, 8, LANES), F32),
            pltpu.VMEM((3, 2, TILE, LANES), F32),
            pltpu.VMEM((2, LINES, LANES), F32),
            pltpu.VMEM((2, LINES, LANES), F32),
            pltpu.VMEM((2, LINES, LANES), F32),
            pltpu.VMEM((4, LINES, LANES), F32),
            pltpu.VMEM((4, LINES, LANES), F32),
            pltpu.VMEM((PIXELS, 2 * cells), F32),
            pltpu.VMEM((PIXELS, 2 * cells), BF16),
            *[pltpu.VMEM((SIDE, SIDE, 1, LANES), F32)] * 3,
            *[pltpu.VMEM((bricks, 1, LANES), F32)] * 2,
            pltpu.VMEM((1, 1, LANES), F32),
            pltpu.VMEM((blocks, 1, LANES), F32),
            dma((8,)),
            *[dma((1,))] * 9,
        ],
        compiler_params=pltpu.CompilerParams(**params),
    )(*[pltpu.with_memory_space_constraint(x, pltpu.HBM) for x in (
        parameters,
        sersic.reshape(1, sources),
        psf_width.reshape(1, sources),
        point_flag.reshape(1, sources),
        owner_brick.reshape(1, sources),
        cell_index.reshape(1, sources),
        exposure,
        inv_noise.reshape(1, cells),
    )])
    return parameters + delta


def solution(mesh):
    bricks, blocks = mesh.shape["brick"], mesh.shape["blk"]
    both = ("brick", "blk")
    in_specs = (P(None, both), P(both), P(both), P(both), P(both, None), P(both), P(both, None), P(both))
    return jax.shard_map(
        functools.partial(step, bricks, blocks, True),
        mesh=mesh, in_specs=in_specs, out_specs=P(None, both), check_vma=False,
    )
```
